128 devices in a mesh: lat: 4 (over z), lon: 32 (over x, y, core).
Axes of the slice: x: 4, y: 4, z: 4, core: 2. Of those that a mesh axis runs over, the one named last changes fastest.
Arguments:
- atm_flux: bfloat16 [8, 256, 4096], P(None, 'lat', 'lon'), may hold values from -6 to 6
- sea_mask: int32 [256, 4096], P('lat', 'lon'), may hold values 0 or 1
- src_block: int32 [32768], P(('lat', 'lon')), may hold values from 0 to 63
- dest_dev: int32 [32768, 1], P(('lat', 'lon')), may hold values from 0 to 127; in each aligned block of 256 rows (0 to 255, 256 to 511, ...) at most 4 rows name the same one
- dest_block: int32 [32768], P(('lat', 'lon')), may hold values from 0 to 31
- intersection_weights: bfloat16 [32768, 128, 128], P(('lat', 'lon')), may hold values from -0.5 to 0.5
- coupling: float32 [4, 8], replicated, may hold values from -2 to 2
- inverses: float32 [4, 128, 32, 80, 80], P(None, 'lat', 'lon'), may hold values from -2 to 2
- ocean_state: float32 [4, 80, 128, 4096], P(None, None, 'lat', 'lon'), may hold values from -6 to 6
- depth_levels: int32 [128, 4096], P('lat', 'lon'), may hold values from 0 to 80
Outputs:
- ocean_out: float32 [4, 80, 128, 4096], P(None, None, 'lat', 'lon')
The draws below stay inside these ranges and needn't reach their ends.
Inputs may be any that keep to these rules, and one draw needn't show every extreme that they name: `dest_dev`: among the 256 pairs of one device no destination device is named more than 4 times, and in every draw some device names one destination exactly 4 times.
All inputs are finite; a program needn't handle non-finite values. No bound on the sum of `sea_mask` on one device may be relied on, other than what follows from the above.
Results may differ from the reference program's by a relative error of at most 0.0003.
Values sent between devices are 32-bit elements; how exact they have to be, the bound alone decides.
A program may use at most 128 MiB of HBM per device.

```python
import math
import jax
import jax.numpy as jnp
import numpy as np
from jax import lax

F = 8
Q = 4
LEV = 80
OX = 128
AX = 128
AY = 64
OY = 32
K = 256
CAP = 4
PAIRS = 32768
ALAT = 256
ALON = 4096
OLAT = 128
OLON = 4096
N_LAT = 4
N_LON = 32


def draw_inverses(key, part):
    first_key, second_key = jax.random.split(jax.random.fold_in(key, 17))
    shape = (Q, OLAT, N_LON, LEV, LEV)
    noise = jnp.clip(jax.random.normal(first_key, shape, jnp.float32), -4.0, 4.0) * (0.3 / math.sqrt(LEV))
    diagonal = jax.random.uniform(second_key, (Q, OLAT, N_LON, 1, LEV), jnp.float32, 0.6, 1.2)
    levels = jnp.arange(LEV, dtype=jnp.int32)
    unit = (levels[:, None] == levels[None, :]).astype(jnp.float32)
    return noise + unit * diagonal


def place_ends(result, rng, low, top_value):
    longest = result.shape.index(max(result.shape))
    spots = []
    for shift in (0, 1):
        where = [jax.random.randint(jax.random.fold_in(rng, axis), (), 0, length) for axis, length in enumerate(result.shape)]
        where[longest] = (where[longest] + shift) % result.shape[longest]
        spots.append(tuple(where))
    return result.at[spots[0]].set(low).at[spots[1]].set(top_value)


def block_scale(rng, shape, cuts, least, largest):
    loudness = 1.0
    for dim, parts in cuts:
        heights = jax.random.uniform(jax.random.fold_in(jax.random.fold_in(rng, 6), dim), (parts,), jnp.float32, least / len(cuts), largest / len(cuts))
        loudness = loudness * jnp.repeat(jnp.exp(heights), shape[dim] // parts).reshape((-1,) + (1,) * (len(shape) - 1 - dim))
    return loudness


def deal_out(rng, own, number, rows, amount, top, bound, skew):
    order = jax.random.permutation(rng, amount)
    heavy_load, ordinary = load_shares(amount, rows * top, bound, skew, True), load_shares(amount, rows * top, bound, skew, False)
    places = jnp.arange(amount)

    def named(lengths, turn):
        used = int((lengths > 0).sum())
        fixed = max(1, used // 4)
        shifted = fixed + (places - fixed + turn * (used - fixed)) % max(1, amount - fixed)
        return jnp.zeros((amount,), jnp.int32).at[order[jnp.where(places < fixed, places, shifted)]].set(jnp.asarray(lengths, jnp.int32))

    lengths = jnp.where(number % 4 == 0, named(heavy_load, number // 4), named(ordinary, number - number // 4 - 1))
    mixed = jax.random.permutation(jax.random.fold_in(own, 3), amount)
    giver, taker = mixed[0:amount // 2 * 2:2], mixed[1:amount // 2 * 2:2]
    slack = jnp.minimum(lengths[giver] - 1, bound - lengths[taker]) // 2
    slack = jnp.where((giver == order[0]) | (taker == order[0]) | (lengths[taker] == 0), 0, jnp.maximum(slack, 0))
    shifted = jax.random.randint(jax.random.fold_in(own, 4), (amount // 2,), 0, 1 << 20) % (slack + 1)
    lengths = lengths.at[giver].add(-shifted).at[taker].add(shifted)
    items = jnp.searchsorted(jnp.cumsum(lengths), jnp.arange(rows * top), side="right").astype(jnp.int32)
    grid = items.reshape(top, rows).T
    grid = grid[jax.random.permutation(jax.random.fold_in(own, 1), rows)]
    turn = jax.random.randint(jax.random.fold_in(own, 2), (rows, 1), 0, top)
    return jnp.take_along_axis(grid, (jnp.arange(top)[None, :] + turn) % top, axis=1)


def load_shares(number_of, total, reach, slope, full):
    weights = [(1 << 20) // math.isqrt(standing ** slope) + 1 for standing in range(1, number_of + 1)]
    largest = reach if full else min(reach, max(-(-total // number_of), total * weights[0] // sum(weights)))
    least = 1 if total - largest >= number_of - 1 else 0
    given, surplus = [largest] + [least] * (number_of - 1), total - largest - least * (number_of - 1)
    while surplus > 0:
        movable = [i for i in range(1, number_of) if given[i] < largest] or [i for i in range(1, number_of) if given[i] < reach]
        mass, budget = sum([weights[i] for i in movable]), surplus
        for i in movable:
            more = min(reach - given[i], max(1, budget * weights[i] // mass), surplus)
            given[i] = given[i] + more
            surplus = surplus - more
    return np.array(given)


def bell_draw(key, shape, deviation, reach, cuts=(), kind=jnp.bfloat16):
    entries = deviation * jax.random.normal(key, shape, jnp.float32)
    if cuts:
        entries = entries * block_scale(key, shape, cuts, -0.22, 0.18)
    return jnp.clip(entries, -reach, reach).astype(kind)


def setup_inputs(seed: int = 0) -> dict:
    splits = jax.random.split(jax.random.key(seed), 11)
    atm_flux = bell_draw(splits[0], (F, ALAT, ALON), 1.0, 6.0, ((1, 4), (2, 32)))
    sea_mask = place_ends((jax.random.randint(splits[1], (ALAT, ALON), 0, 10) < 7).astype(jnp.int32), jax.random.fold_in(splits[1], 1), 0, 1)
    src_block = place_ends(jax.random.randint(splits[2], (PAIRS,), 0, AY), jax.random.fold_in(splits[2], 1), 0, AY - 1).astype(jnp.int32)
    dest_dev_keys = jax.random.split(jax.random.fold_in(splits[3], 1), PAIRS // K)
    dest_dev_turns = jax.random.permutation(jax.random.fold_in(splits[3], 3), PAIRS // K)
    dest_dev = jax.vmap(lambda own, number: deal_out(jax.random.fold_in(splits[3], 2), own, number, K, N_LAT * N_LON, 1, CAP, 1))(dest_dev_keys, dest_dev_turns).reshape((PAIRS, 1))
    dest_block = place_ends(jax.random.randint(splits[4], (PAIRS,), 0, OY), jax.random.fold_in(splits[4], 1), 0, OY - 1).astype(jnp.int32)
    intersection_weights = bell_draw(splits[5], (PAIRS, AX, OX), AX ** -0.5, 0.5, ((0, 128),))
    coupling = bell_draw(splits[6], (Q, F), F ** -0.5, 2.0, (), jnp.float32)
    inverses = draw_inverses(jax.random.fold_in(splits[10], 71), 0)
    ocean_state = bell_draw(splits[8], (Q, LEV, OLAT, OLON), 1.0, 6.0, ((2, 4), (3, 32)), jnp.float32)
    depth_levels = place_ends(jax.random.randint(splits[9], (OLAT, OLON), 0, LEV + 1), jax.random.fold_in(splits[9], 1), 0, LEV).astype(jnp.int32)
    return dict(atm_flux=atm_flux, sea_mask=sea_mask, src_block=src_block, dest_dev=dest_dev, dest_block=dest_block, intersection_weights=intersection_weights, coupling=coupling, inverses=inverses, ocean_state=ocean_state, depth_levels=depth_levels)


diffusion_rate = 0.2


def reference(atm_flux, sea_mask, src_block, dest_dev, dest_block, intersection_weights, coupling, inverses, ocean_state, depth_levels):
    dev_total = N_LAT * N_LON
    masked = atm_flux * sea_mask.astype(jnp.bfloat16)
    pair_dev = jnp.arange(dev_total * K, dtype=jnp.int32) // K
    row_index = (pair_dev // N_LON) * AY + src_block
    col_index = (pair_dev % N_LON)[:, None] * AX + jnp.arange(AX, dtype=jnp.int32)[None, :]
    taken = masked[:, row_index[:, None], col_index]
    taken = jnp.transpose(taken, (1, 0, 2)).reshape(dev_total, K, F, AX)
    weights_dev = intersection_weights.reshape(dev_total, K, AX, OX)

    def regrid(pieces):
        rows_part, weights_part = pieces
        return jnp.einsum("kfa,kao->kfo", rows_part.astype(jnp.float32), weights_part.astype(jnp.float32), precision=lax.Precision.HIGHEST)

    contrib = lax.map(regrid, (taken, weights_dev)).reshape(dev_total * K, F, OX)
    target = dest_dev[:, 0] * OY + dest_block
    summed = jax.ops.segment_sum(contrib, target, num_segments=dev_total * OY)
    flux = summed.reshape(N_LAT, N_LON, OY, F, OX).transpose(3, 0, 2, 1, 4).reshape(F, N_LAT * OY, N_LON * OX)
    forcing = jnp.einsum("qf,fij->qij", coupling, flux, precision=lax.Precision.HIGHEST)
    levels = jnp.arange(LEV, dtype=jnp.int32)[:, None, None]
    active = levels < depth_levels[None]
    surface = ocean_state[:, 0] + forcing
    rhs = jnp.concatenate([surface[:, None], ocean_state[:, 1:]], axis=1)
    rhs = jnp.where(active[None], rhs, jnp.float32(0.0))
    rhs_blocks = rhs.reshape(Q, LEV, N_LAT * OY, N_LON, OX)
    solved = jnp.einsum("qinlm,qminx->qlinx", inverses, rhs_blocks, precision=lax.Precision.HIGHEST)
    solved = solved.reshape(Q, LEV, N_LAT * OY, N_LON * OX)
    mixed = jnp.where(active[None], solved, ocean_state)
    mixed_pad = jnp.pad(mixed, ((0, 0), (0, 0), (1, 1), (0, 0)))
    active_pad = jnp.pad(active, ((0, 0), (1, 1), (0, 0)))
    neighbours = [
        (jnp.roll(mixed, -1, axis=3), jnp.roll(active, -1, axis=2)),
        (jnp.roll(mixed, 1, axis=3), jnp.roll(active, 1, axis=2)),
        (mixed_pad[:, :, 2:], active_pad[:, 2:]),
        (mixed_pad[:, :, :-2], active_pad[:, :-2]),
    ]
    total = jnp.zeros_like(mixed)
    for values, flags in neighbours:
        total = total + jnp.where(flags[None], values - mixed, jnp.float32(0.0))
    return mixed + diffusion_rate * jnp.where(active[None], total, jnp.float32(0.0))
```

```python
import functools

import jax
import jax.numpy as jnp
from jax import lax
from jax.experimental import pallas as pl
from jax.experimental.pallas import tpu as pltpu
from jax.sharding import PartitionSpec as P

diffusion_rate = 0.2
CAP = 4
MESH = pl.DeviceIdType.MESH
f32, bf16, i32 = jnp.float32, jnp.bfloat16, jnp.int32


def halves(x):
    high = x.astype(bf16)
    return high, (x - high.astype(f32)).astype(bf16)


def dot(a, b):
    return jnp.dot(a, b, preferred_element_type=f32)


def pack_kernel(
    src_ref, coupling_ref, dest_ref, block_ref, atm_ref, mask_ref, weights_ref,
    send_ref, meta_ref, table, contrib,
):
    step = pl.program_id(0)
    pairs = weights_ref.shape[0]
    fields, rows, cells = atm_ref.shape
    total = dest_ref.shape[1]
    devices = send_ref.shape[0]
    q_count = coupling_ref.shape[0]

    @pl.when(step == 0)
    def _():
        mask = mask_ref[...].astype(f32)
        masked = [atm_ref[f].astype(f32) * mask for f in range(fields)]
        for q in range(q_count):
            row = masked[0] * coupling_ref[q, 0]
            for f in range(1, fields):
                row = row + masked[f] * coupling_ref[q, f]
            high, low = halves(row)
            table[pl.ds(q, rows, stride=8), :] = high.astype(f32)
            table[pl.ds(q_count + q, rows, stride=8), :] = low.astype(f32)

    def one(i, carry):
        p = step * pairs + i
        left = table[pl.ds(pl.multiple_of(src_ref[p] * 8, 8), 8), :].astype(bf16)
        c = dot(left, weights_ref[i])
        contrib[pl.ds(p, q_count, stride=total), :] = c[:q_count] + c[q_count:]
        return carry

    lax.fori_loop(0, pairs, one, 0, unroll=8)

    @pl.when(step == pl.num_programs(0) - 1)
    def _():
        dest = dest_ref[...]
        named = (lax.broadcasted_iota(i32, (devices, total), 0) == dest).astype(f32)
        named_b = named.astype(bf16)
        before = (
            lax.broadcasted_iota(i32, (total, total), 0)
            < lax.broadcasted_iota(i32, (total, total), 1)
        ).astype(f32).astype(bf16)
        rank = jnp.sum(named * dot(named_b, before), axis=0, keepdims=True).astype(i32)
        lane = lax.broadcasted_iota(i32, (128, total), 0)
        where_slot = (rank == lane % CAP).astype(f32) * block_ref[...].astype(f32)
        blocks = lax.dot_general(
            named_b, where_slot.astype(bf16), (((1,), (1,)), ((), ())),
            preferred_element_type=f32,
        )
        me = lax.axis_index("lat") * lax.axis_size("lon") + lax.axis_index("lon")
        lanes = lax.broadcasted_iota(i32, (devices, 128), 1)
        key = blocks + ((lanes % 16) // CAP * 32).astype(f32)
        meta_ref[...] = jnp.where(lanes // 16 == me % 8, key, 0.0)

        slot = dest * 8 + rank
        keys = jnp.concatenate([slot, slot + CAP], axis=1)
        parts = []
        for q2 in range(2):
            parts.append(contrib[pl.ds(q2 * 2 * total, 2 * total), :])
        high, low = halves(jnp.concatenate(parts, axis=1))
        chunk = 256

        def place(i, carry):
            ids = lax.broadcasted_iota(i32, (chunk, 2 * total), 0) + i * chunk
            hot = (ids == keys).astype(f32).astype(bf16)
            out = dot(hot, high) + dot(hot, low)
            for q2 in range(2):
                send_ref[pl.ds(i * (chunk // 8), chunk // 8), pl.ds(q2 * 8, 8), :] = out[
                    :, q2 * 128 : (q2 + 1) * 128
                ].reshape(chunk // 8, 8, 128)
            return carry

        lax.fori_loop(0, devices * 8 // chunk, place, 0)


def pack(src, coupling, dest, block, atm, mask, weights, devices):
    pairs, cells, out_cells = weights.shape
    group = 32
    full = lambda shape: pl.BlockSpec(shape, lambda i: (0,) * len(shape))
    return pl.pallas_call(
        pack_kernel,
        grid=(pairs // group,),
        in_specs=[
            pl.BlockSpec(memory_space=pltpu.SMEM),
            pl.BlockSpec(memory_space=pltpu.SMEM),
            full((1, pairs)),
            full((1, pairs)),
            full(atm.shape),
            full(mask.shape),
            pl.BlockSpec((group, cells, out_cells), lambda i: (i, 0, 0)),
        ],
        out_specs=[full((devices, 16, 128)), full((devices, 128))],
        out_shape=[
            jax.ShapeDtypeStruct((devices, 16, 128), f32),
            jax.ShapeDtypeStruct((devices, 128), f32),
        ],
        scratch_shapes=[
            pltpu.VMEM((8 * mask.shape[0], 128), f32),
            pltpu.VMEM((4 * pairs, 128), f32),
        ],
        compiler_params=pltpu.CompilerParams(vmem_limit_bytes=32 << 20),
        name="pack",
    )(src, coupling, dest, block, atm, mask, weights)


def exchange_kernel(n_lat, n_lon, send_ref, meta_ref, out_ref, recv, recv_meta, sems):
    devices = n_lat * n_lon
    lat, lon = lax.axis_index("lat"), lax.axis_index("lon")
    me = lat * n_lon + lon
    send_sem, recv_sem, send_meta_sem, recv_meta_sem = (sems.at[i] for i in range(4))

    def peer(k):
        core = (lon + k // 64) % 2
        y = (lon // 2 + k // 4) % 4
        x = (lon // 8 + k) % 4
        z = (lat + k // 16) % 4
        return z, (x * 4 + y) * 2 + core

    barrier = pltpu.get_barrier_semaphore()

    def greet(k, carry):
        pl.semaphore_signal(barrier, inc=1, device_id=peer(k), device_id_type=MESH)
        return carry

    lax.fori_loop(1, devices, greet, 0)
    pl.semaphore_wait(barrier, devices - 1)

    def ship(k, carry):
        z, o = peer(k)
        to = z * n_lon + o
        pltpu.make_async_remote_copy(
            send_ref.at[to], recv.at[me], send_sem, recv_sem, device_id=(z, o), device_id_type=MESH
        ).start()
        pltpu.make_async_remote_copy(
            meta_ref.at[to], recv_meta.at[me], send_meta_sem, recv_meta_sem,
            device_id=(z, o), device_id_type=MESH,
        ).start()
        return carry

    lax.fori_loop(1, devices, ship, 0)
    pltpu.make_async_copy(send_ref.at[me], recv.at[me], recv_sem).start()
    pltpu.make_async_copy(meta_ref.at[me], recv_meta.at[me], recv_meta_sem).start()
    pltpu.make_async_copy(recv_meta, recv_meta, recv_meta_sem).wait()
    pltpu.make_async_copy(recv, recv, recv_sem).wait()

    out_ref[...] = jnp.zeros_like(out_ref)

    def add(i, carry):
        base = i * 16
        keys = jnp.concatenate(
            [jnp.sum(recv_meta[pl.ds(base + 8 * h, 8)], axis=0) for h in range(2)], axis=1
        ).astype(i32)
        hot = (lax.broadcasted_iota(i32, (128, 256), 0) == keys).astype(f32).astype(bf16)
        high, low = halves(recv[pl.ds(base, 16)].reshape(256, 128))
        out_ref[...] += dot(hot, high) + dot(hot, low)
        return carry

    lax.fori_loop(0, devices // 16, add, 0)
    rest = pl.ds(0, devices - 1)
    pltpu.make_async_copy(send_ref.at[rest], send_ref.at[rest], send_sem).wait()
    pltpu.make_async_copy(meta_ref.at[rest], meta_ref.at[rest], send_meta_sem).wait()


def exchange(send, meta, n_lat, n_lon):
    devices = n_lat * n_lon
    return pl.pallas_call(
        functools.partial(exchange_kernel, n_lat, n_lon),
        in_specs=[pl.BlockSpec(memory_space=pltpu.VMEM)] * 2,
        out_specs=pl.BlockSpec(memory_space=pltpu.VMEM),
        out_shape=jax.ShapeDtypeStruct((128, 128), f32),
        scratch_shapes=[
            pltpu.VMEM((devices, 16, 128), f32),
            pltpu.VMEM((devices, 1, 128), f32),
            pltpu.SemaphoreType.DMA((4,)),
        ],
        compiler_params=pltpu.CompilerParams(
            collective_id=0, has_side_effects=True, vmem_limit_bytes=32 << 20
        ),
        name="exchange",
    )(send, meta)


def padded_2(cells, sides, width):
    for axis, dim in sides:
        count = lax.axis_size(axis)
        head = lax.slice_in_dim(cells, 0, width, axis=dim)
        tail = lax.slice_in_dim(cells, cells.shape[dim] - width, cells.shape[dim], axis=dim)
        cells = jnp.concatenate(
            [
                lax.ppermute(tail, axis, [(i, (i + 1) % count) for i in range(count)]),
                cells,
                lax.ppermute(head, axis, [((i + 1) % count, i) for i in range(count)]),
            ],
            axis=dim,
        )
    return cells


def on_device(
    atm_flux,
    sea_mask,
    src_block,
    dest_dev,
    dest_block,
    intersection_weights,
    coupling,
    inverses,
    ocean_state,
    depth_levels,
):
    n_lat, n_lon = lax.axis_size("lat"), lax.axis_size("lon")
    lat_count = n_lat
    blocks_dev = ocean_state.shape[2]
    pairs = src_block.shape[0]
    send, meta = pack(
        src_block, coupling, dest_dev.reshape(1, pairs), dest_block.reshape(1, pairs),
        atm_flux, sea_mask, intersection_weights, n_lat * n_lon,
    )
    forcing = exchange(send, meta.reshape(n_lat * n_lon, 1, 128), n_lat, n_lon)
    forcing = forcing.reshape(4, 32, 128)
    depth_pad = padded_2(depth_levels, (("lat", 0), ("lon", 1)), 1)
    level_ids = jnp.arange(ocean_state.shape[1], dtype=jnp.int32)[:, None, None]
    active = level_ids < depth_levels[None]
    surface = ocean_state[:, 0] + forcing
    rhs = jnp.concatenate([surface[:, None], ocean_state[:, 1:]], axis=1)
    rhs = jnp.where(active[None], rhs, jnp.float32(0.0))
    solved = jnp.einsum("qrlm,qmrx->qlrx", inverses[:, :, 0], rhs, precision=lax.Precision.HIGHEST)
    mixed = jnp.where(active[None], solved, ocean_state)
    padded = padded_2(mixed, (("lat", 2), ("lon", 3)), 1)
    lat_here = lax.axis_index("lat")
    row_ids = jnp.arange(blocks_dev + 2, dtype=jnp.int32)
    band_edge = (row_ids == 0) & (lat_here == 0) | (row_ids == blocks_dev + 1) & (
        lat_here == lat_count - 1
    )
    depth_pad = jnp.where(band_edge[:, None], 0, depth_pad)
    active_pad = level_ids < depth_pad[None]
    neighbours = [
        (padded[:, :, 1:-1, 2:], active_pad[:, 1:-1, 2:]),
        (padded[:, :, 1:-1, :-2], active_pad[:, 1:-1, :-2]),
        (padded[:, :, 2:, 1:-1], active_pad[:, 2:, 1:-1]),
        (padded[:, :, :-2, 1:-1], active_pad[:, :-2, 1:-1]),
    ]
    total = jnp.zeros_like(mixed)
    for values, flags in neighbours:
        total = total + jnp.where(flags[None], values - mixed, jnp.float32(0.0))
    return mixed + diffusion_rate * jnp.where(active[None], total, jnp.float32(0.0))


def solution(mesh):
    placed = (
        P(None, "lat", "lon"),
        P("lat", "lon"),
        P(("lat", "lon")),
        P(("lat", "lon"), None),
        P(("lat", "lon")),
        P(("lat", "lon"), None, None),
        P(),
        P(None, "lat", "lon", None, None),
        P(None, None, "lat", "lon"),
        P("lat", "lon"),
    )
    return jax.shard_map(
        on_device,
        mesh=mesh,
        in_specs=placed,
        out_specs=P(None, None, "lat", "lon"),
        check_vma=False,
    )
```

```python
import functools

import jax
import jax.numpy as jnp
from jax import lax
from jax.experimental import pallas as pl
from jax.experimental.pallas import tpu as pltpu
from jax.sharding import PartitionSpec as P

diffusion_rate = 0.2
CAP = 4
MESH = pl.DeviceIdType.MESH
NORTH, SOUTH, WEST, EAST = range(4)
f32, bf16, i32 = jnp.float32, jnp.bfloat16, jnp.int32
VMEM_BYTES = 62 << 20


def halves(x):
    high = x.astype(bf16)
    return high, (x - high.astype(f32)).astype(bf16)


def dot(a, b):
    return jnp.dot(a, b, preferred_element_type=f32)


def iota(shape, dim):
    return lax.broadcasted_iota(i32, shape, dim)


def one_hot(flags):
    return flags.astype(f32).astype(bf16)


def couple_kernel(
    n_lat, n_lon,
    src_ref, coupling_ref, dest_ref, block_ref, atm_ref, mask_ref, depth_ref,
    weights_hbm, inverses_hbm, ocean_hbm,
    base_hbm, force_ref, gain_ref, rows_ref, cols_ref, sides_ref,
    weights, inverses, ocean, base, table, contrib,
    send, meta, recv, recv_meta, partial, partial_in,
    col_out, gain_t, gain_out, force_out, strip_out,
    row_in, col_in, gain_in, gain_strip_in, depth_in, force_in, strip_in,
    load_sems, ship_sems, halo_send, halo_recv, force_send, force_recv,
):
    chips = n_lat * n_lon // 2
    devices = 2 * chips
    lat, lon = lax.axis_index("lat"), lax.axis_index("lon")
    core = lon % 2
    my_chip = lat * (n_lon // 2) + lon // 2
    q_count = coupling_ref.shape[0]
    pairs = dest_ref.shape[1]
    levels = inverses.shape[2]
    o_rows = depth_ref.shape[0]

    w_chunks = 8
    w_size = pairs // w_chunks

    def weight_copy(c):
        part = pl.ds(c * w_size, w_size)
        return pltpu.make_async_copy(weights_hbm.at[part], weights.at[part], load_sems.at[c])

    for c in range(w_chunks):
        weight_copy(c).start()
    inverse_copy = pltpu.make_async_copy(inverses_hbm, inverses, load_sems.at[w_chunks])
    ocean_copy = pltpu.make_async_copy(ocean_hbm, ocean, load_sems.at[w_chunks + 1])
    inverse_copy.start()
    ocean_copy.start()

    barrier = pltpu.get_barrier_semaphore()

    def peer(k):
        x = (lon // 8 + k) % 4
        y = (lon // 2 + k // 4) % 4
        z = (lat + k // 16) % 4
        return z, (x * 4 + y) * 2 + core

    beside = {
        NORTH: ((lat + n_lat - 1) % n_lat, lon),
        SOUTH: ((lat + 1) % n_lat, lon),
        WEST: (lat, (lon + n_lon - 1) % n_lon),
        EAST: (lat, (lon + 1) % n_lon),
    }
    partner = (lat, lon + 1 - 2 * core)

    def greet(k, carry):
        pl.semaphore_signal(barrier, inc=1, device_id=peer(k), device_id_type=MESH)
        return carry

    lax.fori_loop(1, chips, greet, 0)
    for side in (WEST, EAST):
        pl.semaphore_signal(barrier, inc=1, device_id=beside[side], device_id_type=MESH)

    a_rows = mask_ref.shape[0]
    mask = mask_ref[...].astype(f32)
    masked = [atm_ref[f].astype(f32) * mask for f in range(atm_ref.shape[0])]
    for q in range(q_count):
        row = masked[0] * coupling_ref[q, 0]
        for f in range(1, atm_ref.shape[0]):
            row = row + masked[f] * coupling_ref[q, f]
        high, low = halves(row)
        contrib[pl.ds(q, a_rows, stride=8), :] = high.astype(f32)
        contrib[pl.ds(q_count + q, a_rows, stride=8), :] = low.astype(f32)
    table[...] = contrib[pl.ds(0, 8 * a_rows), :].reshape(a_rows, 8, 128)

    dest = dest_ref[...]
    named = (iota((devices, pairs), 0) == dest).astype(f32)
    before = one_hot(iota((pairs, pairs), 0) < iota((pairs, pairs), 1))
    rank = jnp.sum(named * dot(named.astype(bf16), before), axis=0, keepdims=True).astype(i32)
    lane = iota((128, pairs), 0)
    of_chip = one_hot(iota((chips, pairs), 0) == dest // 2)
    held = ((rank == lane % CAP) & (dest % 2 == lane % 32 // 16)).astype(f32)
    held = (held * block_ref[...].astype(f32)).astype(bf16)
    blocks = lax.dot_general(of_chip, held, (((1,), (1,)), ((), ())), preferred_element_type=f32)
    lanes = iota((chips, 128), 1)
    key = blocks + (lanes % 32 // 16 * 128 + lanes % 16 // CAP * o_rows).astype(f32)
    key = jnp.where(lanes // 32 == my_chip % 4, key, 0.0)
    for h in range(chips):
        meta[h] = key[h : h + 1]
    slot = dest * 8 + rank
    keys = jnp.concatenate([slot, slot + CAP], axis=1)

    def chunk_of_pairs(c, carry):
        weight_copy(c).wait()

        def four(i, carry):
            p = c * w_size + i * 4
            lefts = []
            for j in range(4):
                left = table[src_ref[p + j]]
                zero = jnp.zeros_like(left)
                lefts.append(jnp.concatenate([left, zero] if j % 2 == 0 else [zero, left], axis=1))
            left = jnp.concatenate(lefts, axis=0).astype(bf16)
            w = [weights[p + j] for j in range(4)]
            right = jnp.concatenate(
                [jnp.concatenate(w[:2], axis=0), jnp.concatenate(w[2:], axis=0)], axis=1
            )
            out = dot(left, right)
            for j in range(4):
                both = out[j * 8 : j * 8 + 8, j // 2 * 128 : j // 2 * 128 + 128]
                contrib[pl.ds(p + j, q_count, stride=pairs), :] = both[:q_count] + both[q_count:]
            return carry

        return lax.fori_loop(0, w_size // 4, four, carry, unroll=4)

    lax.fori_loop(0, w_chunks, chunk_of_pairs, 0)

    high, low = halves(
        jnp.concatenate(
            [contrib[pl.ds(h * 2 * pairs, 2 * pairs), :] for h in range(2)], axis=1
        )
    )
    chunk = 256

    def place(i, carry):
        hot = one_hot(iota((chunk, 2 * pairs), 0) + i * chunk == keys)
        out = dot(hot, high) + dot(hot, low)
        for h in range(2):
            send[pl.ds(i * (chunk // 8), chunk // 8), pl.ds(h * 8, 8), :] = out[
                :, h * 128 : (h + 1) * 128
            ].reshape(chunk // 8, 8, 128)
        return carry

    lax.fori_loop(0, devices * 8 // chunk, place, 0)

    pl.semaphore_wait(barrier, chips + 1)
    send_sem, recv_sem, meta_send_sem, meta_recv_sem = (ship_sems.at[i] for i in range(4))

    def ship(k, carry):
        z, o = peer(k)
        to = z * (n_lon // 2) + o // 2
        pltpu.make_async_remote_copy(
            send.at[pl.ds(2 * to, 2)], recv.at[pl.ds(2 * my_chip, 2)], send_sem, recv_sem,
            device_id=(z, o), device_id_type=MESH,
        ).start()
        pltpu.make_async_remote_copy(
            meta.at[to], recv_meta.at[my_chip], meta_send_sem, meta_recv_sem,
            device_id=(z, o), device_id_type=MESH,
        ).start()
        return carry

    lax.fori_loop(1, chips, ship, 0)
    mine = pl.ds(2 * my_chip, 2)
    pltpu.make_async_copy(send.at[mine], recv.at[mine], recv_sem).start()
    pltpu.make_async_copy(meta.at[my_chip], recv_meta.at[my_chip], meta_recv_sem).start()

    inverse_copy.wait()
    ocean_copy.wait()
    gain_ref[...] = jnp.zeros_like(gain_ref)
    level = iota((levels, 128), 0)
    lane_id = iota((levels, 128), 1)

    def mix(i, carry):
        q, r = i // o_rows, i % o_rows
        state = ocean[pl.ds(q * levels * o_rows + r, levels, stride=o_rows), :]
        active = level < depth_ref[pl.ds(r, 1), :]
        inverse = inverses[q, r]
        left = jnp.concatenate(halves(inverse), axis=0)
        right = jnp.concatenate(halves(jnp.where(active, state, 0.0)), axis=1)
        out = dot(left, right)
        solved = out[:levels, :128] + (out[:levels, 128:] + out[levels:, :128])
        mixed = jnp.where(active, solved, state)
        base[q, r] = mixed
        here = lane_id == i
        col_out[0] = jnp.where(here, jnp.broadcast_to(mixed[:, :1], mixed.shape), col_out[0])
        col_out[1] = jnp.where(here, jnp.broadcast_to(mixed[:, 127:], mixed.shape), col_out[1])
        gain_ref[pl.ds(0, levels), :] = jnp.where(
            here, jnp.broadcast_to(inverse[:, :1], mixed.shape), gain_ref[pl.ds(0, levels), :]
        )
        return carry

    lax.fori_loop(0, q_count * o_rows, mix, 0, unroll=2)
    base_copy = pltpu.make_async_copy(base, base_hbm, load_sems.at[w_chunks + 2])
    base_copy.start()
    gain_t[...] = jnp.transpose(gain_ref[...])
    for s, r in ((0, 0), (1, o_rows - 1)):
        gain_out[s, pl.ds(0, q_count), :] = gain_t[pl.ds(r, q_count, stride=o_rows), :]

    copies = []

    def hand(side, source, target):
        opposite = (SOUTH, NORTH, EAST, WEST)[side]
        n = len(copies)
        copy = pltpu.make_async_remote_copy(
            source, target(opposite), halo_send.at[n], halo_recv.at[n],
            device_id=beside[side], device_id_type=MESH,
        )
        copy.start()
        copies.append(copy)

    for side, r in ((NORTH, 0), (SOUTH, o_rows - 1)):
        hand(side, base.at[:, r], lambda o: row_in.at[o])
        hand(side, gain_out.at[side], lambda o: gain_strip_in.at[o])
    for side in (WEST, EAST):
        hand(side, col_out.at[side - 2], lambda o: col_in.at[o - 2])
        hand(side, gain_ref.at[pl.ds(0, levels)], lambda o: gain_in.at[o - 2])
    for side in range(4):
        hand(side, depth_ref, lambda o: depth_in.at[o])
    for copy in copies:
        copy.wait()

    every = pl.ds(0, chips)
    pltpu.make_async_copy(recv_meta, recv_meta, meta_recv_sem).wait()
    pltpu.make_async_copy(recv, recv, recv_sem).wait()
    partial[...] = jnp.zeros_like(partial)

    def add(i, carry):
        at = i * 8
        keys = jnp.concatenate(
            [jnp.sum(recv_meta[pl.ds(at + 4 * h, 4)], axis=0) for h in range(2)], axis=1
        ).astype(i32)
        hot = one_hot(iota((256, 256), 0) == keys)
        high, low = halves(recv[pl.ds(2 * at, 16)].reshape(256, 128))
        partial[...] += (dot(hot, high) + dot(hot, low)).reshape(2, 128, 128)
        return carry

    lax.fori_loop(0, chips // 8, add, 0)
    swap = pltpu.make_async_remote_copy(
        partial.at[1 - core], partial_in, force_send.at[4], force_recv.at[4],
        device_id=partner, device_id_type=MESH,
    )
    swap.start()
    swap.wait()
    force = partial[core] + partial_in[...]
    force_ref[...] = force
    for s, r in ((0, 0), (1, o_rows - 1)):
        force_out[s, pl.ds(0, q_count), :] = force_ref[pl.ds(r, q_count, stride=o_rows), :]
    force_t = jnp.transpose(force)
    strip_out[0, pl.ds(0, 1), :] = force_t[:1]
    strip_out[1, pl.ds(0, 1), :] = force_t[127:]
    forces = []
    for side in range(4):
        opposite = (SOUTH, NORTH, EAST, WEST)[side]
        out, into = (force_out, force_in) if side < 2 else (strip_out, strip_in)
        copy = pltpu.make_async_remote_copy(
            out.at[side % 2], into.at[opposite % 2], force_send.at[side], force_recv.at[side],
            device_id=beside[side], device_id_type=MESH,
        )
        copy.start()
        forces.append(copy)

    depth = depth_ref[...]
    in_band = (lat > 0).astype(i32), (lat < n_lat - 1).astype(i32)
    north_depth = depth_in[NORTH] * in_band[0]
    south_depth = depth_in[SOUTH] * in_band[1]
    row_id, cell_id = iota(depth.shape, 0), iota(depth.shape, 1)
    roll = pltpu.roll
    sides_ref[NORTH] = jnp.where(row_id == 0, roll(north_depth, 1, 0), roll(depth, 1, 0))
    sides_ref[SOUTH] = jnp.where(
        row_id == o_rows - 1, roll(south_depth, o_rows - 1, 0), roll(depth, o_rows - 1, 0)
    )
    sides_ref[WEST] = jnp.where(cell_id == 0, roll(depth_in[WEST], 1, 1), roll(depth, 1, 1))
    sides_ref[EAST] = jnp.where(cell_id == 127, roll(depth_in[EAST], 127, 1), roll(depth, 127, 1))
    turned = [
        jnp.transpose(jnp.concatenate([depth_in[s].astype(f32)] * q_count, axis=0))
        for s in (WEST, EAST)
    ]
    limits = turned[0][127:].astype(i32), turned[1][:1].astype(i32)
    strips = jnp.transpose(
        jnp.concatenate(
            [gain_strip_in[0], gain_strip_in[1], jnp.zeros((112, 128), f32)], axis=0
        )
    )
    for copy in forces:
        copy.wait()
    edges = north_depth[o_rows - 1 :], south_depth[:1]
    for s in range(2):
        for q in range(q_count):
            gain = jnp.broadcast_to(strips[:levels, s * 8 + q : s * 8 + q + 1], (levels, 128))
            value = row_in[s, q] + gain * force_in[s, pl.ds(q, 1), :]
            rows_ref[s, q] = jnp.where(level < edges[s], value, 0.0)
        value = col_in[s] + gain_in[s] * strip_in[s, pl.ds(0, 1), :]
        cols_ref[s] = jnp.where(level < limits[s], value, 0.0)

    rest = pl.ds(0, 2 * (chips - 1))
    pltpu.make_async_copy(send.at[rest], send.at[rest], send_sem).wait()
    rest = pl.ds(0, chips - 1)
    pltpu.make_async_copy(meta.at[rest], meta.at[rest], meta_send_sem).wait()
    base_copy.wait()


def couple(src, coupling, dest, block, atm, mask, depth, weights, inverses, ocean, n_lat, n_lon):
    pairs = src.shape[0]
    q_count, o_rows, levels, _ = inverses.shape
    chips = n_lat * n_lon // 2
    vmem, smem, hbm = (
        pl.BlockSpec(memory_space=s) for s in (pltpu.VMEM, pltpu.SMEM, pl.ANY)
    )
    shape = jax.ShapeDtypeStruct
    V, DMA = pltpu.VMEM, pltpu.SemaphoreType.DMA
    return pl.pallas_call(
        functools.partial(couple_kernel, n_lat, n_lon),
        in_specs=[smem, smem] + [vmem] * 5 + [hbm] * 3,
        out_specs=[hbm] + [vmem] * 5,
        out_shape=[
            shape((q_count, o_rows, levels, 128), f32),
            shape((128, 128), f32),
            shape((128, 128), f32),
            shape((2, q_count, levels, 128), f32),
            shape((2, levels, 128), f32),
            shape((4, o_rows, 128), i32),
        ],
        scratch_shapes=[
            V(weights.shape, bf16),
            V(inverses.shape, f32),
            V(ocean.shape, f32),
            V((q_count, o_rows, levels, 128), f32),
            V((mask.shape[0], 8, 128), f32),
            V((4 * pairs, 128), f32),
            V((2 * chips, 16, 128), f32),
            V((chips, 1, 128), f32),
            V((2 * chips, 16, 128), f32),
            V((chips, 1, 128), f32),
            V((2, 128, 128), f32),
            V((128, 128), f32),
            V((2, levels, 128), f32),
            V((128, 128), f32),
            V((2, 8, 128), f32),
            V((2, 8, 128), f32),
            V((2, 8, 128), f32),
            V((2, q_count, levels, 128), f32),
            V((2, levels, 128), f32),
            V((2, levels, 128), f32),
            V((2, 8, 128), f32),
            V((4, o_rows, 128), i32),
            V((2, 8, 128), f32),
            V((2, 8, 128), f32),
            DMA((11,)),
            DMA((4,)),
            DMA((12,)),
            DMA((12,)),
            DMA((5,)),
            DMA((5,)),
        ],
        compiler_params=pltpu.CompilerParams(
            collective_id=0, has_side_effects=True, vmem_limit_bytes=VMEM_BYTES
        ),
        name="couple",
    )(src, coupling, dest, block, atm, mask, depth, weights, inverses, ocean)


def finish_kernel(
    base_ref, force_ref, gain_ref, rows_ref, cols_ref, sides_ref, depth_ref, out_ref, mixed, keep
):
    q = pl.program_id(0)
    o_rows, levels = base_ref.shape[1:3]
    shape = (levels, 128)
    level = iota(shape, 0)
    cell = iota(shape, 1)

    @pl.when(q == 0)
    def _():
        def weigh(r, carry):
            count = jnp.zeros(shape, f32)
            for s in range(4):
                count = count + (level < sides_ref[s, pl.ds(r, 1), :]).astype(f32)
            keep[r] = 1.0 - diffusion_rate * count
            return carry

        lax.fori_loop(0, o_rows, weigh, 0)

    mixed[0] = rows_ref[0, 0]
    mixed[o_rows + 1] = rows_ref[1, 0]

    def pick(values, k):
        return jnp.take_along_axis(values, jnp.full(shape, k, i32), axis=1)

    def force(r, carry):
        k = q * o_rows + r
        gain = pick(gain_ref[pl.ds(0, levels), :], k)
        value = base_ref[0, r] + gain * force_ref[pl.ds(k, 1), :]
        mixed[r + 1] = jnp.where(level < depth_ref[pl.ds(r, 1), :], value, 0.0)
        return carry

    lax.fori_loop(0, o_rows, force, 0, unroll=2)

    def spread(r, carry):
        k = q * o_rows + r
        here = mixed[r + 1]
        west = jnp.where(cell == 0, pick(cols_ref[0], k), pltpu.roll(here, 1, 1))
        east = jnp.where(cell == 127, pick(cols_ref[1], k), pltpu.roll(here, 127, 1))
        around = (mixed[r] + mixed[r + 2]) + (west + east)
        value = keep[r] * here + diffusion_rate * around
        active = level < depth_ref[pl.ds(r, 1), :]
        out_ref[0, pl.ds(r, levels, stride=o_rows), :] = jnp.where(active, value, base_ref[0, r])
        return carry

    lax.fori_loop(0, o_rows, spread, 0, unroll=2)


def finish(base, force, gain, rows, cols, sides, depth):
    q_count, o_rows, levels, _ = base.shape
    full = lambda a: pl.BlockSpec(a.shape, lambda q: (0,) * a.ndim)
    return pl.pallas_call(
        finish_kernel,
        grid=(q_count,),
        in_specs=[
            pl.BlockSpec((1, o_rows, levels, 128), lambda q: (q, 0, 0, 0)),
            full(force),
            full(gain),
            pl.BlockSpec((2, 1, levels, 128), lambda q: (0, q, 0, 0)),
            full(cols),
            full(sides),
            full(depth),
        ],
        out_specs=pl.BlockSpec((1, levels * o_rows, 128), lambda q: (q, 0, 0)),
        out_shape=jax.ShapeDtypeStruct((q_count, levels * o_rows, 128), f32),
        scratch_shapes=[
            pltpu.VMEM((o_rows + 2, levels, 128), f32),
            pltpu.VMEM((o_rows, levels, 128), f32),
        ],
        compiler_params=pltpu.CompilerParams(vmem_limit_bytes=VMEM_BYTES),
        name="finish",
    )(base, force, gain, rows, cols, sides, depth)


def on_device(
    atm_flux,
    sea_mask,
    src_block,
    dest_dev,
    dest_block,
    intersection_weights,
    coupling,
    inverses,
    ocean_state,
    depth_levels,
):
    n_lat, n_lon = lax.axis_size("lat"), lax.axis_size("lon")
    pairs = src_block.shape[0]
    q_count, levels, o_rows, cells = ocean_state.shape
    base, force, gain, rows, cols, sides = couple(
        src_block, coupling, dest_dev.reshape(1, pairs), dest_block.reshape(1, pairs),
        atm_flux, sea_mask, depth_levels, intersection_weights,
        inverses.reshape(q_count, o_rows, levels, levels),
        ocean_state.reshape(q_count * levels * o_rows, cells), n_lat, n_lon,
    )
    out = finish(base, force, gain, rows, cols, sides, depth_levels)
    return out.reshape(ocean_state.shape)


def solution(mesh):
    placed = (
        P(None, "lat", "lon"),
        P("lat", "lon"),
        P(("lat", "lon")),
        P(("lat", "lon"), None),
        P(("lat", "lon")),
        P(("lat", "lon"), None, None),
        P(),
        P(None, "lat", "lon", None, None),
        P(None, None, "lat", "lon"),
        P("lat", "lon"),
    )
    return jax.shard_map(
        on_device,
        mesh=mesh,
        in_specs=placed,
        out_specs=P(None, None, "lat", "lon"),
        check_vma=False,
    )
```

```python
import functools

import jax
import jax.numpy as jnp
from jax import lax
from jax.experimental import pallas as pl
from jax.experimental.pallas import tpu as pltpu
from jax.sharding import PartitionSpec as P

diffusion_rate = 0.2
CAP = 4
MESH = pl.DeviceIdType.MESH
NORTH, SOUTH, WEST, EAST = range(4)
ORDER = (2, 1, 3, 0)
f32, bf16, i32 = jnp.float32, jnp.bfloat16, jnp.int32
VMEM_BYTES = 62 << 20


def halves(x):
    high = x.astype(bf16)
    return high, (x - high.astype(f32)).astype(bf16)


def dot(a, b):
    return jnp.dot(a, b, preferred_element_type=f32)


def iota(shape, dim):
    return lax.broadcasted_iota(i32, shape, dim)


def one_hot(flags):
    return flags.astype(f32).astype(bf16)


def couple_kernel(
    n_lat, n_lon,
    src_ref, coupling_ref, dest_ref, block_ref, atm_ref, mask_ref, depth_ref,
    weights_hbm, inverses_hbm, ocean_hbm,
    base_hbm, force_ref, gain_ref, rows_ref, cols_ref, sides_ref,
    weights, inverses, ocean, skewed, table, contrib,
    send, meta, recv, recv_meta, partial, partial_in,
    packed, col_out, gain_out, force_out, strip_out, row_out,
    row_in, col_in, gain_in, gain_strip_in, depth_in, force_in, strip_in,
    load_sems, ship_sems, halo_send, halo_recv, force_send, force_recv,
):
    chips = n_lat * n_lon // 2
    devices = 2 * chips
    lat, lon = lax.axis_index("lat"), lax.axis_index("lon")
    core = lon % 2
    my_chip = lat * (n_lon // 2) + lon // 2
    q_count = coupling_ref.shape[0]
    pairs = dest_ref.shape[1]
    levels = inverses.shape[2]
    skew = skewed.shape[0] // levels
    o_rows = depth_ref.shape[0]

    w_chunks = 8
    w_size = pairs // w_chunks

    def weight_copy(c):
        part = pl.ds(c * w_size, w_size)
        return pltpu.make_async_copy(weights_hbm.at[part], weights.at[part], load_sems.at[c])

    for c in range(w_chunks):
        weight_copy(c).start()
    inverse_copy = pltpu.make_async_copy(inverses_hbm, inverses, load_sems.at[w_chunks])
    ocean_copy = pltpu.make_async_copy(ocean_hbm, ocean, load_sems.at[w_chunks + 1])
    inverse_copy.start()
    ocean_copy.start()

    barrier = pltpu.get_barrier_semaphore()

    x_here, y_here = lon // 8, lon // 2 % 4

    def plane(dz, each, first=0):
        z = lax.rem(lat + dz, n_lat)
        xs = [lax.rem(x_here + dx, 4) * 8 + core for dx in range(4)]

        def line(dy, carry):
            y = lax.rem(y_here + dy, 4) * 2
            for dx in range(4):
                each(z, xs[dx] + y)
            return carry

        if dz == 0:
            for dx in range(1, 4):
                each(z, xs[dx] + y_here * 2)
            lax.fori_loop(1, 4, line, 0)
        else:
            lax.fori_loop(0, 4, line, 0)

    beside = {
        NORTH: ((lat + n_lat - 1) % n_lat, lon),
        SOUTH: ((lat + 1) % n_lat, lon),
        WEST: (lat, (lon + n_lon - 1) % n_lon),
        EAST: (lat, (lon + 1) % n_lon),
    }
    partner = (lat, lon + 1 - 2 * core)

    def greet(z, o):
        pl.semaphore_signal(barrier, inc=1, device_id=(z, o), device_id_type=MESH)

    for dz in range(n_lat):
        plane(dz, greet)
    for side in (WEST, EAST):
        pl.semaphore_signal(barrier, inc=1, device_id=beside[side], device_id_type=MESH)

    a_rows = mask_ref.shape[0]
    mask = mask_ref[...].astype(f32)
    masked = [atm_ref[f].astype(f32) * mask for f in range(atm_ref.shape[0])]
    for q in range(q_count):
        row = masked[0] * coupling_ref[q, 0]
        for f in range(1, atm_ref.shape[0]):
            row = row + masked[f] * coupling_ref[q, f]
        high, low = halves(row)
        contrib[pl.ds(q, a_rows, stride=8), :] = high.astype(f32)
        contrib[pl.ds(q_count + q, a_rows, stride=8), :] = low.astype(f32)
    table[...] = contrib[pl.ds(0, 8 * a_rows), :].reshape(a_rows, 8, 128)

    dest = dest_ref[...]
    named = (iota((devices, pairs), 0) == dest).astype(f32)
    before = one_hot(iota((pairs, pairs), 0) < iota((pairs, pairs), 1))
    rank = jnp.sum(named * dot(named.astype(bf16), before), axis=0, keepdims=True).astype(i32)
    lane = iota((128, pairs), 0)
    of_chip = one_hot(iota((chips, pairs), 0) == dest // 2)
    held = ((rank == lane % CAP) & (dest % 2 == lane % 32 // 16)).astype(f32)
    held = (held * block_ref[...].astype(f32)).astype(bf16)
    blocks = lax.dot_general(of_chip, held, (((1,), (1,)), ((), ())), preferred_element_type=f32)
    lanes = iota((chips, 128), 1)
    key = blocks + (lanes % 32 // 16 * 128 + lanes % 16 // CAP * o_rows).astype(f32)
    key = jnp.where(lanes // 32 == my_chip % 4, key, 0.0)
    for h in range(chips):
        meta[h] = key[h : h + 1]
    slot = dest * 8 + rank
    keys = jnp.concatenate([slot, slot + CAP], axis=1)

    def chunk_of_pairs(c, carry):
        weight_copy(c).wait()

        def four(i, carry):
            p = c * w_size + i * 4
            lefts = []
            for j in range(4):
                left = table[src_ref[p + j]]
                zero = jnp.zeros_like(left)
                lefts.append(jnp.concatenate([left, zero] if j % 2 == 0 else [zero, left], axis=1))
            left = jnp.concatenate(lefts, axis=0).astype(bf16)
            w = [weights[p + j] for j in range(4)]
            right = jnp.concatenate(
                [jnp.concatenate(w[:2], axis=0), jnp.concatenate(w[2:], axis=0)], axis=1
            )
            out = dot(left, right)
            for j in range(4):
                both = out[j * 8 : j * 8 + 8, j // 2 * 128 : j // 2 * 128 + 128]
                contrib[pl.ds(p + j, q_count, stride=pairs), :] = both[:q_count] + both[q_count:]
            return carry

        return lax.fori_loop(0, w_size // 4, four, carry, unroll=4)

    lax.fori_loop(0, w_chunks, chunk_of_pairs, 0)

    high, low = halves(
        jnp.concatenate(
            [contrib[pl.ds(h * 2 * pairs, 2 * pairs), :] for h in range(2)], axis=1
        )
    )
    chunk = devices * 8 // n_lat
    send_sem, meta_send_sem = ship_sems.at[0], ship_sems.at[1]
    recv_sems = [ship_sems.at[2 + dz] for dz in range(n_lat)]
    meta_recv_sems = [ship_sems.at[2 + n_lat + dz] for dz in range(n_lat)]

    def place(i):
        hot = one_hot(iota((chunk, 2 * pairs), 0) + i * chunk == keys)
        out = dot(hot, high) + dot(hot, low)
        for h in range(2):
            send[pl.ds(i * (chunk // 8), chunk // 8), pl.ds(h * 8, 8), :] = out[
                :, h * 128 : (h + 1) * 128
            ].reshape(chunk // 8, 8, 128)

    mine = pl.ds(2 * my_chip, 2)
    for n, dz in enumerate(ORDER):
        place(lax.rem(lat + dz, n_lat))
        if n == 0:
            pl.semaphore_wait(barrier, chips + 1)

        def ship(z, o):
            to = z * (n_lon // 2) + o // 2
            pltpu.make_async_remote_copy(
                send.at[pl.ds(2 * to, 2)], recv.at[mine], send_sem, recv_sems[dz],
                device_id=(z, o), device_id_type=MESH,
            ).start()
            pltpu.make_async_remote_copy(
                meta.at[to], recv_meta.at[my_chip], meta_send_sem, meta_recv_sems[dz],
                device_id=(z, o), device_id_type=MESH,
            ).start()

        plane(dz, ship)
    pltpu.make_async_copy(send.at[mine], recv.at[mine], recv_sems[0]).start()
    pltpu.make_async_copy(meta.at[my_chip], recv_meta.at[my_chip], meta_recv_sems[0]).start()

    inverse_copy.wait()
    ocean_copy.wait()
    packed[...] = jnp.zeros_like(packed)
    level = iota((levels, 128), 0)
    lane_id = iota((levels, 128), 1)
    low_levels = pl.ds(0, levels)

    def copy_out(q):
        return pltpu.make_async_copy(ocean.at[q], base_hbm.at[q], load_sems.at[w_chunks + 2 + q])

    def field(q, carry):
        def skew_in(l, carry):
            skewed[pl.ds(l * skew, o_rows), :] = ocean[q, l]
            return carry

        lax.fori_loop(0, levels, skew_in, 0, unroll=8)

        def mix(r, carry):
            i = q * o_rows + r
            column = pl.ds(r, levels, stride=skew)
            state = skewed[column, :]
            active = level < depth_ref[pl.ds(r, 1), :]
            inverse = inverses[q, r]
            left = jnp.concatenate(halves(inverse), axis=0)
            right = jnp.concatenate(halves(jnp.where(active, state, 0.0)), axis=1)
            out = dot(left, right)
            solved = out[:levels, :128] + (out[:levels, 128:] + out[levels:, :128])
            mixed = jnp.where(active, solved, state)
            skewed[column, :] = mixed
            turned = pltpu.roll(mixed, i, 1)
            packed[0, low_levels, :] = jnp.where(lane_id == i, turned, packed[0, low_levels, :])
            last = lax.rem(i + 127, 128)
            packed[1, low_levels, :] = jnp.where(lane_id == last, turned, packed[1, low_levels, :])
            gain = jnp.broadcast_to(inverse[:, :1], mixed.shape)
            packed[2, low_levels, :] = jnp.where(lane_id == i, gain, packed[2, low_levels, :])
            return carry

        lax.fori_loop(0, o_rows, mix, 0, unroll=2)

        def skew_out(l, carry):
            ocean[q, l] = skewed[pl.ds(l * skew, o_rows), :]
            return carry

        lax.fori_loop(0, levels, skew_out, 0, unroll=8)
        for s, r in ((0, 0), (1, o_rows - 1)):
            row_out[s, q] = skewed[pl.ds(r, levels, stride=skew), :]
        copy_out(q).start()
        return carry

    lax.fori_loop(0, q_count, field, 0)
    col_out[0] = jnp.transpose(packed[0])
    col_out[1] = jnp.transpose(pltpu.roll(packed[1], 1, 1))
    gain_ref[...] = jnp.transpose(packed[2])
    for s, r in ((0, 0), (1, o_rows - 1)):
        gain_out[s, pl.ds(0, q_count), :] = gain_ref[pl.ds(r, q_count, stride=o_rows), :]

    copies = []

    def hand(side, source, target):
        opposite = (SOUTH, NORTH, EAST, WEST)[side]
        n = len(copies)
        copy = pltpu.make_async_remote_copy(
            source, target(opposite), halo_send.at[n], halo_recv.at[n],
            device_id=beside[side], device_id_type=MESH,
        )
        copy.start()
        copies.append(copy)

    for side in (NORTH, SOUTH):
        hand(side, row_out.at[side], lambda o: row_in.at[o])
        hand(side, gain_out.at[side], lambda o: gain_strip_in.at[o])
    for side in (WEST, EAST):
        hand(side, col_out.at[side - 2], lambda o: col_in.at[o - 2])
        hand(side, gain_ref, lambda o: gain_in.at[o - 2])
    for side in range(4):
        hand(side, depth_ref, lambda o: depth_in.at[o])
    for copy in copies:
        copy.wait()

    partial[...] = jnp.zeros_like(partial)
    per_plane = chips // n_lat
    for dz in ORDER:
        z = lax.rem(lat + n_lat - dz, n_lat)
        some = pl.ds(z * per_plane, per_plane)
        pltpu.make_async_copy(recv_meta.at[some], recv_meta.at[some], meta_recv_sems[dz]).wait()
        some = pl.ds(z * 2 * per_plane, 2 * per_plane)
        pltpu.make_async_copy(recv.at[some], recv.at[some], recv_sems[dz]).wait()
        out = None
        for i in range(per_plane // 8):
            at = z * per_plane + i * 8
            keys = jnp.concatenate(
                [jnp.sum(recv_meta[pl.ds(at + 4 * h, 4)], axis=0) for h in range(2)], axis=1
            ).astype(i32)
            hot = one_hot(iota((256, 256), 0) == keys)
            both = jnp.concatenate(halves(recv[pl.ds(2 * at, 16)].reshape(256, 128)), axis=1)
            out = dot(hot, both) if out is None else out + dot(hot, both)
        partial[...] += (out[:, :128] + out[:, 128:]).reshape(2, 128, 128)

    swap = pltpu.make_async_remote_copy(
        partial.at[1 - core], partial_in, force_send.at[4], force_recv.at[4],
        device_id=partner, device_id_type=MESH,
    )
    swap.start()
    swap.wait()
    force = partial[core] + partial_in[...]
    force_ref[...] = force
    for s, r in ((0, 0), (1, o_rows - 1)):
        force_out[s, pl.ds(0, q_count), :] = force_ref[pl.ds(r, q_count, stride=o_rows), :]
    force_t = jnp.transpose(force)
    strip_out[0, pl.ds(0, 1), :] = force_t[:1]
    strip_out[1, pl.ds(0, 1), :] = force_t[127:]
    forces = []
    for side in range(4):
        opposite = (SOUTH, NORTH, EAST, WEST)[side]
        out, into = (force_out, force_in) if side < 2 else (strip_out, strip_in)
        copy = pltpu.make_async_remote_copy(
            out.at[side % 2], into.at[opposite % 2], force_send.at[side], force_recv.at[side],
            device_id=beside[side], device_id_type=MESH,
        )
        copy.start()
        forces.append(copy)

    depth = depth_ref[...]
    in_band = (lat > 0).astype(i32), (lat < n_lat - 1).astype(i32)
    north_depth = depth_in[NORTH] * in_band[0]
    south_depth = depth_in[SOUTH] * in_band[1]
    row_id, cell_id = iota(depth.shape, 0), iota(depth.shape, 1)
    roll = pltpu.roll
    sides_ref[NORTH] = jnp.where(row_id == 0, roll(north_depth, 1, 0), roll(depth, 1, 0))
    sides_ref[SOUTH] = jnp.where(
        row_id == o_rows - 1, roll(south_depth, o_rows - 1, 0), roll(depth, o_rows - 1, 0)
    )
    sides_ref[WEST] = jnp.where(cell_id == 0, roll(depth_in[WEST], 1, 1), roll(depth, 1, 1))
    sides_ref[EAST] = jnp.where(cell_id == 127, roll(depth_in[EAST], 127, 1), roll(depth, 127, 1))
    limits = [
        jnp.concatenate([jnp.broadcast_to(edge, (o_rows, 128))] * q_count, axis=0)
        for edge in (depth_in[WEST][:, 127:], depth_in[EAST][:, :1])
    ]
    strips = jnp.transpose(
        jnp.concatenate(
            [gain_strip_in[0], gain_strip_in[1], jnp.zeros((112, 128), f32)], axis=0
        )
    )
    for copy in forces:
        copy.wait()
    edges = north_depth[o_rows - 1 :], south_depth[:1]
    for s in range(2):
        for q in range(q_count):
            gain = jnp.broadcast_to(strips[:levels, s * 8 + q : s * 8 + q + 1], (levels, 128))
            value = row_in[s, q] + gain * force_in[s, pl.ds(q, 1), :]
            rows_ref[s, q] = jnp.where(level < edges[s], value, 0.0)
    level_lane = iota((128, 128), 1)
    edge = []
    for s in range(2):
        strip = jnp.transpose(jnp.broadcast_to(strip_in[s, pl.ds(0, 1), :], (128, 128)))
        value = col_in[s] + gain_in[s] * strip
        edge.append(jnp.where(level_lane < limits[s], value, 0.0))
    cols_ref[0] = jnp.where(level_lane < 64, edge[0], roll(edge[1], 64, 1))
    cols_ref[1] = jnp.where(level_lane < 64, roll(edge[0], 64, 1), edge[1])

    rest = pl.ds(0, 2 * (chips - 1))
    pltpu.make_async_copy(send.at[rest], send.at[rest], send_sem).wait()
    rest = pl.ds(0, chips - 1)
    pltpu.make_async_copy(meta.at[rest], meta.at[rest], meta_send_sem).wait()
    for q in range(q_count):
        copy_out(q).wait()


def couple(src, coupling, dest, block, atm, mask, depth, weights, inverses, ocean, n_lat, n_lon):
    pairs = src.shape[0]
    q_count, o_rows, levels, _ = inverses.shape
    chips = n_lat * n_lon // 2
    vmem, smem, hbm = (
        pl.BlockSpec(memory_space=s) for s in (pltpu.VMEM, pltpu.SMEM, pl.ANY)
    )
    shape = jax.ShapeDtypeStruct
    V, DMA = pltpu.VMEM, pltpu.SemaphoreType.DMA
    return pl.pallas_call(
        functools.partial(couple_kernel, n_lat, n_lon),
        in_specs=[smem, smem] + [vmem] * 5 + [hbm] * 3,
        out_specs=[hbm] + [vmem] * 5,
        out_shape=[
            shape((q_count, levels, o_rows, 128), f32),
            shape((128, 128), f32),
            shape((128, 128), f32),
            shape((2, q_count, levels, 128), f32),
            shape((2, 128, 128), f32),
            shape((4, o_rows, 128), i32),
        ],
        scratch_shapes=[
            V(weights.shape, bf16),
            V(inverses.shape, f32),
            V(ocean.shape, f32),
            V((levels * (o_rows + 1), 128), f32),
            V((mask.shape[0], 8, 128), f32),
            V((4 * pairs, 128), f32),
            V((2 * chips, 16, 128), f32),
            V((chips, 1, 128), f32),
            V((2 * chips, 16, 128), f32),
            V((chips, 1, 128), f32),
            V((2, 128, 128), f32),
            V((128, 128), f32),
            V((3, 128, 128), f32),
            V((2, 128, 128), f32),
            V((2, 8, 128), f32),
            V((2, 8, 128), f32),
            V((2, 8, 128), f32),
            V((2, q_count, levels, 128), f32),
            V((2, q_count, levels, 128), f32),
            V((2, 128, 128), f32),
            V((2, 128, 128), f32),
            V((2, 8, 128), f32),
            V((4, o_rows, 128), i32),
            V((2, 8, 128), f32),
            V((2, 8, 128), f32),
            DMA((14,)),
            DMA((10,)),
            DMA((12,)),
            DMA((12,)),
            DMA((5,)),
            DMA((5,)),
        ],
        compiler_params=pltpu.CompilerParams(
            collective_id=0, has_side_effects=True, vmem_limit_bytes=VMEM_BYTES
        ),
        name="couple",
    )(src, coupling, dest, block, atm, mask, depth, weights, inverses, ocean)


def finish_kernel(
    base_ref, force_ref, gain_ref, rows_ref, cols_ref, sides_ref, depth_ref, out_ref, slab, keep
):
    q, part = pl.program_id(0), pl.program_id(1)
    levels, o_rows = base_ref.shape[1:3]
    shape = (o_rows, 128)
    cell = iota(shape, 1)
    first = part * levels

    @pl.when(q == 0)
    def _():
        def weigh(l, carry):
            count = jnp.zeros(shape, f32)
            for s in range(4):
                count = count + jnp.where(first + l < sides_ref[s], diffusion_rate, 0.0)
            keep[first + l] = 1.0 - count
            return carry

        lax.fori_loop(0, levels, weigh, 0, unroll=4)

    here = pl.ds(q * o_rows, o_rows)
    together = slab.shape[0] // 2
    groups = levels // together

    def force(group):
        at = lax.rem(group, 2) * together
        for j in range(together):
            i = group * together + j
            l = first + i
            gain = jnp.take_along_axis(gain_ref[here, :], jnp.full(shape, l, i32), axis=1)
            mixed = base_ref[0, i] + gain * force_ref[here, :]
            slab[at + j, pl.ds(8, o_rows), :] = jnp.where(l < depth_ref[...], mixed, 0.0)
            slab[at + j, pl.ds(7, 1), :] = rows_ref[0, 0, pl.ds(i, 1), :]
            slab[at + j, pl.ds(8 + o_rows, 1), :] = rows_ref[1, 0, pl.ds(i, 1), :]

    def spread(group):
        at = lax.rem(group, 2) * together
        for j in range(together):
            i = group * together + j
            l = first + i
            spot = l % 64 + jnp.where(cell == 127, 64, 0)
            edge = jnp.take_along_axis(cols_ref[l // 64, here, :], spot, axis=1)
            mixed = slab[at + j, pl.ds(8, o_rows), :]
            west = jnp.where(cell == 0, edge, pltpu.roll(mixed, 1, 1))
            east = jnp.where(cell == 127, edge, pltpu.roll(mixed, 127, 1))
            beside = slab[at + j, pl.ds(7, o_rows), :] + slab[at + j, pl.ds(9, o_rows), :]
            value = keep[l] * mixed + diffusion_rate * (beside + (west + east))
            out_ref[0, i] = jnp.where(l < depth_ref[...], value, base_ref[0, i])

    force(0)

    def step(group, carry):
        spread(group)
        force(lax.rem(group + 1, groups))
        return carry

    lax.fori_loop(0, groups, step, 0)


def finish(base, force, gain, rows, cols, sides, depth):
    q_count, levels, o_rows, _ = base.shape
    parts = 2
    full = lambda a: pl.BlockSpec(a.shape, lambda q, p: (0,) * a.ndim)
    block = pl.BlockSpec((1, levels // parts, o_rows, 128), lambda q, p: (q, p, 0, 0))
    return pl.pallas_call(
        finish_kernel,
        grid=(q_count, parts),
        in_specs=[
            block,
            full(force),
            full(gain),
            pl.BlockSpec((2, 1, levels // parts, 128), lambda q, p: (0, q, p, 0)),
            full(cols),
            full(sides),
            full(depth),
        ],
        out_specs=block,
        out_shape=jax.ShapeDtypeStruct(base.shape, f32),
        scratch_shapes=[
            pltpu.VMEM((8, o_rows + 16, 128), f32),
            pltpu.VMEM((levels, o_rows, 128), f32),
        ],
        compiler_params=pltpu.CompilerParams(vmem_limit_bytes=VMEM_BYTES),
        name="finish",
    )(base, force, gain, rows, cols, sides, depth)


def on_device(
    atm_flux,
    sea_mask,
    src_block,
    dest_dev,
    dest_block,
    intersection_weights,
    coupling,
    inverses,
    ocean_state,
    depth_levels,
):
    n_lat, n_lon = lax.axis_size("lat"), lax.axis_size("lon")
    pairs = src_block.shape[0]
    q_count, levels, o_rows, cells = ocean_state.shape
    base, force, gain, rows, cols, sides = couple(
        src_block, coupling, dest_dev.reshape(1, pairs), dest_block.reshape(1, pairs),
        atm_flux, sea_mask, depth_levels, intersection_weights,
        inverses.reshape(q_count, o_rows, levels, levels),
        ocean_state, n_lat, n_lon,
    )
    return finish(base, force, gain, rows, cols, sides, depth_levels)


def solution(mesh):
    placed = (
        P(None, "lat", "lon"),
        P("lat", "lon"),
        P(("lat", "lon")),
        P(("lat", "lon"), None),
        P(("lat", "lon")),
        P(("lat", "lon"), None, None),
        P(),
        P(None, "lat", "lon", None, None),
        P(None, None, "lat", "lon"),
        P("lat", "lon"),
    )
    return jax.shard_map(
        on_device,
        mesh=mesh,
        in_specs=placed,
        out_specs=P(None, None, "lat", "lon"),
        check_vma=False,
    )
```

```python
import functools

import jax
import jax.numpy as jnp
from jax import lax
from jax.experimental import pallas as pl
from jax.experimental.pallas import tpu as pltpu
from jax.sharding import PartitionSpec as P

diffusion_rate = 0.2
CAP = 4
MESH = pl.DeviceIdType.MESH
NORTH, SOUTH, WEST, EAST = range(4)
ORDER = (2, 1, 3, 0)
f32, bf16, i32 = jnp.float32, jnp.bfloat16, jnp.int32
VMEM_BYTES = 62 << 20


def halves(x):
    high = x.astype(bf16)
    return high, (x - high.astype(f32)).astype(bf16)


def dot(a, b):
    return jnp.dot(a, b, preferred_element_type=f32)


def iota(shape, dim):
    return lax.broadcasted_iota(i32, shape, dim)


def one_hot(flags):
    return flags.astype(f32).astype(bf16)


def couple_kernel(
    n_lat, n_lon,
    src_ref, coupling_ref, dest_ref, block_ref, atm_ref, mask_ref, depth_ref,
    weights_hbm, inverses_hbm, ocean_hbm,
    base_hbm, force_ref, gain_ref, rows_ref, cols_ref, sides_ref,
    weights, inverses, ocean, skewed, table, contrib,
    send, meta, recv, recv_meta, partial, partial_in,
    packed, col_out, gain_out, force_out, strip_out, row_out,
    row_in, col_in, gain_in, gain_strip_in, depth_in, force_in, strip_in,
    load_sems, ship_sems, row_sems, halo_send, halo_recv, force_send, force_recv,
):
    chips = n_lat * n_lon // 2
    devices = 2 * chips
    lat, lon = lax.axis_index("lat"), lax.axis_index("lon")
    core = lon % 2
    my_chip = lat * (n_lon // 2) + lon // 2
    q_count = coupling_ref.shape[0]
    pairs = dest_ref.shape[1]
    levels = inverses.shape[2]
    skew = skewed.shape[0] // levels
    o_rows = depth_ref.shape[0]

    w_chunks = 8
    w_size = pairs // w_chunks

    def weight_copy(c):
        part = pl.ds(c * w_size, w_size)
        return pltpu.make_async_copy(weights_hbm.at[part], weights.at[part], load_sems.at[c])

    for c in range(w_chunks):
        weight_copy(c).start()
    inverse_copy = pltpu.make_async_copy(inverses_hbm, inverses, load_sems.at[w_chunks])
    ocean_copy = pltpu.make_async_copy(ocean_hbm, ocean, load_sems.at[w_chunks + 1])
    inverse_copy.start()
    ocean_copy.start()

    barrier = pltpu.get_barrier_semaphore()

    x_here, y_here = lon // 8, lon // 2 % 4

    def plane(dz, each, first=0):
        z = lax.rem(lat + dz, n_lat)
        xs = [lax.rem(x_here + dx, 4) * 8 + core for dx in range(4)]

        def line(dy, carry):
            y = lax.rem(y_here + dy, 4) * 2
            for dx in range(4):
                each(z, xs[dx] + y)
            return carry

        if dz == 0:
            for dx in range(1, 4):
                each(z, xs[dx] + y_here * 2)
            lax.fori_loop(1, 4, line, 0)
        else:
            lax.fori_loop(0, 4, line, 0)

    beside = {
        NORTH: ((lat + n_lat - 1) % n_lat, lon),
        SOUTH: ((lat + 1) % n_lat, lon),
        WEST: (lat, (lon + n_lon - 1) % n_lon),
        EAST: (lat, (lon + 1) % n_lon),
    }
    partner = (lat, lon + 1 - 2 * core)

    def greet(z, o):
        pl.semaphore_signal(barrier, inc=1, device_id=(z, o), device_id_type=MESH)

    for dz in range(n_lat):
        plane(dz, greet)
    for side in (WEST, EAST):
        pl.semaphore_signal(barrier, inc=1, device_id=beside[side], device_id_type=MESH)

    a_rows = mask_ref.shape[0]
    mask = mask_ref[...].astype(f32)
    masked = [atm_ref[f].astype(f32) * mask for f in range(atm_ref.shape[0])]
    for q in range(q_count):
        row = masked[0] * coupling_ref[q, 0]
        for f in range(1, atm_ref.shape[0]):
            row = row + masked[f] * coupling_ref[q, f]
        high, low = halves(row)
        contrib[pl.ds(q, a_rows, stride=8), :] = high.astype(f32)
        contrib[pl.ds(q_count + q, a_rows, stride=8), :] = low.astype(f32)
    table[...] = contrib[pl.ds(0, 8 * a_rows), :].reshape(a_rows, 8, 128)

    dest = dest_ref[...]
    named = (iota((devices, pairs), 0) == dest).astype(f32)
    before = one_hot(iota((pairs, pairs), 0) < iota((pairs, pairs), 1))
    rank = jnp.sum(named * dot(named.astype(bf16), before), axis=0, keepdims=True).astype(i32)
    lane = iota((128, pairs), 0)
    of_chip = one_hot(iota((chips, pairs), 0) == dest // 2)
    held = ((rank == lane % CAP) & (dest % 2 == lane % 32 // 16)).astype(f32)
    held = (held * block_ref[...].astype(f32)).astype(bf16)
    blocks = lax.dot_general(of_chip, held, (((1,), (1,)), ((), ())), preferred_element_type=f32)
    lanes = iota((chips, 128), 1)
    key = blocks + (lanes % 32 // 16 * 128 + lanes % 16 // CAP * o_rows).astype(f32)
    key = jnp.where(lanes // 32 == my_chip % 4, key, 0.0)
    for h in range(chips):
        meta[h] = key[h : h + 1]
    slot = dest * 8 + rank
    keys = jnp.concatenate([slot, slot + CAP], axis=1)

    def chunk_of_pairs(c, carry):
        weight_copy(c).wait()

        def four(i, carry):
            p = c * w_size + i * 4
            lefts = []
            for j in range(4):
                left = table[src_ref[p + j]]
                zero = jnp.zeros_like(left)
                lefts.append(jnp.concatenate([left, zero] if j % 2 == 0 else [zero, left], axis=1))
            left = jnp.concatenate(lefts, axis=0).astype(bf16)
            w = [weights[p + j] for j in range(4)]
            right = jnp.concatenate(
                [jnp.concatenate(w[:2], axis=0), jnp.concatenate(w[2:], axis=0)], axis=1
            )
            out = dot(left, right)
            for j in range(4):
                both = out[j * 8 : j * 8 + 8, j // 2 * 128 : j // 2 * 128 + 128]
                contrib[pl.ds(p + j, q_count, stride=pairs), :] = both[:q_count] + both[q_count:]
            return carry

        return lax.fori_loop(0, w_size // 4, four, carry, unroll=4)

    lax.fori_loop(0, w_chunks, chunk_of_pairs, 0)

    high, low = halves(
        jnp.concatenate(
            [contrib[pl.ds(h * 2 * pairs, 2 * pairs), :] for h in range(2)], axis=1
        )
    )
    chunk = devices * 8 // n_lat
    send_sem, meta_send_sem = ship_sems.at[0], ship_sems.at[1]
    recv_sems = [ship_sems.at[2 + dz] for dz in range(n_lat)]
    meta_recv_sems = [ship_sems.at[2 + n_lat + dz] for dz in range(n_lat)]

    def place(i):
        hot = one_hot(iota((chunk, 2 * pairs), 0) + i * chunk == keys)
        out = dot(hot, high) + dot(hot, low)
        for h in range(2):
            send[pl.ds(i * (chunk // 8), chunk // 8), pl.ds(h * 8, 8), :] = out[
                :, h * 128 : (h + 1) * 128
            ].reshape(chunk // 8, 8, 128)

    mine = pl.ds(2 * my_chip, 2)
    for n, dz in enumerate(ORDER):
        place(lax.rem(lat + dz, n_lat))
        if n == 0:
            pl.semaphore_wait(barrier, chips + 1)

        def ship(z, o):
            to = z * (n_lon // 2) + o // 2
            pltpu.make_async_remote_copy(
                send.at[pl.ds(2 * to, 2)], recv.at[mine], send_sem, recv_sems[dz],
                device_id=(z, o), device_id_type=MESH,
            ).start()
            pltpu.make_async_remote_copy(
                meta.at[to], recv_meta.at[my_chip], meta_send_sem, meta_recv_sems[dz],
                device_id=(z, o), device_id_type=MESH,
            ).start()

        plane(dz, ship)
    pltpu.make_async_copy(send.at[mine], recv.at[mine], recv_sems[0]).start()
    pltpu.make_async_copy(meta.at[my_chip], recv_meta.at[my_chip], meta_recv_sems[0]).start()

    inverse_copy.wait()
    ocean_copy.wait()
    packed[...] = jnp.zeros_like(packed)
    level = iota((levels, 128), 0)
    lane_id = iota((levels, 128), 1)
    low_levels = pl.ds(0, levels)

    def copy_out(q):
        return pltpu.make_async_copy(ocean.at[q], base_hbm.at[q], load_sems.at[w_chunks + 2 + q])

    def row_copy(side, q):
        return pltpu.make_async_remote_copy(
            row_out.at[side, q], row_in.at[1 - side, q],
            row_sems.at[side, q], row_sems.at[3 - side, q],
            device_id=beside[side], device_id_type=MESH,
        )

    def field(q, carry):
        def skew_in(l, carry):
            skewed[pl.ds(l * skew, o_rows), :] = ocean[q, l]
            return carry

        lax.fori_loop(0, levels, skew_in, 0, unroll=8)

        def mix(r, carry):
            i = q * o_rows + r
            column = pl.ds(r, levels, stride=skew)
            state = skewed[column, :]
            active = level < depth_ref[pl.ds(r, 1), :]
            inverse = inverses[q, r]
            left = jnp.concatenate(halves(inverse), axis=0)
            right = jnp.concatenate(halves(jnp.where(active, state, 0.0)), axis=1)
            out = dot(left, right)
            solved = out[:levels, :128] + (out[:levels, 128:] + out[levels:, :128])
            mixed = jnp.where(active, solved, state)
            skewed[column, :] = mixed
            turned = pltpu.roll(mixed, i, 1)
            packed[0, low_levels, :] = jnp.where(lane_id == i, turned, packed[0, low_levels, :])
            last = lax.rem(i + 127, 128)
            packed[1, low_levels, :] = jnp.where(lane_id == last, turned, packed[1, low_levels, :])
            gain = jnp.broadcast_to(inverse[:, :1], mixed.shape)
            packed[2, low_levels, :] = jnp.where(lane_id == i, gain, packed[2, low_levels, :])
            return carry

        lax.fori_loop(0, o_rows, mix, 0, unroll=4)

        def skew_out(l, carry):
            ocean[q, l] = skewed[pl.ds(l * skew, o_rows), :]
            return carry

        lax.fori_loop(0, levels, skew_out, 0, unroll=8)
        for s, r in ((0, 0), (1, o_rows - 1)):
            row_out[s, q] = skewed[pl.ds(r, levels, stride=skew), :]
        copy_out(q).start()
        for side in (NORTH, SOUTH):
            row_copy(side, q).start()
        return carry

    lax.fori_loop(0, q_count, field, 0)
    col_out[0] = jnp.transpose(packed[0])
    col_out[1] = jnp.transpose(pltpu.roll(packed[1], 1, 1))
    gain_ref[...] = jnp.transpose(packed[2])
    for s, r in ((0, 0), (1, o_rows - 1)):
        gain_out[s, pl.ds(0, q_count), :] = gain_ref[pl.ds(r, q_count, stride=o_rows), :]

    copies = []

    def hand(side, source, target):
        opposite = (SOUTH, NORTH, EAST, WEST)[side]
        n = len(copies)
        copy = pltpu.make_async_remote_copy(
            source, target(opposite), halo_send.at[n], halo_recv.at[n],
            device_id=beside[side], device_id_type=MESH,
        )
        copy.start()
        copies.append(copy)

    for side in range(4):
        hand(side, depth_ref, lambda o: depth_in.at[o])
    for side in (NORTH, SOUTH):
        hand(side, gain_out.at[side], lambda o: gain_strip_in.at[o])
    for side in (WEST, EAST):
        hand(side, col_out.at[side - 2], lambda o: col_in.at[o - 2])
        hand(side, gain_ref, lambda o: gain_in.at[o - 2])

    partial[...] = jnp.zeros_like(partial)
    per_plane = chips // n_lat
    for dz in ORDER:
        z = lax.rem(lat + n_lat - dz, n_lat)
        some = pl.ds(z * per_plane, per_plane)
        pltpu.make_async_copy(recv_meta.at[some], recv_meta.at[some], meta_recv_sems[dz]).wait()
        some = pl.ds(z * 2 * per_plane, 2 * per_plane)
        pltpu.make_async_copy(recv.at[some], recv.at[some], recv_sems[dz]).wait()
        out = None
        for i in range(per_plane // 8):
            at = z * per_plane + i * 8
            keys = jnp.concatenate(
                [jnp.sum(recv_meta[pl.ds(at + 4 * h, 4)], axis=0) for h in range(2)], axis=1
            ).astype(i32)
            hot = one_hot(iota((256, 256), 0) == keys)
            both = jnp.concatenate(halves(recv[pl.ds(2 * at, 16)].reshape(256, 128)), axis=1)
            out = dot(hot, both) if out is None else out + dot(hot, both)
        partial[...] += (out[:, :128] + out[:, 128:]).reshape(2, 128, 128)

    swap = pltpu.make_async_remote_copy(
        partial.at[1 - core], partial_in, force_send.at[4], force_recv.at[4],
        device_id=partner, device_id_type=MESH,
    )
    swap.start()
    swap.wait()
    force = partial[core] + partial_in[...]
    force_ref[...] = force
    for s, r in ((0, 0), (1, o_rows - 1)):
        force_out[s, pl.ds(0, q_count), :] = force_ref[pl.ds(r, q_count, stride=o_rows), :]
    force_t = jnp.transpose(force)
    strip_out[0, pl.ds(0, 1), :] = force_t[:1]
    strip_out[1, pl.ds(0, 1), :] = force_t[127:]
    forces = []
    for side in range(4):
        opposite = (SOUTH, NORTH, EAST, WEST)[side]
        out, into = (force_out, force_in) if side < 2 else (strip_out, strip_in)
        copy = pltpu.make_async_remote_copy(
            out.at[side % 2], into.at[opposite % 2], force_send.at[side], force_recv.at[side],
            device_id=beside[side], device_id_type=MESH,
        )
        copy.start()
        forces.append(copy)

    for copy in copies:
        copy.wait()
    for q in range(q_count):
        for side in (NORTH, SOUTH):
            row_copy(side, q).wait()
    depth = depth_ref[...]
    in_band = (lat > 0).astype(i32), (lat < n_lat - 1).astype(i32)
    north_depth = depth_in[NORTH] * in_band[0]
    south_depth = depth_in[SOUTH] * in_band[1]
    row_id, cell_id = iota(depth.shape, 0), iota(depth.shape, 1)
    roll = pltpu.roll
    sides_ref[NORTH] = jnp.where(row_id == 0, roll(north_depth, 1, 0), roll(depth, 1, 0))
    sides_ref[SOUTH] = jnp.where(
        row_id == o_rows - 1, roll(south_depth, o_rows - 1, 0), roll(depth, o_rows - 1, 0)
    )
    sides_ref[WEST] = jnp.where(cell_id == 0, roll(depth_in[WEST], 1, 1), roll(depth, 1, 1))
    sides_ref[EAST] = jnp.where(cell_id == 127, roll(depth_in[EAST], 127, 1), roll(depth, 127, 1))
    limits = [
        jnp.concatenate([jnp.broadcast_to(edge, (o_rows, 128))] * q_count, axis=0)
        for edge in (depth_in[WEST][:, 127:], depth_in[EAST][:, :1])
    ]
    strips = jnp.transpose(
        jnp.concatenate(
            [gain_strip_in[0], gain_strip_in[1], jnp.zeros((112, 128), f32)], axis=0
        )
    )
    for copy in forces:
        copy.wait()
    edges = north_depth[o_rows - 1 :], south_depth[:1]
    for s in range(2):
        for q in range(q_count):
            gain = jnp.broadcast_to(strips[:levels, s * 8 + q : s * 8 + q + 1], (levels, 128))
            value = row_in[s, q] + gain * force_in[s, pl.ds(q, 1), :]
            rows_ref[s, q] = jnp.where(level < edges[s], value, 0.0)
    level_lane = iota((128, 128), 1)
    edge = []
    for s in range(2):
        strip = jnp.transpose(jnp.broadcast_to(strip_in[s, pl.ds(0, 1), :], (128, 128)))
        value = col_in[s] + gain_in[s] * strip
        edge.append(jnp.where(level_lane < limits[s], value, 0.0))
    cols_ref[0] = jnp.where(level_lane < 64, edge[0], roll(edge[1], 64, 1))
    cols_ref[1] = jnp.where(level_lane < 64, roll(edge[0], 64, 1), edge[1])

    rest = pl.ds(0, 2 * (chips - 1))
    pltpu.make_async_copy(send.at[rest], send.at[rest], send_sem).wait()
    rest = pl.ds(0, chips - 1)
    pltpu.make_async_copy(meta.at[rest], meta.at[rest], meta_send_sem).wait()
    for q in range(q_count):
        copy_out(q).wait()


def couple(src, coupling, dest, block, atm, mask, depth, weights, inverses, ocean, n_lat, n_lon):
    pairs = src.shape[0]
    q_count, o_rows, levels, _ = inverses.shape
    chips = n_lat * n_lon // 2
    vmem, smem, hbm = (
        pl.BlockSpec(memory_space=s) for s in (pltpu.VMEM, pltpu.SMEM, pl.ANY)
    )
    shape = jax.ShapeDtypeStruct
    V, DMA = pltpu.VMEM, pltpu.SemaphoreType.DMA
    return pl.pallas_call(
        functools.partial(couple_kernel, n_lat, n_lon),
        in_specs=[smem, smem] + [vmem] * 5 + [hbm] * 3,
        out_specs=[hbm] + [vmem] * 5,
        out_shape=[
            shape((q_count, levels, o_rows, 128), f32),
            shape((128, 128), f32),
            shape((128, 128), f32),
            shape((2, q_count, levels, 128), f32),
            shape((2, 128, 128), f32),
            shape((4, o_rows, 128), i32),
        ],
        scratch_shapes=[
            V(weights.shape, bf16),
            V(inverses.shape, f32),
            V(ocean.shape, f32),
            V((levels * (o_rows + 1), 128), f32),
            V((mask.shape[0], 8, 128), f32),
            V((4 * pairs, 128), f32),
            V((2 * chips, 16, 128), f32),
            V((chips, 1, 128), f32),
            V((2 * chips, 16, 128), f32),
            V((chips, 1, 128), f32),
            V((2, 128, 128), f32),
            V((128, 128), f32),
            V((3, 128, 128), f32),
            V((2, 128, 128), f32),
            V((2, 8, 128), f32),
            V((2, 8, 128), f32),
            V((2, 8, 128), f32),
            V((2, q_count, levels, 128), f32),
            V((2, q_count, levels, 128), f32),
            V((2, 128, 128), f32),
            V((2, 128, 128), f32),
            V((2, 8, 128), f32),
            V((4, o_rows, 128), i32),
            V((2, 8, 128), f32),
            V((2, 8, 128), f32),
            DMA((14,)),
            DMA((10,)),
            DMA((4, q_count)),
            DMA((12,)),
            DMA((12,)),
            DMA((5,)),
            DMA((5,)),
        ],
        compiler_params=pltpu.CompilerParams(
            collective_id=0, has_side_effects=True, vmem_limit_bytes=VMEM_BYTES
        ),
        name="couple",
    )(src, coupling, dest, block, atm, mask, depth, weights, inverses, ocean)


def finish_kernel(
    base_ref, force_ref, gain_ref, rows_ref, cols_ref, sides_ref, depth_ref, out_ref,
    slabs, splits, sums, keep,
):
    q = pl.program_id(0)
    levels, o_rows = base_ref.shape[1:3]
    shape = (o_rows, 128)
    cell = iota(shape, 1)
    here = pl.ds(q * o_rows, o_rows)
    group = slabs[0].shape[0]
    groups = levels // group
    first, last = cell == 0, cell == 127
    rim = first | last
    far = jnp.where(last, 64, 0)
    apart = iota((256, 128), 0) % 128 - iota((256, 128), 1)
    beside = one_hot((apart == 1) | (apart == -1))

    @pl.when(q == 0)
    def _():
        def weigh(l, carry):
            count = jnp.zeros(shape, f32)
            for s in range(4):
                count = count + jnp.where(l < sides_ref[s], diffusion_rate, 0.0)
            keep[l] = 1.0 - count
            return carry

        lax.fori_loop(0, levels, weigh, 0, unroll=4)

    def force(n, j):
        slab, split, l = slabs[n % 2], splits[n % 2], n * group + j
        gain = jnp.take_along_axis(gain_ref[here, :], jnp.full(shape, l, i32), axis=1)
        mixed = base_ref[0, l] + gain * force_ref[here, :]
        mixed = jnp.where(l < depth_ref[...], mixed, 0.0)
        slab[j, pl.ds(8, o_rows), :] = mixed
        slab[j, pl.ds(7, 1), :] = rows_ref[0, 0, pl.ds(l, 1), :]
        slab[j, pl.ds(8 + o_rows, 1), :] = rows_ref[1, 0, pl.ds(l, 1), :]
        high, low = halves(mixed)
        split[pl.ds(j * o_rows, o_rows), pl.ds(0, 128)] = high
        split[pl.ds(j * o_rows, o_rows), pl.ds(128, 128)] = low

    def spread(n, j):
        slab, total, l = slabs[n % 2], sums[n % 2], n * group + j
        edge = jnp.take_along_axis(cols_ref[l // 64, here, :], far + l % 64, axis=1)
        near = slab[j, pl.ds(7, o_rows), :] + slab[j, pl.ds(9, o_rows), :]
        near = near + total[pl.ds(j * o_rows, o_rows), :]
        near = near + jnp.where(rim, edge, 0.0)
        value = keep[l] * slab[j, pl.ds(8, o_rows), :] + diffusion_rate * near
        out_ref[0, l] = jnp.where(l < depth_ref[...], value, base_ref[0, l])

    for j in range(group):
        force(0, j)
    for n in range(groups):
        sums[n % 2][...] = dot(splits[n % 2][...], beside)
        for j in range(group):
            if n + 1 < groups:
                force(n + 1, j)
            spread(n, j)


def finish(base, force, gain, rows, cols, sides, depth):
    q_count, levels, o_rows, _ = base.shape
    group = 16
    full = lambda a: pl.BlockSpec(a.shape, lambda q: (0,) * a.ndim)
    block = pl.BlockSpec((1, levels, o_rows, 128), lambda q: (q, 0, 0, 0))
    V = pltpu.VMEM
    return pl.pallas_call(
        finish_kernel,
        grid=(q_count,),
        in_specs=[
            block,
            full(force),
            full(gain),
            pl.BlockSpec((2, 1, levels, 128), lambda q: (0, q, 0, 0)),
            full(cols),
            full(sides),
            full(depth),
        ],
        out_specs=block,
        out_shape=jax.ShapeDtypeStruct(base.shape, f32),
        scratch_shapes=[
            [V((group, o_rows + 16, 128), f32)] * 2,
            [V((group * o_rows, 256), bf16)] * 2,
            [V((group * o_rows, 128), f32)] * 2,
            V((levels, o_rows, 128), f32),
        ],
        compiler_params=pltpu.CompilerParams(vmem_limit_bytes=VMEM_BYTES),
        name="finish",
    )(base, force, gain, rows, cols, sides, depth)


def on_device(
    atm_flux,
    sea_mask,
    src_block,
    dest_dev,
    dest_block,
    intersection_weights,
    coupling,
    inverses,
    ocean_state,
    depth_levels,
):
    n_lat, n_lon = lax.axis_size("lat"), lax.axis_size("lon")
    pairs = src_block.shape[0]
    q_count, levels, o_rows, cells = ocean_state.shape
    base, force, gain, rows, cols, sides = couple(
        src_block, coupling, dest_dev.reshape(1, pairs), dest_block.reshape(1, pairs),
        atm_flux, sea_mask, depth_levels, intersection_weights,
        inverses.reshape(q_count, o_rows, levels, levels),
        ocean_state, n_lat, n_lon,
    )
    return finish(base, force, gain, rows, cols, sides, depth_levels)


def solution(mesh):
    placed = (
        P(None, "lat", "lon"),
        P("lat", "lon"),
        P(("lat", "lon")),
        P(("lat", "lon"), None),
        P(("lat", "lon")),
        P(("lat", "lon"), None, None),
        P(),
        P(None, "lat", "lon", None, None),
        P(None, None, "lat", "lon"),
        P("lat", "lon"),
    )
    return jax.shard_map(
        on_device,
        mesh=mesh,
        in_specs=placed,
        out_specs=P(None, None, "lat", "lon"),
        check_vma=False,
    )
```

```python
import functools

import jax
import jax.numpy as jnp
from jax import lax
from jax.experimental import pallas as pl
from jax.experimental.pallas import tpu as pltpu
from jax.sharding import PartitionSpec as P

diffusion_rate = 0.2
CAP = 4
MESH = pl.DeviceIdType.MESH
NORTH, SOUTH, WEST, EAST = range(4)
ORDER = (2, 1, 3, 0)
f32, bf16, i32 = jnp.float32, jnp.bfloat16, jnp.int32
VMEM_BYTES = 62 << 20


def halves(x):
    high = x.astype(bf16)
    return high, (x - high.astype(f32)).astype(bf16)


def dot(a, b):
    return jnp.dot(a, b, preferred_element_type=f32)


def iota(shape, dim):
    return lax.broadcasted_iota(i32, shape, dim)


def one_hot(flags):
    return flags.astype(f32).astype(bf16)


def couple_kernel(
    n_lat, n_lon,
    src_ref, coupling_ref, dest_ref, block_ref, atm_ref, mask_ref, depth_ref,
    weights_hbm, inverses_hbm, ocean_hbm,
    base_hbm, keep_hbm, force_ref, gains_ref, rows_ref, cols_ref,
    weights, inverses, ocean, skewed, table, contrib,
    send, meta, recv, recv_meta, partial, partial_in,
    packed, col_out, gain_ref, gain_out, force_out, strip_out, row_out,
    row_in, col_in, gain_in, gain_strip_in, depth_in, force_in, strip_in, sides_ref, keep,
    load_sems, ship_sems, row_sems, depth_sems, halo_send, halo_recv, force_send, force_recv,
):
    chips = n_lat * n_lon // 2
    devices = 2 * chips
    lat, lon = lax.axis_index("lat"), lax.axis_index("lon")
    core = lon % 2
    my_chip = lat * (n_lon // 2) + lon // 2
    q_count = coupling_ref.shape[0]
    pairs = dest_ref.shape[1]
    levels = inverses.shape[2]
    skew = skewed.shape[0] // levels
    o_rows = depth_ref.shape[0]

    w_chunks = 8
    w_size = pairs // w_chunks

    def weight_copy(c):
        part = pl.ds(c * w_size, w_size)
        return pltpu.make_async_copy(weights_hbm.at[part], weights.at[part], load_sems.at[c])

    for c in range(w_chunks):
        weight_copy(c).start()
    inverse_copy = pltpu.make_async_copy(inverses_hbm, inverses, load_sems.at[w_chunks])
    ocean_copy = pltpu.make_async_copy(ocean_hbm, ocean, load_sems.at[w_chunks + 1])
    inverse_copy.start()
    ocean_copy.start()

    barrier = pltpu.get_barrier_semaphore()

    x_here, y_here = lon // 8, lon // 2 % 4

    def plane(dz, each, first=0):
        z = lax.rem(lat + dz, n_lat)
        xs = [lax.rem(x_here + dx, 4) * 8 + core for dx in range(4)]

        def line(dy, carry):
            y = lax.rem(y_here + dy, 4) * 2
            for dx in range(4):
                each(z, xs[dx] + y)
            return carry

        if dz == 0:
            for dx in range(1, 4):
                each(z, xs[dx] + y_here * 2)
            lax.fori_loop(1, 4, line, 0)
        else:
            lax.fori_loop(0, 4, line, 0)

    beside = {
        NORTH: ((lat + n_lat - 1) % n_lat, lon),
        SOUTH: ((lat + 1) % n_lat, lon),
        WEST: (lat, (lon + n_lon - 1) % n_lon),
        EAST: (lat, (lon + 1) % n_lon),
    }
    partner = (lat, lon + 1 - 2 * core)

    def greet(z, o):
        pl.semaphore_signal(barrier, inc=1, device_id=(z, o), device_id_type=MESH)

    for dz in range(n_lat):
        plane(dz, greet)
    slant = [(beside[side][0], partner[1]) for side in (NORTH, SOUTH)]
    for other in (beside[WEST], beside[EAST], *slant):
        pl.semaphore_signal(barrier, inc=1, device_id=other, device_id_type=MESH)

    a_rows = mask_ref.shape[0]
    mask = mask_ref[...].astype(f32)
    masked = [atm_ref[f].astype(f32) * mask for f in range(atm_ref.shape[0])]
    for q in range(q_count):
        row = masked[0] * coupling_ref[q, 0]
        for f in range(1, atm_ref.shape[0]):
            row = row + masked[f] * coupling_ref[q, f]
        high, low = halves(row)
        contrib[pl.ds(q, a_rows, stride=8), :] = high.astype(f32)
        contrib[pl.ds(q_count + q, a_rows, stride=8), :] = low.astype(f32)
    table[...] = contrib[pl.ds(0, 8 * a_rows), :].reshape(a_rows, 8, 128)

    dest = dest_ref[...]
    named = (iota((devices, pairs), 0) == dest).astype(f32)
    before = one_hot(iota((pairs, pairs), 0) < iota((pairs, pairs), 1))
    rank = jnp.sum(named * dot(named.astype(bf16), before), axis=0, keepdims=True).astype(i32)
    lane = iota((128, pairs), 0)
    of_chip = one_hot(iota((chips, pairs), 0) == dest // 2)
    held = ((rank == lane % CAP) & (dest % 2 == lane % 32 // 16)).astype(f32)
    held = (held * block_ref[...].astype(f32)).astype(bf16)
    blocks = lax.dot_general(of_chip, held, (((1,), (1,)), ((), ())), preferred_element_type=f32)
    lanes = iota((chips, 128), 1)
    key = blocks + (lanes % 32 // 16 * 128 + lanes % 16 // CAP * o_rows).astype(f32)
    key = jnp.where(lanes // 32 == my_chip % 4, key, 0.0)
    for h in range(chips):
        meta[h] = key[h : h + 1]
    slot = dest * 8 + rank
    keys = jnp.concatenate([slot, slot + CAP], axis=1)

    def chunk_of_pairs(c, carry):
        weight_copy(c).wait()

        def four(i, carry):
            p = c * w_size + i * 4
            lefts = []
            for j in range(4):
                left = table[src_ref[p + j]]
                zero = jnp.zeros_like(left)
                lefts.append(jnp.concatenate([left, zero] if j % 2 == 0 else [zero, left], axis=1))
            left = jnp.concatenate(lefts, axis=0).astype(bf16)
            w = [weights[p + j] for j in range(4)]
            right = jnp.concatenate(
                [jnp.concatenate(w[:2], axis=0), jnp.concatenate(w[2:], axis=0)], axis=1
            )
            out = dot(left, right)
            for j in range(4):
                both = out[j * 8 : j * 8 + 8, j // 2 * 128 : j // 2 * 128 + 128]
                contrib[pl.ds(p + j, q_count, stride=pairs), :] = both[:q_count] + both[q_count:]
            return carry

        return lax.fori_loop(0, w_size // 4, four, carry, unroll=4)

    lax.fori_loop(0, w_chunks, chunk_of_pairs, 0)

    high, low = halves(
        jnp.concatenate(
            [contrib[pl.ds(h * 2 * pairs, 2 * pairs), :] for h in range(2)], axis=1
        )
    )
    chunk = devices * 8 // n_lat
    send_sem, meta_send_sem = ship_sems.at[0], ship_sems.at[1]
    recv_sems = [ship_sems.at[2 + dz] for dz in range(n_lat)]
    meta_recv_sems = [ship_sems.at[2 + n_lat + dz] for dz in range(n_lat)]

    def place(i):
        hot = one_hot(iota((chunk, 2 * pairs), 0) + i * chunk == keys)
        out = dot(hot, high) + dot(hot, low)
        for h in range(2):
            send[pl.ds(i * (chunk // 8), chunk // 8), pl.ds(h * 8, 8), :] = out[
                :, h * 128 : (h + 1) * 128
            ].reshape(chunk // 8, 8, 128)

    depth_copies = [
        pltpu.make_async_remote_copy(
            depth_ref, depth_in.at[(SOUTH, NORTH, EAST, WEST)[side]],
            depth_sems.at[side], depth_sems.at[4 + side],
            device_id=beside[side], device_id_type=MESH,
        )
        for side in range(4)
    ]
    mine = pl.ds(2 * my_chip, 2)
    for n, dz in enumerate(ORDER):
        place(lax.rem(lat + dz, n_lat))
        if n == 0:
            pl.semaphore_wait(barrier, chips + 3)
            for copy in depth_copies:
                copy.start()

        def ship(z, o):
            to = z * (n_lon // 2) + o // 2
            pltpu.make_async_remote_copy(
                send.at[pl.ds(2 * to, 2)], recv.at[mine], send_sem, recv_sems[dz],
                device_id=(z, o), device_id_type=MESH,
            ).start()
            pltpu.make_async_remote_copy(
                meta.at[to], recv_meta.at[my_chip], meta_send_sem, meta_recv_sems[dz],
                device_id=(z, o), device_id_type=MESH,
            ).start()

        plane(dz, ship)
    pltpu.make_async_copy(send.at[mine], recv.at[mine], recv_sems[0]).start()
    pltpu.make_async_copy(meta.at[my_chip], recv_meta.at[my_chip], meta_recv_sems[0]).start()

    inverse_copy.wait()
    ocean_copy.wait()
    packed[...] = jnp.zeros_like(packed)
    level = iota((levels, 128), 0)
    lane_id = iota((levels, 128), 1)
    low_levels = pl.ds(0, levels)

    def copy_out(q):
        return pltpu.make_async_copy(ocean.at[q], base_hbm.at[q], load_sems.at[w_chunks + 2 + q])

    def row_copy(side, q):
        return pltpu.make_async_remote_copy(
            row_out.at[side, q], row_in.at[1 - side, q],
            row_sems.at[side, q], row_sems.at[3 - side, q],
            device_id=beside[side], device_id_type=MESH,
        )

    def field(q, carry):
        def skew_in(l, carry):
            skewed[pl.ds(l * skew, o_rows), :] = ocean[q, l]
            return carry

        lax.fori_loop(0, levels, skew_in, 0, unroll=8)

        def mix(r, carry):
            i = q * o_rows + r
            column = pl.ds(r, levels, stride=skew)
            state = skewed[column, :]
            active = level < depth_ref[pl.ds(r, 1), :]
            inverse = inverses[q, r]
            left = jnp.concatenate(halves(inverse), axis=0)
            right = jnp.concatenate(halves(jnp.where(active, state, 0.0)), axis=1)
            out = dot(left, right)
            solved = out[:levels, :128] + (out[:levels, 128:] + out[levels:, :128])
            mixed = jnp.where(active, solved, state)
            skewed[column, :] = mixed
            turned = pltpu.roll(mixed, i, 1)
            packed[0, low_levels, :] = jnp.where(lane_id == i, turned, packed[0, low_levels, :])
            last = lax.rem(i + 127, 128)
            packed[1, low_levels, :] = jnp.where(lane_id == last, turned, packed[1, low_levels, :])
            gain = jnp.broadcast_to(inverse[:, :1], mixed.shape)
            packed[2, low_levels, :] = jnp.where(lane_id == i, gain, packed[2, low_levels, :])
            return carry

        lax.fori_loop(0, o_rows, mix, 0, unroll=4)

        def skew_out(l, carry):
            ocean[q, l] = skewed[pl.ds(l * skew, o_rows), :]
            return carry

        lax.fori_loop(0, levels, skew_out, 0, unroll=8)
        for s, r in ((0, 0), (1, o_rows - 1)):
            row_out[s, q] = skewed[pl.ds(r, levels, stride=skew), :]
        copy_out(q).start()
        for side in (NORTH, SOUTH):
            row_copy(side, q).start()
        return carry

    lax.fori_loop(0, q_count, field, 0)
    col_out[0] = jnp.transpose(packed[0])
    col_out[1] = jnp.transpose(pltpu.roll(packed[1], 1, 1))
    gain_ref[...] = jnp.transpose(packed[2])
    for s, r in ((0, 0), (1, o_rows - 1)):
        gain_out[s, pl.ds(0, q_count), :] = gain_ref[pl.ds(r, q_count, stride=o_rows), :]

    copies = []

    def hand(side, source, target):
        opposite = (SOUTH, NORTH, EAST, WEST)[side]
        n = len(copies)
        copy = pltpu.make_async_remote_copy(
            source, target(opposite), halo_send.at[n], halo_recv.at[n],
            device_id=beside[side], device_id_type=MESH,
        )
        copy.start()
        copies.append(copy)

    for side in (NORTH, SOUTH):
        hand(side, gain_out.at[side], lambda o: gain_strip_in.at[o])
    for side in (WEST, EAST):
        hand(side, col_out.at[side - 2], lambda o: col_in.at[o - 2])
        hand(side, gain_ref, lambda o: gain_in.at[o - 2])

    for copy in depth_copies:
        copy.wait()
    depth = depth_ref[...]
    in_band = (lat > 0).astype(i32), (lat < n_lat - 1).astype(i32)
    north_depth = depth_in[NORTH] * in_band[0]
    south_depth = depth_in[SOUTH] * in_band[1]
    row_id, cell_id = iota(depth.shape, 0), iota(depth.shape, 1)
    roll = pltpu.roll
    sides_ref[NORTH] = jnp.where(row_id == 0, roll(north_depth, 1, 0), roll(depth, 1, 0))
    sides_ref[SOUTH] = jnp.where(
        row_id == o_rows - 1, roll(south_depth, o_rows - 1, 0), roll(depth, o_rows - 1, 0)
    )
    sides_ref[WEST] = jnp.where(cell_id == 0, roll(depth_in[WEST], 1, 1), roll(depth, 1, 1))
    sides_ref[EAST] = jnp.where(cell_id == 127, roll(depth_in[EAST], 127, 1), roll(depth, 127, 1))

    def weigh(l, carry):
        count = jnp.zeros(depth.shape, f32)
        for s in range(4):
            count = count + jnp.where(l < sides_ref[s], diffusion_rate, 0.0)
        keep[l] = 1.0 - count
        return carry

    lax.fori_loop(0, levels, weigh, 0, unroll=4)
    keep_copy = pltpu.make_async_copy(keep, keep_hbm, load_sems.at[w_chunks + 2 + q_count])
    keep_copy.start()
    for q in range(q_count):
        gain = packed[2, low_levels, :]
        gain = gain if q == 0 else roll(gain, 128 - q * o_rows, 1)
        high, low = (part.astype(f32) for part in halves(gain))
        third = lane_id // o_rows
        gain = jnp.where(third == 0, high, jnp.where(third == 1, roll(low, 32, 1), roll(high, 64, 1)))
        gains_ref[q] = jnp.where(third == 3, 0.0, gain)

    partial[...] = jnp.zeros_like(partial)
    per_plane = chips // n_lat
    for dz in ORDER:
        z = lax.rem(lat + n_lat - dz, n_lat)
        some = pl.ds(z * per_plane, per_plane)
        pltpu.make_async_copy(recv_meta.at[some], recv_meta.at[some], meta_recv_sems[dz]).wait()
        some = pl.ds(z * 2 * per_plane, 2 * per_plane)
        pltpu.make_async_copy(recv.at[some], recv.at[some], recv_sems[dz]).wait()
        out = None
        for i in range(per_plane // 8):
            at = z * per_plane + i * 8
            keys = jnp.concatenate(
                [jnp.sum(recv_meta[pl.ds(at + 4 * h, 4)], axis=0) for h in range(2)], axis=1
            ).astype(i32)
            hot = one_hot(iota((256, 256), 0) == keys)
            both = jnp.concatenate(halves(recv[pl.ds(2 * at, 16)].reshape(256, 128)), axis=1)
            out = dot(hot, both) if out is None else out + dot(hot, both)
        partial[...] += (out[:, :128] + out[:, 128:]).reshape(2, 128, 128)

    own, other = partial[core], partial[1 - core]
    for e, mine_or in enumerate((core, 1 - core)):
        for side, r in ((0, 0), (1, o_rows - 1)):
            force_out[e, side, pl.ds(0, q_count), :] = partial[
                mine_or, pl.ds(r, q_count, stride=o_rows), :
            ]
    turned, turned_other = jnp.transpose(own), jnp.transpose(other)
    on_left = core == 0
    strip_out[0, pl.ds(0, 1), :] = turned[:1]
    strip_out[1, pl.ds(0, 1), :] = turned[127:]
    strip_out[2, pl.ds(0, 1), :] = jnp.where(on_left, turned_other[127:], turned_other[:1])
    inner = jnp.where(on_left, turned_other[:1], turned_other[127:])
    hops = [
        (partial.at[1 - core], partial_in, partner),
        (force_out.at[0, 0], force_in.at[0, 1], beside[NORTH]),
        (force_out.at[0, 1], force_in.at[0, 0], beside[SOUTH]),
        (force_out.at[1, 0], force_in.at[1, 1], slant[0]),
        (force_out.at[1, 1], force_in.at[1, 0], slant[1]),
        (strip_out.at[0], strip_in.at[1], beside[WEST]),
        (strip_out.at[1], strip_in.at[0], beside[EAST]),
        (strip_out.at[2], strip_in.at[2], (lat, lax.rem(lon + n_lon + 2 - 4 * core, n_lon))),
    ]
    forces = []
    for n, (source, target, device) in enumerate(hops):
        copy = pltpu.make_async_remote_copy(
            source, target, force_send.at[n], force_recv.at[n],
            device_id=device, device_id_type=MESH,
        )
        copy.start()
        forces.append(copy)

    for copy in copies:
        copy.wait()
    for q in range(q_count):
        for side in (NORTH, SOUTH):
            row_copy(side, q).wait()
    limits = [
        jnp.concatenate([jnp.broadcast_to(edge, (o_rows, 128))] * q_count, axis=0)
        for edge in (depth_in[WEST][:, 127:], depth_in[EAST][:, :1])
    ]
    strips = jnp.transpose(
        jnp.concatenate(
            [gain_strip_in[0], gain_strip_in[1], jnp.zeros((112, 128), f32)], axis=0
        )
    )
    for copy in forces:
        copy.wait()
    force_ref[...] = own + partial_in[...]
    edges = north_depth[o_rows - 1 :], south_depth[:1]
    for s in range(2):
        for q in range(q_count):
            gain = jnp.broadcast_to(strips[:levels, s * 8 + q : s * 8 + q + 1], (levels, 128))
            force = force_in[0, s, pl.ds(q, 1), :] + force_in[1, s, pl.ds(q, 1), :]
            value = row_in[s, q] + gain * force
            rows_ref[s, q] = jnp.where(level < edges[s], value, 0.0)
    level_lane = iota((128, 128), 1)
    edge = []
    for s in range(2):
        outer = strip_in[2, pl.ds(0, 1), :]
        rest_of = jnp.where(on_left, *((outer, inner) if s == 0 else (inner, outer)))
        strip = strip_in[s, pl.ds(0, 1), :] + rest_of
        strip = jnp.transpose(jnp.broadcast_to(strip, (128, 128)))
        value = col_in[s] + gain_in[s] * strip
        edge.append(jnp.where(level_lane < limits[s], value, 0.0))
    cols_ref[0] = jnp.where(level_lane < 64, edge[0], roll(edge[1], 64, 1))
    cols_ref[1] = jnp.where(level_lane < 64, roll(edge[0], 64, 1), edge[1])

    rest = pl.ds(0, 2 * (chips - 1))
    pltpu.make_async_copy(send.at[rest], send.at[rest], send_sem).wait()
    rest = pl.ds(0, chips - 1)
    pltpu.make_async_copy(meta.at[rest], meta.at[rest], meta_send_sem).wait()
    for q in range(q_count):
        copy_out(q).wait()
    keep_copy.wait()


def couple(src, coupling, dest, block, atm, mask, depth, weights, inverses, ocean, n_lat, n_lon):
    pairs = src.shape[0]
    q_count, o_rows, levels, _ = inverses.shape
    chips = n_lat * n_lon // 2
    vmem, smem, hbm = (
        pl.BlockSpec(memory_space=s) for s in (pltpu.VMEM, pltpu.SMEM, pl.ANY)
    )
    shape = jax.ShapeDtypeStruct
    V, DMA = pltpu.VMEM, pltpu.SemaphoreType.DMA
    return pl.pallas_call(
        functools.partial(couple_kernel, n_lat, n_lon),
        in_specs=[smem, smem] + [vmem] * 5 + [hbm] * 3,
        out_specs=[hbm] * 2 + [vmem] * 4,
        out_shape=[
            shape((q_count, levels, o_rows, 128), f32),
            shape((levels, o_rows, 128), f32),
            shape((128, 128), f32),
            shape((q_count, levels, 128), f32),
            shape((2, q_count, levels, 128), f32),
            shape((2, 128, 128), f32),
        ],
        scratch_shapes=[
            V(weights.shape, bf16),
            V(inverses.shape, f32),
            V(ocean.shape, f32),
            V((levels * (o_rows + 1), 128), f32),
            V((mask.shape[0], 8, 128), f32),
            V((4 * pairs, 128), f32),
            V((2 * chips, 16, 128), f32),
            V((chips, 1, 128), f32),
            V((2 * chips, 16, 128), f32),
            V((chips, 1, 128), f32),
            V((2, 128, 128), f32),
            V((128, 128), f32),
            V((3, 128, 128), f32),
            V((2, 128, 128), f32),
            V((128, 128), f32),
            V((2, 8, 128), f32),
            V((2, 2, 8, 128), f32),
            V((3, 8, 128), f32),
            V((2, q_count, levels, 128), f32),
            V((2, q_count, levels, 128), f32),
            V((2, 128, 128), f32),
            V((2, 128, 128), f32),
            V((2, 8, 128), f32),
            V((4, o_rows, 128), i32),
            V((2, 2, 8, 128), f32),
            V((3, 8, 128), f32),
            V((4, o_rows, 128), i32),
            V((levels, o_rows, 128), f32),
            DMA((15,)),
            DMA((10,)),
            DMA((4, q_count)),
            DMA((8,)),
            DMA((12,)),
            DMA((12,)),
            DMA((8,)),
            DMA((8,)),
        ],
        compiler_params=pltpu.CompilerParams(
            collective_id=0, has_side_effects=True, vmem_limit_bytes=VMEM_BYTES
        ),
        name="couple",
    )(src, coupling, dest, block, atm, mask, depth, weights, inverses, ocean)


def finish_kernel(
    base_ref, keep_ref, force_ref, gains_ref, rows_ref, cols_ref, depth_ref, out_ref,
    slabs, splits, sums, spots, forced,
):
    q = pl.program_id(0)
    levels, o_rows = base_ref.shape[1:3]
    cell = iota((o_rows, 128), 1)
    here = pl.ds(q * o_rows, o_rows)
    group = slabs[0].shape[0]
    groups = levels // group
    rim = (cell == 0) | (cell == 127)
    far = jnp.where(cell == 127, 64, 0)
    own_row = cell % o_rows == iota((o_rows, 128), 0)
    apart = iota((256, 128), 0) % 128 - iota((256, 128), 1)
    beside = one_hot((apart == 1) | (apart == -1))
    high, low = halves(force_ref[here, :])
    forces = jnp.concatenate([high, high, low, jnp.zeros_like(low)], axis=0)

    def tile(j):
        return pl.ds(j * o_rows, o_rows)

    def spot(n, j):
        gain = gains_ref[0, pl.ds(n * group + j, 1), :]
        spots[n % 2][tile(j), :] = jnp.where(own_row, gain, 0.0).astype(bf16)

    def force(n, j):
        slab, split, l = slabs[n % 2], splits[n % 2], n * group + j
        mixed = base_ref[0, l] + forced[n % 2][tile(j), :]
        mixed = jnp.where(l < depth_ref[...], mixed, 0.0)
        slab[j, pl.ds(8, o_rows), :] = mixed
        slab[j, pl.ds(7, 1), :] = rows_ref[0, 0, pl.ds(l, 1), :]
        slab[j, pl.ds(8 + o_rows, 1), :] = rows_ref[1, 0, pl.ds(l, 1), :]
        high, low = halves(mixed)
        split[tile(j), pl.ds(0, 128)] = high
        split[tile(j), pl.ds(128, 128)] = low

    def spread(n, j):
        slab, l = slabs[n % 2], n * group + j
        edge = jnp.take_along_axis(cols_ref[l // 64, here, :], far + l % 64, axis=1)
        near = slab[j, pl.ds(7, o_rows), :] + slab[j, pl.ds(9, o_rows), :]
        near = near + sums[n % 2][tile(j), :]
        near = near + jnp.where(rim, edge, 0.0)
        value = keep_ref[l] * slab[j, pl.ds(8, o_rows), :] + diffusion_rate * near
        out_ref[0, l] = jnp.where(l < depth_ref[...], value, base_ref[0, l])

    for n in range(-2, groups):
        if n >= 0:
            sums[n % 2][...] = dot(splits[n % 2][...], beside)
        if 0 <= n + 1 < groups:
            forced[(n + 1) % 2][...] = dot(spots[(n + 1) % 2][...], forces)
        for j in range(group):
            if n + 2 < groups:
                spot(n + 2, j)
            if n >= 0:
                spread(n, j)
            if 0 <= n + 1 < groups:
                force(n + 1, j)


def finish(base, keep, force, gains, rows, cols, depth):
    q_count, levels, o_rows, _ = base.shape
    group = 16
    full = lambda a: pl.BlockSpec(a.shape, lambda q: (0,) * a.ndim)
    block = pl.BlockSpec((1, levels, o_rows, 128), lambda q: (q, 0, 0, 0))
    V = pltpu.VMEM
    return pl.pallas_call(
        finish_kernel,
        grid=(q_count,),
        in_specs=[
            block,
            full(keep),
            full(force),
            pl.BlockSpec((1, levels, 128), lambda q: (q, 0, 0)),
            pl.BlockSpec((2, 1, levels, 128), lambda q: (0, q, 0, 0)),
            full(cols),
            full(depth),
        ],
        out_specs=block,
        out_shape=jax.ShapeDtypeStruct(base.shape, f32),
        scratch_shapes=[
            [V((group, o_rows + 16, 128), f32)] * 2,
            [V((group * o_rows, 256), bf16)] * 2,
            [V((group * o_rows, 128), f32)] * 2,
            [V((group * o_rows, 128), bf16)] * 2,
            [V((group * o_rows, 128), f32)] * 2,
        ],
        compiler_params=pltpu.CompilerParams(vmem_limit_bytes=VMEM_BYTES),
        name="finish",
    )(base, keep, force, gains, rows, cols, depth)


def on_device(
    atm_flux,
    sea_mask,
    src_block,
    dest_dev,
    dest_block,
    intersection_weights,
    coupling,
    inverses,
    ocean_state,
    depth_levels,
):
    n_lat, n_lon = lax.axis_size("lat"), lax.axis_size("lon")
    pairs = src_block.shape[0]
    q_count, levels, o_rows, cells = ocean_state.shape
    base, keep, force, gains, rows, cols = couple(
        src_block, coupling, dest_dev.reshape(1, pairs), dest_block.reshape(1, pairs),
        atm_flux, sea_mask, depth_levels, intersection_weights,
        inverses.reshape(q_count, o_rows, levels, levels),
        ocean_state, n_lat, n_lon,
    )
    return finish(base, keep, force, gains, rows, cols, depth_levels)


def solution(mesh):
    placed = (
        P(None, "lat", "lon"),
        P("lat", "lon"),
        P(("lat", "lon")),
        P(("lat", "lon"), None),
        P(("lat", "lon")),
        P(("lat", "lon"), None, None),
        P(),
        P(None, "lat", "lon", None, None),
        P(None, None, "lat", "lon"),
        P("lat", "lon"),
    )
    return jax.shard_map(
        on_device,
        mesh=mesh,
        in_specs=placed,
        out_specs=P(None, None, "lat", "lon"),
        check_vma=False,
    )
```

```python
import functools

import jax
import jax.numpy as jnp
from jax import lax
from jax.experimental import pallas as pl
from jax.experimental.pallas import tpu as pltpu
from jax.sharding import PartitionSpec as P

diffusion_rate = 0.2
CAP = 4
MESH = pl.DeviceIdType.MESH
NORTH, SOUTH, WEST, EAST = range(4)
ORDER = (1, 3, 2, 0)
f32, bf16, i32 = jnp.float32, jnp.bfloat16, jnp.int32
VMEM_BYTES = 62 << 20


def halves(x):
    high = x.astype(bf16)
    return high, (x - high.astype(f32)).astype(bf16)


def dot(a, b):
    return jnp.dot(a, b, preferred_element_type=f32)


def iota(shape, dim):
    return lax.broadcasted_iota(i32, shape, dim)


def one_hot(flags):
    return flags.astype(f32).astype(bf16)


def couple_kernel(
    n_lat, n_lon,
    src_ref, coupling_ref, dest_ref, block_ref, atm_ref, mask_ref, depth_ref,
    weights_hbm, inverses_hbm, ocean_hbm,
    base_hbm, keep_hbm, force_ref, gains_ref, rows_ref, cols_ref,
    weights, inverses, ocean, skewed, table, contrib,
    send, meta, recv, recv_meta, partial, partial_in,
    packed, col_out, gain_ref, gain_out, force_out, strip_out, row_out,
    row_in, col_in, gain_in, gain_strip_in, depth_in, force_in, strip_in, sides_ref, keep,
    load_sems, ship_sems, row_sems, depth_sems, halo_send, halo_recv, force_send, force_recv,
):
    chips = n_lat * n_lon // 2
    devices = 2 * chips
    lat, lon = lax.axis_index("lat"), lax.axis_index("lon")
    core = lon % 2
    my_chip = lat * (n_lon // 2) + lon // 2
    q_count = coupling_ref.shape[0]
    pairs = dest_ref.shape[1]
    levels = inverses.shape[2]
    skew = skewed.shape[0] // levels
    o_rows = depth_ref.shape[0]

    w_chunks = 8
    w_size = pairs // w_chunks

    def weight_copy(c):
        part = pl.ds(c * w_size, w_size)
        return pltpu.make_async_copy(weights_hbm.at[part], weights.at[part], load_sems.at[c])

    for c in range(w_chunks):
        weight_copy(c).start()
    inverse_copy = pltpu.make_async_copy(inverses_hbm, inverses, load_sems.at[w_chunks])
    ocean_copy = pltpu.make_async_copy(ocean_hbm, ocean, load_sems.at[w_chunks + 1])
    inverse_copy.start()
    ocean_copy.start()

    barrier = pltpu.get_barrier_semaphore()

    x_here, y_here = lon // 8, lon // 2 % 4

    xs = [lax.rem(x_here + dx, 4) * 8 + core for dx in range(4)]
    ys = [lax.rem(y_here + dy, 4) * 2 for dy in range(4)]

    def plane(dz, each):
        z = lax.rem(lat + dz, n_lat)
        for dy in range(4):
            for dx in range(4):
                if dx or dy or dz:
                    each(z, xs[dx] + ys[dy])

    beside = {
        NORTH: ((lat + n_lat - 1) % n_lat, lon),
        SOUTH: ((lat + 1) % n_lat, lon),
        WEST: (lat, (lon + n_lon - 1) % n_lon),
        EAST: (lat, (lon + 1) % n_lon),
    }
    partner = (lat, lon + 1 - 2 * core)

    def greet(z, o):
        pl.semaphore_signal(barrier, inc=1, device_id=(z, o), device_id_type=MESH)

    for dz in (2, 1, 3, 0):
        plane(dz, greet)
    slant = [(beside[side][0], partner[1]) for side in (NORTH, SOUTH)]
    for other in (beside[WEST], beside[EAST], *slant):
        pl.semaphore_signal(barrier, inc=1, device_id=other, device_id_type=MESH)

    a_rows = mask_ref.shape[0]
    mask = mask_ref[...].astype(f32)
    masked = [atm_ref[f].astype(f32) * mask for f in range(atm_ref.shape[0])]
    for q in range(q_count):
        row = masked[0] * coupling_ref[q, 0]
        for f in range(1, atm_ref.shape[0]):
            row = row + masked[f] * coupling_ref[q, f]
        high, low = halves(row)
        contrib[pl.ds(q, a_rows, stride=8), :] = high.astype(f32)
        contrib[pl.ds(q_count + q, a_rows, stride=8), :] = low.astype(f32)
    table[...] = contrib[pl.ds(0, 8 * a_rows), :].reshape(a_rows, 8, 128)

    dest = dest_ref[...]
    named = (iota((devices, pairs), 0) == dest).astype(f32)
    before = one_hot(iota((pairs, pairs), 0) < iota((pairs, pairs), 1))
    rank = jnp.sum(named * dot(named.astype(bf16), before), axis=0, keepdims=True).astype(i32)
    lane = iota((128, pairs), 0)
    of_chip = one_hot(iota((chips, pairs), 0) == dest // 2)
    held = ((rank == lane % CAP) & (dest % 2 == lane % 32 // 16)).astype(f32)
    held = (held * block_ref[...].astype(f32)).astype(bf16)
    blocks = lax.dot_general(of_chip, held, (((1,), (1,)), ((), ())), preferred_element_type=f32)
    lanes = iota((chips, 128), 1)
    key = blocks + (lanes % 32 // 16 * 128 + lanes % 16 // CAP * o_rows).astype(f32)
    key = jnp.where(lanes // 32 == my_chip % 4, key, 0.0)
    for h in range(chips):
        meta[h] = key[h : h + 1]
    slot = dest * 8 + rank
    keys = jnp.concatenate([slot, slot + CAP], axis=1)

    def chunk_of_pairs(c, carry):
        weight_copy(c).wait()

        def four(i, carry):
            p = c * w_size + i * 4
            lefts = []
            for j in range(4):
                left = table[src_ref[p + j]]
                zero = jnp.zeros_like(left)
                lefts.append(jnp.concatenate([left, zero] if j % 2 == 0 else [zero, left], axis=1))
            left = jnp.concatenate(lefts, axis=0).astype(bf16)
            w = [weights[p + j] for j in range(4)]
            right = jnp.concatenate(
                [jnp.concatenate(w[:2], axis=0), jnp.concatenate(w[2:], axis=0)], axis=1
            )
            out = dot(left, right)
            for j in range(4):
                both = out[j * 8 : j * 8 + 8, j // 2 * 128 : j // 2 * 128 + 128]
                contrib[pl.ds(p + j, q_count, stride=pairs), :] = both[:q_count] + both[q_count:]
            return carry

        return lax.fori_loop(0, w_size // 4, four, carry, unroll=4)

    lax.fori_loop(0, w_chunks, chunk_of_pairs, 0)

    high, low = halves(
        jnp.concatenate(
            [contrib[pl.ds(h * 2 * pairs, 2 * pairs), :] for h in range(2)], axis=1
        )
    )
    chunk = devices * 8 // n_lat
    send_sem, meta_send_sem = ship_sems.at[0], ship_sems.at[1]
    recv_sems = [ship_sems.at[2 + dz] for dz in range(n_lat)]
    meta_recv_sems = [ship_sems.at[2 + n_lat + dz] for dz in range(n_lat)]

    def place(i):
        hot = one_hot(iota((chunk, 2 * pairs), 0) + i * chunk == keys)
        out = dot(hot, high) + dot(hot, low)
        for h in range(2):
            send[pl.ds(i * (chunk // 8), chunk // 8), pl.ds(h * 8, 8), :] = out[
                :, h * 128 : (h + 1) * 128
            ].reshape(chunk // 8, 8, 128)

    depth_copies = [
        pltpu.make_async_remote_copy(
            depth_ref, depth_in.at[(SOUTH, NORTH, EAST, WEST)[side]],
            depth_sems.at[side], depth_sems.at[4 + side],
            device_id=beside[side], device_id_type=MESH,
        )
        for side in range(4)
    ]
    mine = pl.ds(2 * my_chip, 2)
    for n, dz in enumerate(ORDER):
        place(lax.rem(lat + dz, n_lat))
        if n == 0:
            pl.semaphore_wait(barrier, chips + 3)
            for copy in depth_copies:
                copy.start()

        def ship(z, o):
            to = z * (n_lon // 2) + o // 2
            pltpu.make_async_remote_copy(
                send.at[pl.ds(2 * to, 2)], recv.at[mine], send_sem, recv_sems[dz],
                device_id=(z, o), device_id_type=MESH,
            ).start()
            pltpu.make_async_remote_copy(
                meta.at[to], recv_meta.at[my_chip], meta_send_sem, meta_recv_sems[dz],
                device_id=(z, o), device_id_type=MESH,
            ).start()

        plane(dz, ship)
    pltpu.make_async_copy(send.at[mine], recv.at[mine], recv_sems[0]).start()
    pltpu.make_async_copy(meta.at[my_chip], recv_meta.at[my_chip], meta_recv_sems[0]).start()

    inverse_copy.wait()
    ocean_copy.wait()
    packed[...] = jnp.zeros_like(packed)
    level = iota((levels, 128), 0)
    lane_id = iota((levels, 128), 1)
    low_levels = pl.ds(0, levels)

    def copy_out(q):
        return pltpu.make_async_copy(ocean.at[q], base_hbm.at[q], load_sems.at[w_chunks + 2 + q])

    def row_copy(side, q):
        return pltpu.make_async_remote_copy(
            row_out.at[side, q], row_in.at[1 - side, q],
            row_sems.at[side, q], row_sems.at[3 - side, q],
            device_id=beside[side], device_id_type=MESH,
        )

    def field(q, carry):
        def skew_in(l, carry):
            skewed[pl.ds(l * skew, o_rows), :] = ocean[q, l]
            return carry

        lax.fori_loop(0, levels, skew_in, 0, unroll=8)

        def mix(r, carry):
            i = q * o_rows + r
            column = pl.ds(r, levels, stride=skew)
            state = skewed[column, :]
            active = level < depth_ref[pl.ds(r, 1), :]
            inverse = inverses[q, r]
            left = jnp.concatenate(halves(inverse), axis=0)
            right = jnp.concatenate(halves(jnp.where(active, state, 0.0)), axis=1)
            out = dot(left, right)
            solved = out[:levels, :128] + (out[:levels, 128:] + out[levels:, :128])
            mixed = jnp.where(active, solved, state)
            skewed[column, :] = mixed
            turned = pltpu.roll(mixed, i, 1)
            packed[0, low_levels, :] = jnp.where(lane_id == i, turned, packed[0, low_levels, :])
            last = lax.rem(i + 127, 128)
            packed[1, low_levels, :] = jnp.where(lane_id == last, turned, packed[1, low_levels, :])
            gain = jnp.broadcast_to(inverse[:, :1], mixed.shape)
            packed[2, low_levels, :] = jnp.where(lane_id == i, gain, packed[2, low_levels, :])
            return carry

        lax.fori_loop(0, o_rows, mix, 0, unroll=4)

        def skew_out(l, carry):
            ocean[q, l] = skewed[pl.ds(l * skew, o_rows), :]
            return carry

        lax.fori_loop(0, levels, skew_out, 0, unroll=8)
        for s, r in ((0, 0), (1, o_rows - 1)):
            row_out[s, q] = skewed[pl.ds(r, levels, stride=skew), :]
        copy_out(q).start()
        for side in (NORTH, SOUTH):
            row_copy(side, q).start()
        return carry

    lax.fori_loop(0, q_count, field, 0)
    col_out[0] = jnp.transpose(packed[0])
    col_out[1] = jnp.transpose(pltpu.roll(packed[1], 1, 1))
    gain_ref[...] = jnp.transpose(packed[2])
    for s, r in ((0, 0), (1, o_rows - 1)):
        gain_out[s, pl.ds(0, q_count), :] = gain_ref[pl.ds(r, q_count, stride=o_rows), :]

    copies = []

    def hand(side, source, target):
        opposite = (SOUTH, NORTH, EAST, WEST)[side]
        n = len(copies)
        copy = pltpu.make_async_remote_copy(
            source, target(opposite), halo_send.at[n], halo_recv.at[n],
            device_id=beside[side], device_id_type=MESH,
        )
        copy.start()
        copies.append(copy)

    for side in (NORTH, SOUTH):
        hand(side, gain_out.at[side], lambda o: gain_strip_in.at[o])
    for side in (WEST, EAST):
        hand(side, col_out.at[side - 2], lambda o: col_in.at[o - 2])
        hand(side, gain_ref, lambda o: gain_in.at[o - 2])

    for copy in depth_copies:
        copy.wait()
    depth = depth_ref[...]
    in_band = (lat > 0).astype(i32), (lat < n_lat - 1).astype(i32)
    north_depth = depth_in[NORTH] * in_band[0]
    south_depth = depth_in[SOUTH] * in_band[1]
    row_id, cell_id = iota(depth.shape, 0), iota(depth.shape, 1)
    roll = pltpu.roll
    sides_ref[NORTH] = jnp.where(row_id == 0, roll(north_depth, 1, 0), roll(depth, 1, 0))
    sides_ref[SOUTH] = jnp.where(
        row_id == o_rows - 1, roll(south_depth, o_rows - 1, 0), roll(depth, o_rows - 1, 0)
    )
    sides_ref[WEST] = jnp.where(cell_id == 0, roll(depth_in[WEST], 1, 1), roll(depth, 1, 1))
    sides_ref[EAST] = jnp.where(cell_id == 127, roll(depth_in[EAST], 127, 1), roll(depth, 127, 1))

    def weigh(l, carry):
        count = jnp.zeros(depth.shape, f32)
        for s in range(4):
            count = count + jnp.where(l < sides_ref[s], diffusion_rate, 0.0)
        keep[l] = 1.0 - count
        return carry

    lax.fori_loop(0, levels, weigh, 0, unroll=4)
    keep_copy = pltpu.make_async_copy(keep, keep_hbm, load_sems.at[w_chunks + 2 + q_count])
    keep_copy.start()
    for q in range(q_count):
        gain = packed[2, low_levels, :]
        gain = gain if q == 0 else roll(gain, 128 - q * o_rows, 1)
        high, low = (part.astype(f32) for part in halves(gain))
        third = lane_id // o_rows
        gain = jnp.where(third == 0, high, jnp.where(third == 1, roll(low, 32, 1), roll(high, 64, 1)))
        gains_ref[q] = jnp.where(third == 3, 0.0, gain)

    partial[...] = jnp.zeros_like(partial)
    per_plane = chips // n_lat
    for dz in ORDER:
        z = lax.rem(lat + n_lat - dz, n_lat)
        some = pl.ds(z * per_plane, per_plane)
        pltpu.make_async_copy(recv_meta.at[some], recv_meta.at[some], meta_recv_sems[dz]).wait()
        some = pl.ds(z * 2 * per_plane, 2 * per_plane)
        pltpu.make_async_copy(recv.at[some], recv.at[some], recv_sems[dz]).wait()
        out = None
        for i in range(per_plane // 8):
            at = z * per_plane + i * 8
            keys = jnp.concatenate(
                [jnp.sum(recv_meta[pl.ds(at + 4 * h, 4)], axis=0) for h in range(2)], axis=1
            ).astype(i32)
            hot = one_hot(iota((256, 256), 0) == keys)
            both = jnp.concatenate(halves(recv[pl.ds(2 * at, 16)].reshape(256, 128)), axis=1)
            out = dot(hot, both) if out is None else out + dot(hot, both)
        partial[...] += (out[:, :128] + out[:, 128:]).reshape(2, 128, 128)

    own, other = partial[core], partial[1 - core]
    for e, mine_or in enumerate((core, 1 - core)):
        for side, r in ((0, 0), (1, o_rows - 1)):
            force_out[e, side, pl.ds(0, q_count), :] = partial[
                mine_or, pl.ds(r, q_count, stride=o_rows), :
            ]
    turned, turned_other = jnp.transpose(own), jnp.transpose(other)
    on_left = core == 0
    strip_out[0, pl.ds(0, 1), :] = turned[:1]
    strip_out[1, pl.ds(0, 1), :] = turned[127:]
    strip_out[2, pl.ds(0, 1), :] = jnp.where(on_left, turned_other[127:], turned_other[:1])
    inner = jnp.where(on_left, turned_other[:1], turned_other[127:])
    hops = [
        (partial.at[1 - core], partial_in, partner),
        (force_out.at[0, 0], force_in.at[0, 1], beside[NORTH]),
        (force_out.at[0, 1], force_in.at[0, 0], beside[SOUTH]),
        (force_out.at[1, 0], force_in.at[1, 1], slant[0]),
        (force_out.at[1, 1], force_in.at[1, 0], slant[1]),
        (strip_out.at[0], strip_in.at[1], beside[WEST]),
        (strip_out.at[1], strip_in.at[0], beside[EAST]),
        (strip_out.at[2], strip_in.at[2], (lat, lax.rem(lon + n_lon + 2 - 4 * core, n_lon))),
    ]
    forces = []
    for n, (source, target, device) in enumerate(hops):
        copy = pltpu.make_async_remote_copy(
            source, target, force_send.at[n], force_recv.at[n],
            device_id=device, device_id_type=MESH,
        )
        copy.start()
        forces.append(copy)

    for copy in copies:
        copy.wait()
    for q in range(q_count):
        for side in (NORTH, SOUTH):
            row_copy(side, q).wait()
    limits = [
        jnp.concatenate([jnp.broadcast_to(edge, (o_rows, 128))] * q_count, axis=0)
        for edge in (depth_in[WEST][:, 127:], depth_in[EAST][:, :1])
    ]
    strips = jnp.transpose(
        jnp.concatenate(
            [gain_strip_in[0], gain_strip_in[1], jnp.zeros((112, 128), f32)], axis=0
        )
    )
    for copy in forces:
        copy.wait()
    force_ref[...] = own + partial_in[...]
    edges = north_depth[o_rows - 1 :], south_depth[:1]
    for s in range(2):
        for q in range(q_count):
            gain = jnp.broadcast_to(strips[:levels, s * 8 + q : s * 8 + q + 1], (levels, 128))
            force = force_in[0, s, pl.ds(q, 1), :] + force_in[1, s, pl.ds(q, 1), :]
            value = row_in[s, q] + gain * force
            rows_ref[s, q] = jnp.where(level < edges[s], value, 0.0)
    level_lane = iota((128, 128), 1)
    edge = []
    for s in range(2):
        outer = strip_in[2, pl.ds(0, 1), :]
        rest_of = jnp.where(on_left, *((outer, inner) if s == 0 else (inner, outer)))
        strip = strip_in[s, pl.ds(0, 1), :] + rest_of
        strip = jnp.transpose(jnp.broadcast_to(strip, (128, 128)))
        value = col_in[s] + gain_in[s] * strip
        edge.append(jnp.where(level_lane < limits[s], value, 0.0))
    cols_ref[0] = jnp.where(level_lane < 64, edge[0], roll(edge[1], 64, 1))
    cols_ref[1] = jnp.where(level_lane < 64, roll(edge[0], 64, 1), edge[1])

    rest = pl.ds(0, 2 * (chips - 1))
    pltpu.make_async_copy(send.at[rest], send.at[rest], send_sem).wait()
    rest = pl.ds(0, chips - 1)
    pltpu.make_async_copy(meta.at[rest], meta.at[rest], meta_send_sem).wait()
    for q in range(q_count):
        copy_out(q).wait()
    keep_copy.wait()


def couple(src, coupling, dest, block, atm, mask, depth, weights, inverses, ocean, n_lat, n_lon):
    pairs = src.shape[0]
    q_count, o_rows, levels, _ = inverses.shape
    chips = n_lat * n_lon // 2
    vmem, smem, hbm = (
        pl.BlockSpec(memory_space=s) for s in (pltpu.VMEM, pltpu.SMEM, pl.ANY)
    )
    shape = jax.ShapeDtypeStruct
    V, DMA = pltpu.VMEM, pltpu.SemaphoreType.DMA
    return pl.pallas_call(
        functools.partial(couple_kernel, n_lat, n_lon),
        in_specs=[smem, smem] + [vmem] * 5 + [hbm] * 3,
        out_specs=[hbm] * 2 + [vmem] * 4,
        out_shape=[
            shape((q_count, levels, o_rows, 128), f32),
            shape((levels, o_rows, 128), f32),
            shape((128, 128), f32),
            shape((q_count, levels, 128), f32),
            shape((2, q_count, levels, 128), f32),
            shape((2, 128, 128), f32),
        ],
        scratch_shapes=[
            V(weights.shape, bf16),
            V(inverses.shape, f32),
            V(ocean.shape, f32),
            V((levels * (o_rows + 1), 128), f32),
            V((mask.shape[0], 8, 128), f32),
            V((4 * pairs, 128), f32),
            V((2 * chips, 16, 128), f32),
            V((chips, 1, 128), f32),
            V((2 * chips, 16, 128), f32),
            V((chips, 1, 128), f32),
            V((2, 128, 128), f32),
            V((128, 128), f32),
            V((3, 128, 128), f32),
            V((2, 128, 128), f32),
            V((128, 128), f32),
            V((2, 8, 128), f32),
            V((2, 2, 8, 128), f32),
            V((3, 8, 128), f32),
            V((2, q_count, levels, 128), f32),
            V((2, q_count, levels, 128), f32),
            V((2, 128, 128), f32),
            V((2, 128, 128), f32),
            V((2, 8, 128), f32),
            V((4, o_rows, 128), i32),
            V((2, 2, 8, 128), f32),
            V((3, 8, 128), f32),
            V((4, o_rows, 128), i32),
            V((levels, o_rows, 128), f32),
            DMA((15,)),
            DMA((10,)),
            DMA((4, q_count)),
            DMA((8,)),
            DMA((12,)),
            DMA((12,)),
            DMA((8,)),
            DMA((8,)),
        ],
        compiler_params=pltpu.CompilerParams(
            collective_id=0, has_side_effects=True, vmem_limit_bytes=VMEM_BYTES
        ),
        name="couple",
    )(src, coupling, dest, block, atm, mask, depth, weights, inverses, ocean)


def finish_kernel(
    base_ref, keep_ref, force_ref, gains_ref, rows_ref, cols_ref, depth_ref, out_ref,
    slabs, splits, sums, spots, forced,
):
    q = pl.program_id(0)
    levels, o_rows = base_ref.shape[1:3]
    cell = iota((o_rows, 128), 1)
    here = pl.ds(q * o_rows, o_rows)
    group = slabs[0].shape[0]
    groups = levels // group
    rim = (cell == 0) | (cell == 127)
    far = jnp.where(cell == 127, 64, 0)
    own_row = cell % o_rows == iota((o_rows, 128), 0)
    apart = iota((256, 128), 0) % 128 - iota((256, 128), 1)
    beside = one_hot((apart == 1) | (apart == -1))
    high, low = halves(force_ref[here, :])
    forces = jnp.concatenate([high, high, low, jnp.zeros_like(low)], axis=0)

    def tile(j):
        return pl.ds(j * o_rows, o_rows)

    def spot(n, j):
        gain = gains_ref[0, pl.ds(n * group + j, 1), :]
        spots[n % 2][tile(j), :] = jnp.where(own_row, gain, 0.0).astype(bf16)

    def force(n, j):
        slab, split, l = slabs[n % 2], splits[n % 2], n * group + j
        mixed = base_ref[0, l] + forced[n % 2][tile(j), :]
        mixed = jnp.where(l < depth_ref[...], mixed, 0.0)
        slab[j, pl.ds(8, o_rows), :] = mixed
        slab[j, pl.ds(7, 1), :] = rows_ref[0, 0, pl.ds(l, 1), :]
        slab[j, pl.ds(8 + o_rows, 1), :] = rows_ref[1, 0, pl.ds(l, 1), :]
        high, low = halves(mixed)
        split[tile(j), pl.ds(0, 128)] = high
        split[tile(j), pl.ds(128, 128)] = low

    def spread(n, j):
        slab, l = slabs[n % 2], n * group + j
        edge = jnp.take_along_axis(cols_ref[l // 64, here, :], far + l % 64, axis=1)
        near = slab[j, pl.ds(7, o_rows), :] + slab[j, pl.ds(9, o_rows), :]
        near = near + sums[n % 2][tile(j), :]
        near = near + jnp.where(rim, edge, 0.0)
        value = keep_ref[l] * slab[j, pl.ds(8, o_rows), :] + diffusion_rate * near
        out_ref[0, l] = jnp.where(l < depth_ref[...], value, base_ref[0, l])

    for n in range(-2, groups):
        if n >= 0:
            sums[n % 2][...] = dot(splits[n % 2][...], beside)
        if 0 <= n + 1 < groups:
            forced[(n + 1) % 2][...] = dot(spots[(n + 1) % 2][...], forces)
        for j in range(group):
            if n + 2 < groups:
                spot(n + 2, j)
            if n >= 0:
                spread(n, j)
            if 0 <= n + 1 < groups:
                force(n + 1, j)


def finish(base, keep, force, gains, rows, cols, depth):
    q_count, levels, o_rows, _ = base.shape
    group = 16
    full = lambda a: pl.BlockSpec(a.shape, lambda q: (0,) * a.ndim)
    block = pl.BlockSpec((1, levels, o_rows, 128), lambda q: (q, 0, 0, 0))
    V = pltpu.VMEM
    return pl.pallas_call(
        finish_kernel,
        grid=(q_count,),
        in_specs=[
            block,
            full(keep),
            full(force),
            pl.BlockSpec((1, levels, 128), lambda q: (q, 0, 0)),
            pl.BlockSpec((2, 1, levels, 128), lambda q: (0, q, 0, 0)),
            full(cols),
            full(depth),
        ],
        out_specs=block,
        out_shape=jax.ShapeDtypeStruct(base.shape, f32),
        scratch_shapes=[
            [V((group, o_rows + 16, 128), f32)] * 2,
            [V((group * o_rows, 256), bf16)] * 2,
            [V((group * o_rows, 128), f32)] * 2,
            [V((group * o_rows, 128), bf16)] * 2,
            [V((group * o_rows, 128), f32)] * 2,
        ],
        compiler_params=pltpu.CompilerParams(vmem_limit_bytes=VMEM_BYTES),
        name="finish",
    )(base, keep, force, gains, rows, cols, depth)


def on_device(
    atm_flux,
    sea_mask,
    src_block,
    dest_dev,
    dest_block,
    intersection_weights,
    coupling,
    inverses,
    ocean_state,
    depth_levels,
):
    n_lat, n_lon = lax.axis_size("lat"), lax.axis_size("lon")
    pairs = src_block.shape[0]
    q_count, levels, o_rows, cells = ocean_state.shape
    base, keep, force, gains, rows, cols = couple(
        src_block, coupling, dest_dev.reshape(1, pairs), dest_block.reshape(1, pairs),
        atm_flux, sea_mask, depth_levels, intersection_weights,
        inverses.reshape(q_count, o_rows, levels, levels),
        ocean_state, n_lat, n_lon,
    )
    return finish(base, keep, force, gains, rows, cols, depth_levels)


def solution(mesh):
    placed = (
        P(None, "lat", "lon"),
        P("lat", "lon"),
        P(("lat", "lon")),
        P(("lat", "lon"), None),
        P(("lat", "lon")),
        P(("lat", "lon"), None, None),
        P(),
        P(None, "lat", "lon", None, None),
        P(None, None, "lat", "lon"),
        P("lat", "lon"),
    )
    return jax.shard_map(
        on_device,
        mesh=mesh,
        in_specs=placed,
        out_specs=P(None, None, "lat", "lon"),
        check_vma=False,
    )
```

```python
import functools

import jax
import jax.numpy as jnp
from jax import lax
from jax.experimental import pallas as pl
from jax.experimental.pallas import tpu as pltpu
from jax.sharding import PartitionSpec as P

diffusion_rate = 0.2
CAP = 4
MESH = pl.DeviceIdType.MESH
NORTH, SOUTH, WEST, EAST = range(4)
ORDER = (1, 3, 2, 0)
f32, bf16, i32 = jnp.float32, jnp.bfloat16, jnp.int32
VMEM_BYTES = 62 << 20


def halves(x):
    high = x.astype(bf16)
    return high, (x - high.astype(f32)).astype(bf16)


def dot(a, b):
    return jnp.dot(a, b, preferred_element_type=f32)


def iota(shape, dim):
    return lax.broadcasted_iota(i32, shape, dim)


def one_hot(flags):
    return flags.astype(f32).astype(bf16)


def couple_kernel(
    n_lat, n_lon,
    src_ref, coupling_ref, dest_ref, block_ref, atm_ref, mask_ref, depth_ref,
    weights_hbm, inverses_hbm, ocean_hbm,
    base_hbm, keep_hbm, force_ref, gains_ref, rows_ref, cols_ref,
    weights, inverses, ocean, skewed, table, contrib,
    send, meta, recv, recv_meta, partial, partial_in,
    packed, col_out, gain_ref, gain_out, force_out, strip_out, row_out,
    row_in, col_in, gain_in, gain_strip_in, depth_in, force_in, strip_in, sides_ref, keep,
    load_sems, ship_sems, row_sems, depth_sems, halo_send, halo_recv, force_send, force_recv,
):
    chips = n_lat * n_lon // 2
    devices = 2 * chips
    lat, lon = lax.axis_index("lat"), lax.axis_index("lon")
    core = lon % 2
    my_chip = lat * (n_lon // 2) + lon // 2
    q_count = coupling_ref.shape[0]
    pairs = dest_ref.shape[1]
    levels = inverses.shape[2]
    skew = skewed.shape[0] // levels
    o_rows = depth_ref.shape[0]

    w_chunks = 8
    w_size = pairs // w_chunks

    def weight_copy(c):
        part = pl.ds(c * w_size, w_size)
        return pltpu.make_async_copy(weights_hbm.at[part], weights.at[part], load_sems.at[c])

    for c in range(w_chunks):
        weight_copy(c).start()
    inverse_copy = pltpu.make_async_copy(inverses_hbm, inverses, load_sems.at[w_chunks])
    ocean_copy = pltpu.make_async_copy(ocean_hbm, ocean, load_sems.at[w_chunks + 1])

    barrier = pltpu.get_barrier_semaphore()

    x_here, y_here = lon // 8, lon // 2 % 4

    xs = [lax.rem(x_here + dx, 4) * 8 + core for dx in range(4)]
    ys = [lax.rem(y_here + dy, 4) * 2 for dy in range(4)]

    def plane(dz, each):
        z = lax.rem(lat + dz, n_lat)
        for dy in range(4):
            for dx in range(4):
                if dx or dy or dz:
                    each(z, xs[dx] + ys[dy])

    beside = {
        NORTH: ((lat + n_lat - 1) % n_lat, lon),
        SOUTH: ((lat + 1) % n_lat, lon),
        WEST: (lat, (lon + n_lon - 1) % n_lon),
        EAST: (lat, (lon + 1) % n_lon),
    }
    partner = (lat, lon + 1 - 2 * core)

    def greet(z, o):
        pl.semaphore_signal(barrier, inc=1, device_id=(z, o), device_id_type=MESH)

    for dz in (2, 1, 3, 0):
        plane(dz, greet)
    slant = [(beside[side][0], partner[1]) for side in (NORTH, SOUTH)]
    for other in (beside[WEST], beside[EAST], *slant):
        pl.semaphore_signal(barrier, inc=1, device_id=other, device_id_type=MESH)

    a_rows = mask_ref.shape[0]
    mask = mask_ref[...].astype(f32)
    masked = [atm_ref[f].astype(f32) * mask for f in range(atm_ref.shape[0])]
    for q in range(q_count):
        row = masked[0] * coupling_ref[q, 0]
        for f in range(1, atm_ref.shape[0]):
            row = row + masked[f] * coupling_ref[q, f]
        high, low = halves(row)
        contrib[pl.ds(q, a_rows, stride=8), :] = high.astype(f32)
        contrib[pl.ds(q_count + q, a_rows, stride=8), :] = low.astype(f32)
    table[...] = contrib[pl.ds(0, 8 * a_rows), :].reshape(a_rows, 8, 128)

    dest = dest_ref[...]
    named = (iota((devices, pairs), 0) == dest).astype(f32)
    before = one_hot(iota((pairs, pairs), 0) < iota((pairs, pairs), 1))
    rank = jnp.sum(named * dot(named.astype(bf16), before), axis=0, keepdims=True).astype(i32)
    lane = iota((128, pairs), 0)
    of_chip = one_hot(iota((chips, pairs), 0) == dest // 2)
    held = ((rank == lane % CAP) & (dest % 2 == lane % 32 // 16)).astype(f32)
    held = (held * block_ref[...].astype(f32)).astype(bf16)
    blocks = lax.dot_general(of_chip, held, (((1,), (1,)), ((), ())), preferred_element_type=f32)
    lanes = iota((chips, 128), 1)
    key = blocks + (lanes % 32 // 16 * 128 + lanes % 16 // CAP * o_rows).astype(f32)
    key = jnp.where(lanes // 32 == my_chip % 4, key, 0.0)
    for h in range(chips):
        meta[h] = key[h : h + 1]
    slot = dest * 8 + rank
    keys = jnp.concatenate([slot, slot + CAP], axis=1)

    def chunk_of_pairs(c, carry):
        weight_copy(c).wait()

        def four(i, carry):
            p = c * w_size + i * 4
            lefts = []
            for j in range(4):
                left = table[src_ref[p + j]]
                zero = jnp.zeros_like(left)
                lefts.append(jnp.concatenate([left, zero] if j % 2 == 0 else [zero, left], axis=1))
            left = jnp.concatenate(lefts, axis=0).astype(bf16)
            w = [weights[p + j] for j in range(4)]
            right = jnp.concatenate(
                [jnp.concatenate(w[:2], axis=0), jnp.concatenate(w[2:], axis=0)], axis=1
            )
            out = dot(left, right)
            for j in range(4):
                both = out[j * 8 : j * 8 + 8, j // 2 * 128 : j // 2 * 128 + 128]
                contrib[pl.ds(p + j, q_count, stride=pairs), :] = both[:q_count] + both[q_count:]
            return carry

        return lax.fori_loop(0, w_size // 4, four, carry, unroll=4)

    early = w_chunks - 2
    lax.fori_loop(0, early, chunk_of_pairs, 0)
    inverse_copy.start()
    ocean_copy.start()
    lax.fori_loop(early, w_chunks, chunk_of_pairs, 0)

    high, low = halves(
        jnp.concatenate(
            [contrib[pl.ds(h * 2 * pairs, 2 * pairs), :] for h in range(2)], axis=1
        )
    )
    chunk = devices * 8 // n_lat
    send_sem, meta_send_sem = ship_sems.at[0], ship_sems.at[1]
    recv_sems = [ship_sems.at[2 + dz] for dz in range(n_lat)]
    meta_recv_sems = [ship_sems.at[2 + n_lat + dz] for dz in range(n_lat)]

    def place(i):
        hot = one_hot(iota((chunk, 2 * pairs), 0) + i * chunk == keys)
        out = dot(hot, high) + dot(hot, low)
        for h in range(2):
            send[pl.ds(i * (chunk // 8), chunk // 8), pl.ds(h * 8, 8), :] = out[
                :, h * 128 : (h + 1) * 128
            ].reshape(chunk // 8, 8, 128)

    depth_copies = [
        pltpu.make_async_remote_copy(
            depth_ref, depth_in.at[(SOUTH, NORTH, EAST, WEST)[side]],
            depth_sems.at[side], depth_sems.at[4 + side],
            device_id=beside[side], device_id_type=MESH,
        )
        for side in range(4)
    ]
    mine = pl.ds(2 * my_chip, 2)
    for n, dz in enumerate(ORDER):
        place(lax.rem(lat + dz, n_lat))
        if n == 0:
            pl.semaphore_wait(barrier, chips + 3)
            for copy in depth_copies:
                copy.start()

        def ship(z, o):
            to = z * (n_lon // 2) + o // 2
            pltpu.make_async_remote_copy(
                send.at[pl.ds(2 * to, 2)], recv.at[mine], send_sem, recv_sems[dz],
                device_id=(z, o), device_id_type=MESH,
            ).start()
            pltpu.make_async_remote_copy(
                meta.at[to], recv_meta.at[my_chip], meta_send_sem, meta_recv_sems[dz],
                device_id=(z, o), device_id_type=MESH,
            ).start()

        plane(dz, ship)
    pltpu.make_async_copy(send.at[mine], recv.at[mine], recv_sems[0]).start()
    pltpu.make_async_copy(meta.at[my_chip], recv_meta.at[my_chip], meta_recv_sems[0]).start()

    inverse_copy.wait()
    ocean_copy.wait()
    packed[...] = jnp.zeros_like(packed)
    level = iota((levels, 128), 0)
    lane_id = iota((levels, 128), 1)
    low_levels = pl.ds(0, levels)

    def copy_out(q):
        return pltpu.make_async_copy(ocean.at[q], base_hbm.at[q], load_sems.at[w_chunks + 2 + q])

    def row_copy(side, q):
        return pltpu.make_async_remote_copy(
            row_out.at[side, q], row_in.at[1 - side, q],
            row_sems.at[side, q], row_sems.at[3 - side, q],
            device_id=beside[side], device_id_type=MESH,
        )

    def field(q, carry):
        def skew_in(l, carry):
            skewed[pl.ds(l * skew, o_rows), :] = ocean[q, l]
            return carry

        lax.fori_loop(0, levels, skew_in, 0, unroll=8)

        def mix(r, carry):
            i = q * o_rows + r
            column = pl.ds(r, levels, stride=skew)
            state = skewed[column, :]
            active = level < depth_ref[pl.ds(r, 1), :]
            inverse = inverses[q, r]
            left = jnp.concatenate(halves(inverse), axis=0)
            right = jnp.concatenate(halves(jnp.where(active, state, 0.0)), axis=1)
            out = dot(left, right)
            solved = out[:levels, :128] + (out[:levels, 128:] + out[levels:, :128])
            mixed = jnp.where(active, solved, state)
            skewed[column, :] = mixed
            turned = pltpu.roll(mixed, i, 1)
            packed[0, low_levels, :] = jnp.where(lane_id == i, turned, packed[0, low_levels, :])
            last = lax.rem(i + 127, 128)
            packed[1, low_levels, :] = jnp.where(lane_id == last, turned, packed[1, low_levels, :])
            gain = jnp.broadcast_to(inverse[:, :1], mixed.shape)
            packed[2, low_levels, :] = jnp.where(lane_id == i, gain, packed[2, low_levels, :])
            return carry

        lax.fori_loop(0, o_rows, mix, 0, unroll=4)

        def skew_out(l, carry):
            ocean[q, l] = skewed[pl.ds(l * skew, o_rows), :]
            return carry

        lax.fori_loop(0, levels, skew_out, 0, unroll=8)
        for s, r in ((0, 0), (1, o_rows - 1)):
            row_out[s, q] = skewed[pl.ds(r, levels, stride=skew), :]
        copy_out(q).start()
        for side in (NORTH, SOUTH):
            row_copy(side, q).start()
        return carry

    lax.fori_loop(0, q_count, field, 0)
    col_out[0] = jnp.transpose(packed[0])
    col_out[1] = jnp.transpose(pltpu.roll(packed[1], 1, 1))
    gain_ref[...] = jnp.transpose(packed[2])
    for s, r in ((0, 0), (1, o_rows - 1)):
        gain_out[s, pl.ds(0, q_count), :] = gain_ref[pl.ds(r, q_count, stride=o_rows), :]

    copies = []

    def hand(side, source, target):
        opposite = (SOUTH, NORTH, EAST, WEST)[side]
        n = len(copies)
        copy = pltpu.make_async_remote_copy(
            source, target(opposite), halo_send.at[n], halo_recv.at[n],
            device_id=beside[side], device_id_type=MESH,
        )
        copy.start()
        copies.append(copy)

    for side in (NORTH, SOUTH):
        hand(side, gain_out.at[side], lambda o: gain_strip_in.at[o])
    for side in (WEST, EAST):
        hand(side, col_out.at[side - 2], lambda o: col_in.at[o - 2])
        hand(side, gain_ref, lambda o: gain_in.at[o - 2])

    for copy in depth_copies:
        copy.wait()
    depth = depth_ref[...]
    in_band = (lat > 0).astype(i32), (lat < n_lat - 1).astype(i32)
    north_depth = depth_in[NORTH] * in_band[0]
    south_depth = depth_in[SOUTH] * in_band[1]
    row_id, cell_id = iota(depth.shape, 0), iota(depth.shape, 1)
    roll = pltpu.roll
    sides_ref[NORTH] = jnp.where(row_id == 0, roll(north_depth, 1, 0), roll(depth, 1, 0))
    sides_ref[SOUTH] = jnp.where(
        row_id == o_rows - 1, roll(south_depth, o_rows - 1, 0), roll(depth, o_rows - 1, 0)
    )
    sides_ref[WEST] = jnp.where(cell_id == 0, roll(depth_in[WEST], 1, 1), roll(depth, 1, 1))
    sides_ref[EAST] = jnp.where(cell_id == 127, roll(depth_in[EAST], 127, 1), roll(depth, 127, 1))

    def weigh(l, carry):
        count = jnp.zeros(depth.shape, f32)
        for s in range(4):
            count = count + jnp.where(l < sides_ref[s], diffusion_rate, 0.0)
        keep[l] = 1.0 - count
        return carry

    lax.fori_loop(0, levels, weigh, 0, unroll=4)
    keep_copy = pltpu.make_async_copy(keep, keep_hbm, load_sems.at[w_chunks + 2 + q_count])
    keep_copy.start()
    for q in range(q_count):
        gain = packed[2, low_levels, :]
        gain = gain if q == 0 else roll(gain, 128 - q * o_rows, 1)
        high, low = (part.astype(f32) for part in halves(gain))
        third = lane_id // o_rows
        gain = jnp.where(third == 0, high, jnp.where(third == 1, roll(low, 32, 1), roll(high, 64, 1)))
        gains_ref[q] = jnp.where(third == 3, 0.0, gain)

    partial[...] = jnp.zeros_like(partial)
    per_plane = chips // n_lat
    for dz in ORDER:
        z = lax.rem(lat + n_lat - dz, n_lat)
        some = pl.ds(z * per_plane, per_plane)
        pltpu.make_async_copy(recv_meta.at[some], recv_meta.at[some], meta_recv_sems[dz]).wait()
        some = pl.ds(z * 2 * per_plane, 2 * per_plane)
        pltpu.make_async_copy(recv.at[some], recv.at[some], recv_sems[dz]).wait()
        out = None
        for i in range(per_plane // 8):
            at = z * per_plane + i * 8
            keys = jnp.concatenate(
                [jnp.sum(recv_meta[pl.ds(at + 4 * h, 4)], axis=0) for h in range(2)], axis=1
            ).astype(i32)
            hot = one_hot(iota((256, 256), 0) == keys)
            both = jnp.concatenate(halves(recv[pl.ds(2 * at, 16)].reshape(256, 128)), axis=1)
            out = dot(hot, both) if out is None else out + dot(hot, both)
        partial[...] += (out[:, :128] + out[:, 128:]).reshape(2, 128, 128)

    own, other = partial[core], partial[1 - core]
    for e, mine_or in enumerate((core, 1 - core)):
        for side, r in ((0, 0), (1, o_rows - 1)):
            force_out[e, side, pl.ds(0, q_count), :] = partial[
                mine_or, pl.ds(r, q_count, stride=o_rows), :
            ]
    turned, turned_other = jnp.transpose(own), jnp.transpose(other)
    on_left = core == 0
    strip_out[0, pl.ds(0, 1), :] = turned[:1]
    strip_out[1, pl.ds(0, 1), :] = turned[127:]
    strip_out[2, pl.ds(0, 1), :] = jnp.where(on_left, turned_other[127:], turned_other[:1])
    inner = jnp.where(on_left, turned_other[:1], turned_other[127:])
    hops = [
        (partial.at[1 - core], partial_in, partner),
        (force_out.at[0, 0], force_in.at[0, 1], beside[NORTH]),
        (force_out.at[0, 1], force_in.at[0, 0], beside[SOUTH]),
        (force_out.at[1, 0], force_in.at[1, 1], slant[0]),
        (force_out.at[1, 1], force_in.at[1, 0], slant[1]),
        (strip_out.at[0], strip_in.at[1], beside[WEST]),
        (strip_out.at[1], strip_in.at[0], beside[EAST]),
        (strip_out.at[2], strip_in.at[2], (lat, lax.rem(lon + n_lon + 2 - 4 * core, n_lon))),
    ]
    forces = []
    for n, (source, target, device) in enumerate(hops):
        copy = pltpu.make_async_remote_copy(
            source, target, force_send.at[n], force_recv.at[n],
            device_id=device, device_id_type=MESH,
        )
        copy.start()
        forces.append(copy)

    for copy in copies:
        copy.wait()
    for q in range(q_count):
        for side in (NORTH, SOUTH):
            row_copy(side, q).wait()
    limits = [
        jnp.concatenate([jnp.broadcast_to(edge, (o_rows, 128))] * q_count, axis=0)
        for edge in (depth_in[WEST][:, 127:], depth_in[EAST][:, :1])
    ]
    strips = jnp.transpose(
        jnp.concatenate(
            [gain_strip_in[0], gain_strip_in[1], jnp.zeros((112, 128), f32)], axis=0
        )
    )
    for copy in forces:
        copy.wait()
    force_ref[...] = own + partial_in[...]
    edges = north_depth[o_rows - 1 :], south_depth[:1]
    for s in range(2):
        for q in range(q_count):
            gain = jnp.broadcast_to(strips[:levels, s * 8 + q : s * 8 + q + 1], (levels, 128))
            force = force_in[0, s, pl.ds(q, 1), :] + force_in[1, s, pl.ds(q, 1), :]
            value = row_in[s, q] + gain * force
            rows_ref[s, q] = jnp.where(level < edges[s], value, 0.0)
    level_lane = iota((128, 128), 1)
    edge = []
    for s in range(2):
        outer = strip_in[2, pl.ds(0, 1), :]
        rest_of = jnp.where(on_left, *((outer, inner) if s == 0 else (inner, outer)))
        strip = strip_in[s, pl.ds(0, 1), :] + rest_of
        strip = jnp.transpose(jnp.broadcast_to(strip, (128, 128)))
        value = col_in[s] + gain_in[s] * strip
        edge.append(jnp.where(level_lane < limits[s], value, 0.0))
    cols_ref[0] = jnp.where(level_lane < 64, edge[0], roll(edge[1], 64, 1))
    cols_ref[1] = jnp.where(level_lane < 64, roll(edge[0], 64, 1), edge[1])

    rest = pl.ds(0, 2 * (chips - 1))
    pltpu.make_async_copy(send.at[rest], send.at[rest], send_sem).wait()
    rest = pl.ds(0, chips - 1)
    pltpu.make_async_copy(meta.at[rest], meta.at[rest], meta_send_sem).wait()
    for q in range(q_count):
        copy_out(q).wait()
    keep_copy.wait()


def couple(src, coupling, dest, block, atm, mask, depth, weights, inverses, ocean, n_lat, n_lon):
    pairs = src.shape[0]
    q_count, o_rows, levels, _ = inverses.shape
    chips = n_lat * n_lon // 2
    vmem, smem, hbm = (
        pl.BlockSpec(memory_space=s) for s in (pltpu.VMEM, pltpu.SMEM, pl.ANY)
    )
    shape = jax.ShapeDtypeStruct
    V, DMA = pltpu.VMEM, pltpu.SemaphoreType.DMA
    return pl.pallas_call(
        functools.partial(couple_kernel, n_lat, n_lon),
        in_specs=[smem, smem] + [vmem] * 5 + [hbm] * 3,
        out_specs=[hbm] * 2 + [vmem] * 4,
        out_shape=[
            shape((q_count, levels, o_rows, 128), f32),
            shape((levels, o_rows, 128), f32),
            shape((128, 128), f32),
            shape((q_count, levels, 128), f32),
            shape((2, q_count, levels, 128), f32),
            shape((2, 128, 128), f32),
        ],
        scratch_shapes=[
            V(weights.shape, bf16),
            V(inverses.shape, f32),
            V(ocean.shape, f32),
            V((levels * (o_rows + 1), 128), f32),
            V((mask.shape[0], 8, 128), f32),
            V((4 * pairs, 128), f32),
            V((2 * chips, 16, 128), f32),
            V((chips, 1, 128), f32),
            V((2 * chips, 16, 128), f32),
            V((chips, 1, 128), f32),
            V((2, 128, 128), f32),
            V((128, 128), f32),
            V((3, 128, 128), f32),
            V((2, 128, 128), f32),
            V((128, 128), f32),
            V((2, 8, 128), f32),
            V((2, 2, 8, 128), f32),
            V((3, 8, 128), f32),
            V((2, q_count, levels, 128), f32),
            V((2, q_count, levels, 128), f32),
            V((2, 128, 128), f32),
            V((2, 128, 128), f32),
            V((2, 8, 128), f32),
            V((4, o_rows, 128), i32),
            V((2, 2, 8, 128), f32),
            V((3, 8, 128), f32),
            V((4, o_rows, 128), i32),
            V((levels, o_rows, 128), f32),
            DMA((15,)),
            DMA((10,)),
            DMA((4, q_count)),
            DMA((8,)),
            DMA((12,)),
            DMA((12,)),
            DMA((8,)),
            DMA((8,)),
        ],
        compiler_params=pltpu.CompilerParams(
            collective_id=0, has_side_effects=True, vmem_limit_bytes=VMEM_BYTES
        ),
        name="couple",
    )(src, coupling, dest, block, atm, mask, depth, weights, inverses, ocean)


def finish_kernel(
    base_ref, keep_ref, force_ref, gains_ref, rows_ref, cols_ref, depth_ref, out_ref,
    slabs, splits, sums, spots, forced,
):
    q = pl.program_id(0)
    levels, o_rows = base_ref.shape[1:3]
    cell = iota((o_rows, 128), 1)
    here = pl.ds(q * o_rows, o_rows)
    group = slabs[0].shape[0]
    groups = levels // group
    rim = (cell == 0) | (cell == 127)
    far = jnp.where(cell == 127, 64, 0)
    own_row = cell % o_rows == iota((o_rows, 128), 0)
    apart = iota((256, 128), 0) % 128 - iota((256, 128), 1)
    beside = one_hot((apart == 1) | (apart == -1))
    high, low = halves(force_ref[here, :])
    forces = jnp.concatenate([high, high, low, jnp.zeros_like(low)], axis=0)

    def tile(j):
        return pl.ds(j * o_rows, o_rows)

    def spot(n, j):
        gain = gains_ref[0, pl.ds(n * group + j, 1), :]
        spots[n % 2][tile(j), :] = jnp.where(own_row, gain, 0.0).astype(bf16)

    def force(n, j):
        slab, split, l = slabs[n % 2], splits[n % 2], n * group + j
        mixed = base_ref[0, l] + forced[n % 2][tile(j), :]
        mixed = jnp.where(l < depth_ref[...], mixed, 0.0)
        slab[j, pl.ds(8, o_rows), :] = mixed
        slab[j, pl.ds(7, 1), :] = rows_ref[0, 0, pl.ds(l, 1), :]
        slab[j, pl.ds(8 + o_rows, 1), :] = rows_ref[1, 0, pl.ds(l, 1), :]
        high, low = halves(mixed)
        split[tile(j), pl.ds(0, 128)] = high
        split[tile(j), pl.ds(128, 128)] = low

    def spread(n, j):
        slab, l = slabs[n % 2], n * group + j
        edge = jnp.take_along_axis(cols_ref[l // 64, here, :], far + l % 64, axis=1)
        near = slab[j, pl.ds(7, o_rows), :] + slab[j, pl.ds(9, o_rows), :]
        near = near + sums[n % 2][tile(j), :]
        near = near + jnp.where(rim, edge, 0.0)
        value = keep_ref[l] * slab[j, pl.ds(8, o_rows), :] + diffusion_rate * near
        out_ref[0, l] = jnp.where(l < depth_ref[...], value, base_ref[0, l])

    for n in range(-2, groups):
        if n >= 0:
            sums[n % 2][...] = dot(splits[n % 2][...], beside)
        if 0 <= n + 1 < groups:
            forced[(n + 1) % 2][...] = dot(spots[(n + 1) % 2][...], forces)
        for j in range(group):
            if n + 2 < groups:
                spot(n + 2, j)
            if n >= 0:
                spread(n, j)
            if 0 <= n + 1 < groups:
                force(n + 1, j)


def finish(base, keep, force, gains, rows, cols, depth):
    q_count, levels, o_rows, _ = base.shape
    group = 20
    full = lambda a: pl.BlockSpec(a.shape, lambda q: (0,) * a.ndim)
    block = pl.BlockSpec((1, levels, o_rows, 128), lambda q: (q, 0, 0, 0))
    V = pltpu.VMEM
    return pl.pallas_call(
        finish_kernel,
        grid=(q_count,),
        in_specs=[
            block,
            full(keep),
            full(force),
            pl.BlockSpec((1, levels, 128), lambda q: (q, 0, 0)),
            pl.BlockSpec((2, 1, levels, 128), lambda q: (0, q, 0, 0)),
            full(cols),
            full(depth),
        ],
        out_specs=block,
        out_shape=jax.ShapeDtypeStruct(base.shape, f32),
        scratch_shapes=[
            [V((group, o_rows + 16, 128), f32)] * 2,
            [V((group * o_rows, 256), bf16)] * 2,
            [V((group * o_rows, 128), f32)] * 2,
            [V((group * o_rows, 128), bf16)] * 2,
            [V((group * o_rows, 128), f32)] * 2,
        ],
        compiler_params=pltpu.CompilerParams(vmem_limit_bytes=VMEM_BYTES),
        name="finish",
    )(base, keep, force, gains, rows, cols, depth)


def on_device(
    atm_flux,
    sea_mask,
    src_block,
    dest_dev,
    dest_block,
    intersection_weights,
    coupling,
    inverses,
    ocean_state,
    depth_levels,
):
    n_lat, n_lon = lax.axis_size("lat"), lax.axis_size("lon")
    pairs = src_block.shape[0]
    q_count, levels, o_rows, cells = ocean_state.shape
    base, keep, force, gains, rows, cols = couple(
        src_block, coupling, dest_dev.reshape(1, pairs), dest_block.reshape(1, pairs),
        atm_flux, sea_mask, depth_levels, intersection_weights,
        inverses.reshape(q_count, o_rows, levels, levels),
        ocean_state, n_lat, n_lon,
    )
    return finish(base, keep, force, gains, rows, cols, depth_levels)


def solution(mesh):
    placed = (
        P(None, "lat", "lon"),
        P("lat", "lon"),
        P(("lat", "lon")),
        P(("lat", "lon"), None),
        P(("lat", "lon")),
        P(("lat", "lon"), None, None),
        P(),
        P(None, "lat", "lon", None, None),
        P(None, None, "lat", "lon"),
        P("lat", "lon"),
    )
    return jax.shard_map(
        on_device,
        mesh=mesh,
        in_specs=placed,
        out_specs=P(None, None, "lat", "lon"),
        check_vma=False,
    )
```

```python
import functools

import jax
import jax.numpy as jnp
from jax import lax
from jax.experimental import pallas as pl
from jax.experimental.pallas import tpu as pltpu
from jax.sharding import PartitionSpec as P

diffusion_rate = 0.2
CAP = 4
MESH = pl.DeviceIdType.MESH
NORTH, SOUTH, WEST, EAST = range(4)
ORDER = (1, 3, 2, 0)
f32, bf16, i32 = jnp.float32, jnp.bfloat16, jnp.int32
VMEM_BYTES = 62 << 20


def halves(x):
    high = x.astype(bf16)
    return high, (x - high.astype(f32)).astype(bf16)


def dot(a, b):
    return jnp.dot(a, b, preferred_element_type=f32)


def iota(shape, dim):
    return lax.broadcasted_iota(i32, shape, dim)


def one_hot(flags):
    return flags.astype(f32).astype(bf16)


def couple_kernel(
    n_lat, n_lon,
    src_ref, coupling_ref, dest_ref, block_ref, atm_ref, mask_ref, depth_ref,
    weights_hbm, inverses_hbm, ocean_hbm,
    base_hbm, keep_hbm, force_ref, gains_ref, rows_ref, cols_ref,
    weights, inverses, ocean, skewed, table, contrib,
    send, meta, recv, recv_meta, partial, partial_in,
    packed, col_out, gain_ref, gain_out, force_out, strip_out, row_out,
    row_in, col_in, gain_in, gain_strip_in, depth_in, force_in, strip_in, sides_ref, keep,
    load_sems, ship_sems, row_sems, depth_sems, halo_send, halo_recv, force_send, force_recv,
):
    chips = n_lat * n_lon // 2
    devices = 2 * chips
    lat, lon = lax.axis_index("lat"), lax.axis_index("lon")
    core = lon % 2
    my_chip = lat * (n_lon // 2) + lon // 2
    q_count = coupling_ref.shape[0]
    pairs = dest_ref.shape[1]
    levels = inverses.shape[2]
    skew = skewed.shape[0] // levels
    o_rows = depth_ref.shape[0]

    barrier = pltpu.get_barrier_semaphore()

    x_here, y_here = lon // 8, lon // 2 % 4

    xs = [lax.rem(x_here + dx, 4) * 8 + core for dx in range(4)]
    ys = [lax.rem(y_here + dy, 4) * 2 for dy in range(4)]

    def plane(dz, each):
        z = lax.rem(lat + dz, n_lat)
        for dy in range(4):
            for dx in range(4):
                if dx or dy or dz:
                    each(z, xs[dx] + ys[dy])

    beside = {
        NORTH: ((lat + n_lat - 1) % n_lat, lon),
        SOUTH: ((lat + 1) % n_lat, lon),
        WEST: (lat, (lon + n_lon - 1) % n_lon),
        EAST: (lat, (lon + 1) % n_lon),
    }
    partner = (lat, lon + 1 - 2 * core)

    def greet(z, o):
        pl.semaphore_signal(barrier, inc=1, device_id=(z, o), device_id_type=MESH)

    for dz in (2, 1, 3, 0):
        plane(dz, greet)
    slant = [(beside[side][0], partner[1]) for side in (NORTH, SOUTH)]
    for other in (beside[WEST], beside[EAST], *slant):
        pl.semaphore_signal(barrier, inc=1, device_id=other, device_id_type=MESH)

    w_chunks = 8
    w_size = pairs // w_chunks

    def weight_copy(c):
        part = pl.ds(c * w_size, w_size)
        return pltpu.make_async_copy(weights_hbm.at[part], weights.at[part], load_sems.at[c])

    for c in range(w_chunks):
        weight_copy(c).start()
    inverse_copy = pltpu.make_async_copy(inverses_hbm, inverses, load_sems.at[w_chunks])
    ocean_copy = pltpu.make_async_copy(ocean_hbm, ocean, load_sems.at[w_chunks + 1])

    a_rows = mask_ref.shape[0]
    mask = mask_ref[...].astype(f32)
    masked = [atm_ref[f].astype(f32) * mask for f in range(atm_ref.shape[0])]
    for q in range(q_count):
        row = masked[0] * coupling_ref[q, 0]
        for f in range(1, atm_ref.shape[0]):
            row = row + masked[f] * coupling_ref[q, f]
        high, low = halves(row)
        contrib[pl.ds(q, a_rows, stride=8), :] = high.astype(f32)
        contrib[pl.ds(q_count + q, a_rows, stride=8), :] = low.astype(f32)
    table[...] = contrib[pl.ds(0, 8 * a_rows), :].reshape(a_rows, 8, 128)

    dest = dest_ref[...]
    named = (iota((devices, pairs), 0) == dest).astype(f32)
    before = one_hot(iota((pairs, pairs), 0) < iota((pairs, pairs), 1))
    rank = jnp.sum(named * dot(named.astype(bf16), before), axis=0, keepdims=True).astype(i32)
    lane = iota((128, pairs), 0)
    of_chip = one_hot(iota((chips, pairs), 0) == dest // 2)
    held = ((rank == lane % CAP) & (dest % 2 == lane % 32 // 16)).astype(f32)
    held = (held * block_ref[...].astype(f32)).astype(bf16)
    blocks = lax.dot_general(of_chip, held, (((1,), (1,)), ((), ())), preferred_element_type=f32)
    lanes = iota((chips, 128), 1)
    key = blocks + (lanes % 32 // 16 * 128 + lanes % 16 // CAP * o_rows).astype(f32)
    key = jnp.where(lanes // 32 == my_chip % 4, key, 0.0)
    for h in range(chips):
        meta[h] = key[h : h + 1]
    slot = dest * 8 + rank
    keys = jnp.concatenate([slot, slot + CAP], axis=1)

    def chunk_of_pairs(c, carry):
        weight_copy(c).wait()

        def four(i, carry):
            p = c * w_size + i * 4
            lefts = []
            for j in range(4):
                left = table[src_ref[p + j]]
                zero = jnp.zeros_like(left)
                lefts.append(jnp.concatenate([left, zero] if j % 2 == 0 else [zero, left], axis=1))
            left = jnp.concatenate(lefts, axis=0).astype(bf16)
            w = [weights[p + j] for j in range(4)]
            right = jnp.concatenate(
                [jnp.concatenate(w[:2], axis=0), jnp.concatenate(w[2:], axis=0)], axis=1
            )
            out = dot(left, right)
            for j in range(4):
                both = out[j * 8 : j * 8 + 8, j // 2 * 128 : j // 2 * 128 + 128]
                contrib[pl.ds(p + j, q_count, stride=pairs), :] = both[:q_count] + both[q_count:]
            return carry

        return lax.fori_loop(0, w_size // 4, four, carry, unroll=4)

    early = w_chunks - 2
    lax.fori_loop(0, early, chunk_of_pairs, 0)
    inverse_copy.start()
    ocean_copy.start()
    lax.fori_loop(early, w_chunks, chunk_of_pairs, 0)

    high, low = halves(
        jnp.concatenate(
            [contrib[pl.ds(h * 2 * pairs, 2 * pairs), :] for h in range(2)], axis=1
        )
    )
    chunk = devices * 8 // n_lat
    send_sem, meta_send_sem = ship_sems.at[0], ship_sems.at[1]
    recv_sems = [ship_sems.at[2 + dz] for dz in range(n_lat)]
    meta_recv_sems = [ship_sems.at[2 + n_lat + dz] for dz in range(n_lat)]

    def place(i):
        hot = one_hot(iota((chunk, 2 * pairs), 0) + i * chunk == keys)
        out = dot(hot, high) + dot(hot, low)
        for h in range(2):
            send[pl.ds(i * (chunk // 8), chunk // 8), pl.ds(h * 8, 8), :] = out[
                :, h * 128 : (h + 1) * 128
            ].reshape(chunk // 8, 8, 128)

    depth_copies = [
        pltpu.make_async_remote_copy(
            depth_ref, depth_in.at[(SOUTH, NORTH, EAST, WEST)[side]],
            depth_sems.at[side], depth_sems.at[4 + side],
            device_id=beside[side], device_id_type=MESH,
        )
        for side in range(4)
    ]
    mine = pl.ds(2 * my_chip, 2)
    for n, dz in enumerate(ORDER):
        place(lax.rem(lat + dz, n_lat))
        if n == 0:
            pl.semaphore_wait(barrier, chips + 3)
            for copy in depth_copies:
                copy.start()

        def ship(z, o):
            to = z * (n_lon // 2) + o // 2
            pltpu.make_async_remote_copy(
                send.at[pl.ds(2 * to, 2)], recv.at[mine], send_sem, recv_sems[dz],
                device_id=(z, o), device_id_type=MESH,
            ).start()
            pltpu.make_async_remote_copy(
                meta.at[to], recv_meta.at[my_chip], meta_send_sem, meta_recv_sems[dz],
                device_id=(z, o), device_id_type=MESH,
            ).start()

        plane(dz, ship)
    pltpu.make_async_copy(send.at[mine], recv.at[mine], recv_sems[0]).start()
    pltpu.make_async_copy(meta.at[my_chip], recv_meta.at[my_chip], meta_recv_sems[0]).start()

    inverse_copy.wait()
    ocean_copy.wait()
    packed[...] = jnp.zeros_like(packed)
    level = iota((levels, 128), 0)
    lane_id = iota((levels, 128), 1)
    low_levels = pl.ds(0, levels)

    def copy_out(q):
        return pltpu.make_async_copy(ocean.at[q], base_hbm.at[q], load_sems.at[w_chunks + 2 + q])

    def row_copy(side, q):
        return pltpu.make_async_remote_copy(
            row_out.at[side, q], row_in.at[1 - side, q],
            row_sems.at[side, q], row_sems.at[3 - side, q],
            device_id=beside[side], device_id_type=MESH,
        )

    def field(q, carry):
        def skew_in(l, carry):
            skewed[pl.ds(l * skew, o_rows), :] = ocean[q, l]
            return carry

        lax.fori_loop(0, levels, skew_in, 0, unroll=8)

        def mix(r, carry):
            i = q * o_rows + r
            column = pl.ds(r, levels, stride=skew)
            state = skewed[column, :]
            active = level < depth_ref[pl.ds(r, 1), :]
            inverse = inverses[q, r]
            left = jnp.concatenate(halves(inverse), axis=0)
            right = jnp.concatenate(halves(jnp.where(active, state, 0.0)), axis=1)
            out = dot(left, right)
            solved = out[:levels, :128] + (out[:levels, 128:] + out[levels:, :128])
            mixed = jnp.where(active, solved, state)
            skewed[column, :] = mixed
            turned = pltpu.roll(mixed, i, 1)
            packed[0, low_levels, :] = jnp.where(lane_id == i, turned, packed[0, low_levels, :])
            last = lax.rem(i + 127, 128)
            packed[1, low_levels, :] = jnp.where(lane_id == last, turned, packed[1, low_levels, :])
            gain = jnp.broadcast_to(inverse[:, :1], mixed.shape)
            packed[2, low_levels, :] = jnp.where(lane_id == i, gain, packed[2, low_levels, :])
            return carry

        lax.fori_loop(0, o_rows, mix, 0, unroll=4)

        def skew_out(l, carry):
            ocean[q, l] = skewed[pl.ds(l * skew, o_rows), :]
            return carry

        lax.fori_loop(0, levels, skew_out, 0, unroll=8)
        for s, r in ((0, 0), (1, o_rows - 1)):
            row_out[s, q] = skewed[pl.ds(r, levels, stride=skew), :]
        copy_out(q).start()
        for side in (NORTH, SOUTH):
            row_copy(side, q).start()
        return carry

    lax.fori_loop(0, q_count, field, 0)
    col_out[0] = jnp.transpose(packed[0])
    col_out[1] = jnp.transpose(pltpu.roll(packed[1], 1, 1))
    gain_ref[...] = jnp.transpose(packed[2])
    for s, r in ((0, 0), (1, o_rows - 1)):
        gain_out[s, pl.ds(0, q_count), :] = gain_ref[pl.ds(r, q_count, stride=o_rows), :]

    copies = []

    def hand(side, source, target):
        opposite = (SOUTH, NORTH, EAST, WEST)[side]
        n = len(copies)
        copy = pltpu.make_async_remote_copy(
            source, target(opposite), halo_send.at[n], halo_recv.at[n],
            device_id=beside[side], device_id_type=MESH,
        )
        copy.start()
        copies.append(copy)

    for side in (NORTH, SOUTH):
        hand(side, gain_out.at[side], lambda o: gain_strip_in.at[o])
    for side in (WEST, EAST):
        hand(side, col_out.at[side - 2], lambda o: col_in.at[o - 2])
        hand(side, gain_ref, lambda o: gain_in.at[o - 2])

    for copy in depth_copies:
        copy.wait()
    depth = depth_ref[...]
    in_band = (lat > 0).astype(i32), (lat < n_lat - 1).astype(i32)
    north_depth = depth_in[NORTH] * in_band[0]
    south_depth = depth_in[SOUTH] * in_band[1]
    row_id, cell_id = iota(depth.shape, 0), iota(depth.shape, 1)
    roll = pltpu.roll
    sides_ref[NORTH] = jnp.where(row_id == 0, roll(north_depth, 1, 0), roll(depth, 1, 0))
    sides_ref[SOUTH] = jnp.where(
        row_id == o_rows - 1, roll(south_depth, o_rows - 1, 0), roll(depth, o_rows - 1, 0)
    )
    sides_ref[WEST] = jnp.where(cell_id == 0, roll(depth_in[WEST], 1, 1), roll(depth, 1, 1))
    sides_ref[EAST] = jnp.where(cell_id == 127, roll(depth_in[EAST], 127, 1), roll(depth, 127, 1))

    def weigh(l, carry):
        count = jnp.zeros(depth.shape, f32)
        for s in range(4):
            count = count + jnp.where(l < sides_ref[s], diffusion_rate, 0.0)
        keep[l] = 1.0 - count
        return carry

    lax.fori_loop(0, levels, weigh, 0, unroll=4)
    keep_copy = pltpu.make_async_copy(keep, keep_hbm, load_sems.at[w_chunks + 2 + q_count])
    keep_copy.start()
    for q in range(q_count):
        gain = packed[2, low_levels, :]
        gain = gain if q == 0 else roll(gain, 128 - q * o_rows, 1)
        high, low = (part.astype(f32) for part in halves(gain))
        third = lane_id // o_rows
        gain = jnp.where(third == 0, high, jnp.where(third == 1, roll(low, 32, 1), roll(high, 64, 1)))
        gains_ref[q] = jnp.where(third == 3, 0.0, gain)

    partial[...] = jnp.zeros_like(partial)
    per_plane = chips // n_lat
    for dz in ORDER:
        z = lax.rem(lat + n_lat - dz, n_lat)
        some = pl.ds(z * per_plane, per_plane)
        pltpu.make_async_copy(recv_meta.at[some], recv_meta.at[some], meta_recv_sems[dz]).wait()
        some = pl.ds(z * 2 * per_plane, 2 * per_plane)
        pltpu.make_async_copy(recv.at[some], recv.at[some], recv_sems[dz]).wait()
        out = None
        for i in range(per_plane // 8):
            at = z * per_plane + i * 8
            keys = jnp.concatenate(
                [jnp.sum(recv_meta[pl.ds(at + 4 * h, 4)], axis=0) for h in range(2)], axis=1
            ).astype(i32)
            hot = one_hot(iota((256, 256), 0) == keys)
            both = jnp.concatenate(halves(recv[pl.ds(2 * at, 16)].reshape(256, 128)), axis=1)
            out = dot(hot, both) if out is None else out + dot(hot, both)
        partial[...] += (out[:, :128] + out[:, 128:]).reshape(2, 128, 128)

    own, other = partial[core], partial[1 - core]
    for e, mine_or in enumerate((core, 1 - core)):
        for side, r in ((0, 0), (1, o_rows - 1)):
            force_out[e, side, pl.ds(0, q_count), :] = partial[
                mine_or, pl.ds(r, q_count, stride=o_rows), :
            ]
    turned, turned_other = jnp.transpose(own), jnp.transpose(other)
    on_left = core == 0
    strip_out[0, pl.ds(0, 1), :] = turned[:1]
    strip_out[1, pl.ds(0, 1), :] = turned[127:]
    strip_out[2, pl.ds(0, 1), :] = jnp.where(on_left, turned_other[127:], turned_other[:1])
    inner = jnp.where(on_left, turned_other[:1], turned_other[127:])
    hops = [
        (partial.at[1 - core], partial_in, partner),
        (force_out.at[0, 0], force_in.at[0, 1], beside[NORTH]),
        (force_out.at[0, 1], force_in.at[0, 0], beside[SOUTH]),
        (force_out.at[1, 0], force_in.at[1, 1], slant[0]),
        (force_out.at[1, 1], force_in.at[1, 0], slant[1]),
        (strip_out.at[0], strip_in.at[1], beside[WEST]),
        (strip_out.at[1], strip_in.at[0], beside[EAST]),
        (strip_out.at[2], strip_in.at[2], (lat, lax.rem(lon + n_lon + 2 - 4 * core, n_lon))),
    ]
    forces = []
    for n, (source, target, device) in enumerate(hops):
        copy = pltpu.make_async_remote_copy(
            source, target, force_send.at[n], force_recv.at[n],
            device_id=device, device_id_type=MESH,
        )
        copy.start()
        forces.append(copy)

    for copy in copies:
        copy.wait()
    for q in range(q_count):
        for side in (NORTH, SOUTH):
            row_copy(side, q).wait()
    limits = [
        jnp.concatenate([jnp.broadcast_to(edge, (o_rows, 128))] * q_count, axis=0)
        for edge in (depth_in[WEST][:, 127:], depth_in[EAST][:, :1])
    ]
    strips = jnp.transpose(
        jnp.concatenate(
            [gain_strip_in[0], gain_strip_in[1], jnp.zeros((112, 128), f32)], axis=0
        )
    )
    for copy in forces:
        copy.wait()
    force_ref[...] = own + partial_in[...]
    edges = north_depth[o_rows - 1 :], south_depth[:1]
    for s in range(2):
        for q in range(q_count):
            gain = jnp.broadcast_to(strips[:levels, s * 8 + q : s * 8 + q + 1], (levels, 128))
            force = force_in[0, s, pl.ds(q, 1), :] + force_in[1, s, pl.ds(q, 1), :]
            value = row_in[s, q] + gain * force
            rows_ref[s, q] = jnp.where(level < edges[s], value, 0.0)
    level_lane = iota((128, 128), 1)
    edge = []
    for s in range(2):
        outer = strip_in[2, pl.ds(0, 1), :]
        rest_of = jnp.where(on_left, *((outer, inner) if s == 0 else (inner, outer)))
        strip = strip_in[s, pl.ds(0, 1), :] + rest_of
        strip = jnp.transpose(jnp.broadcast_to(strip, (128, 128)))
        value = col_in[s] + gain_in[s] * strip
        edge.append(jnp.where(level_lane < limits[s], value, 0.0))
    cols_ref[0] = jnp.where(level_lane < 64, edge[0], roll(edge[1], 64, 1))
    cols_ref[1] = jnp.where(level_lane < 64, roll(edge[0], 64, 1), edge[1])

    rest = pl.ds(0, 2 * (chips - 1))
    pltpu.make_async_copy(send.at[rest], send.at[rest], send_sem).wait()
    rest = pl.ds(0, chips - 1)
    pltpu.make_async_copy(meta.at[rest], meta.at[rest], meta_send_sem).wait()
    for q in range(q_count):
        copy_out(q).wait()
    keep_copy.wait()


def couple(src, coupling, dest, block, atm, mask, depth, weights, inverses, ocean, n_lat, n_lon):
    pairs = src.shape[0]
    q_count, o_rows, levels, _ = inverses.shape
    chips = n_lat * n_lon // 2
    vmem, smem, hbm = (
        pl.BlockSpec(memory_space=s) for s in (pltpu.VMEM, pltpu.SMEM, pl.ANY)
    )
    shape = jax.ShapeDtypeStruct
    V, DMA = pltpu.VMEM, pltpu.SemaphoreType.DMA
    return pl.pallas_call(
        functools.partial(couple_kernel, n_lat, n_lon),
        in_specs=[smem, smem] + [vmem] * 5 + [hbm] * 3,
        out_specs=[hbm] * 2 + [vmem] * 4,
        out_shape=[
            shape((q_count, levels, o_rows, 128), f32),
            shape((levels, o_rows, 128), f32),
            shape((128, 128), f32),
            shape((q_count, levels, 128), f32),
            shape((2, q_count, levels, 128), f32),
            shape((2, 128, 128), f32),
        ],
        scratch_shapes=[
            V(weights.shape, bf16),
            V(inverses.shape, f32),
            V(ocean.shape, f32),
            V((levels * (o_rows + 1), 128), f32),
            V((mask.shape[0], 8, 128), f32),
            V((4 * pairs, 128), f32),
            V((2 * chips, 16, 128), f32),
            V((chips, 1, 128), f32),
            V((2 * chips, 16, 128), f32),
            V((chips, 1, 128), f32),
            V((2, 128, 128), f32),
            V((128, 128), f32),
            V((3, 128, 128), f32),
            V((2, 128, 128), f32),
            V((128, 128), f32),
            V((2, 8, 128), f32),
            V((2, 2, 8, 128), f32),
            V((3, 8, 128), f32),
            V((2, q_count, levels, 128), f32),
            V((2, q_count, levels, 128), f32),
            V((2, 128, 128), f32),
            V((2, 128, 128), f32),
            V((2, 8, 128), f32),
            V((4, o_rows, 128), i32),
            V((2, 2, 8, 128), f32),
            V((3, 8, 128), f32),
            V((4, o_rows, 128), i32),
            V((levels, o_rows, 128), f32),
            DMA((15,)),
            DMA((10,)),
            DMA((4, q_count)),
            DMA((8,)),
            DMA((12,)),
            DMA((12,)),
            DMA((8,)),
            DMA((8,)),
        ],
        compiler_params=pltpu.CompilerParams(
            collective_id=0, has_side_effects=True, vmem_limit_bytes=VMEM_BYTES
        ),
        name="couple",
    )(src, coupling, dest, block, atm, mask, depth, weights, inverses, ocean)


def finish_kernel(
    base_ref, keep_ref, force_ref, gains_ref, rows_ref, cols_ref, depth_ref, out_ref,
    slabs, splits, sums, spots, forced,
):
    q = pl.program_id(0)
    levels, o_rows = base_ref.shape[1:3]
    cell = iota((o_rows, 128), 1)
    here = pl.ds(q * o_rows, o_rows)
    group = slabs[0].shape[0]
    groups = levels // group
    rim = (cell == 0) | (cell == 127)
    far = jnp.where(cell == 127, 64, 0)
    own_row = cell % o_rows == iota((o_rows, 128), 0)
    apart = iota((256, 128), 0) % 128 - iota((256, 128), 1)
    beside = one_hot((apart == 1) | (apart == -1))
    high, low = halves(force_ref[here, :])
    forces = jnp.concatenate([high, high, low, jnp.zeros_like(low)], axis=0)

    def tile(j):
        return pl.ds(j * o_rows, o_rows)

    def spot(n, j):
        gain = gains_ref[0, pl.ds(n * group + j, 1), :]
        spots[n % 2][tile(j), :] = jnp.where(own_row, gain, 0.0).astype(bf16)

    def force(n, j):
        slab, split, l = slabs[n % 2], splits[n % 2], n * group + j
        mixed = base_ref[0, l] + forced[n % 2][tile(j), :]
        mixed = jnp.where(l < depth_ref[...], mixed, 0.0)
        slab[j, pl.ds(8, o_rows), :] = mixed
        slab[j, pl.ds(7, 1), :] = rows_ref[0, 0, pl.ds(l, 1), :]
        slab[j, pl.ds(8 + o_rows, 1), :] = rows_ref[1, 0, pl.ds(l, 1), :]
        high, low = halves(mixed)
        split[tile(j), pl.ds(0, 128)] = high
        split[tile(j), pl.ds(128, 128)] = low

    def spread(n, j):
        slab, l = slabs[n % 2], n * group + j
        edge = jnp.take_along_axis(cols_ref[l // 64, here, :], far + l % 64, axis=1)
        near = slab[j, pl.ds(7, o_rows), :] + slab[j, pl.ds(9, o_rows), :]
        near = near + sums[n % 2][tile(j), :]
        near = near + jnp.where(rim, edge, 0.0)
        value = keep_ref[l] * slab[j, pl.ds(8, o_rows), :] + diffusion_rate * near
        out_ref[0, l] = jnp.where(l < depth_ref[...], value, base_ref[0, l])

    for n in range(-2, groups):
        if n >= 0:
            sums[n % 2][...] = dot(splits[n % 2][...], beside)
        if 0 <= n + 1 < groups:
            forced[(n + 1) % 2][...] = dot(spots[(n + 1) % 2][...], forces)
        for j in range(group):
            if n + 2 < groups:
                spot(n + 2, j)
            if n >= 0:
                spread(n, j)
            if 0 <= n + 1 < groups:
                force(n + 1, j)


def finish(base, keep, force, gains, rows, cols, depth):
    q_count, levels, o_rows, _ = base.shape
    group = 20
    full = lambda a: pl.BlockSpec(a.shape, lambda q: (0,) * a.ndim)
    block = pl.BlockSpec((1, levels, o_rows, 128), lambda q: (q, 0, 0, 0))
    V = pltpu.VMEM
    return pl.pallas_call(
        finish_kernel,
        grid=(q_count,),
        in_specs=[
            block,
            full(keep),
            full(force),
            pl.BlockSpec((1, levels, 128), lambda q: (q, 0, 0)),
            pl.BlockSpec((2, 1, levels, 128), lambda q: (0, q, 0, 0)),
            full(cols),
            full(depth),
        ],
        out_specs=block,
        out_shape=jax.ShapeDtypeStruct(base.shape, f32),
        scratch_shapes=[
            [V((group, o_rows + 16, 128), f32)] * 2,
            [V((group * o_rows, 256), bf16)] * 2,
            [V((group * o_rows, 128), f32)] * 2,
            [V((group * o_rows, 128), bf16)] * 2,
            [V((group * o_rows, 128), f32)] * 2,
        ],
        compiler_params=pltpu.CompilerParams(vmem_limit_bytes=VMEM_BYTES),
        name="finish",
    )(base, keep, force, gains, rows, cols, depth)


def on_device(
    atm_flux,
    sea_mask,
    src_block,
    dest_dev,
    dest_block,
    intersection_weights,
    coupling,
    inverses,
    ocean_state,
    depth_levels,
):
    n_lat, n_lon = lax.axis_size("lat"), lax.axis_size("lon")
    pairs = src_block.shape[0]
    q_count, levels, o_rows, cells = ocean_state.shape
    base, keep, force, gains, rows, cols = couple(
        src_block, coupling, dest_dev.reshape(1, pairs), dest_block.reshape(1, pairs),
        atm_flux, sea_mask, depth_levels, intersection_weights,
        inverses.reshape(q_count, o_rows, levels, levels),
        ocean_state, n_lat, n_lon,
    )
    return finish(base, keep, force, gains, rows, cols, depth_levels)


def solution(mesh):
    placed = (
        P(None, "lat", "lon"),
        P("lat", "lon"),
        P(("lat", "lon")),
        P(("lat", "lon"), None),
        P(("lat", "lon")),
        P(("lat", "lon"), None, None),
        P(),
        P(None, "lat", "lon", None, None),
        P(None, None, "lat", "lon"),
        P("lat", "lon"),
    )
    return jax.shard_map(
        on_device,
        mesh=mesh,
        in_specs=placed,
        out_specs=P(None, None, "lat", "lon"),
        check_vma=False,
    )
```

```python
import functools

import jax
import jax.numpy as jnp
from jax import lax
from jax.experimental import pallas as pl
from jax.experimental.pallas import tpu as pltpu
from jax.sharding import PartitionSpec as P

diffusion_rate = 0.2
CAP = 4
MESH = pl.DeviceIdType.MESH
NORTH, SOUTH, WEST, EAST = range(4)
ORDER = (1, 3, 2, 0)
f32, bf16, i32 = jnp.float32, jnp.bfloat16, jnp.int32
VMEM_BYTES = 62 << 20


def halves(x):
    high = x.astype(bf16)
    return high, (x - high.astype(f32)).astype(bf16)


def dot(a, b):
    return jnp.dot(a, b, preferred_element_type=f32)


def iota(shape, dim):
    return lax.broadcasted_iota(i32, shape, dim)


def one_hot(flags):
    return flags.astype(f32).astype(bf16)


def couple_kernel(
    n_lat, n_lon,
    src_ref, coupling_ref, dest_ref, block_ref, atm_ref, mask_ref, depth_ref,
    weights_hbm, inverses_hbm, ocean_hbm,
    base_hbm, keep_hbm, force_ref, gains_ref, rows_ref, cols_ref,
    weights, inverses, ocean, skewed, table, contrib,
    send, meta, recv, recv_meta, partial, partial_in,
    packed, col_out, gain_ref, gain_out, force_out, strip_out, row_out,
    row_in, col_in, gain_in, gain_strip_in, depth_in, force_in, strip_in, sides_ref, keep,
    load_sems, ship_sems, row_sems, depth_sems, halo_send, halo_recv, force_send, force_recv,
):
    chips = n_lat * n_lon // 2
    devices = 2 * chips
    lat, lon = lax.axis_index("lat"), lax.axis_index("lon")
    core = lon % 2
    my_chip = lat * (n_lon // 2) + lon // 2
    q_count = coupling_ref.shape[0]
    pairs = dest_ref.shape[1]
    levels = inverses.shape[2]
    skew = skewed.shape[0] // levels
    o_rows = depth_ref.shape[0]

    w_chunks = 8
    w_size = pairs // w_chunks

    def weight_copy(c):
        part = pl.ds(c * w_size, w_size)
        return pltpu.make_async_copy(weights_hbm.at[part], weights.at[part], load_sems.at[c])

    for c in range(w_chunks):
        weight_copy(c).start()
    inverse_copy = pltpu.make_async_copy(inverses_hbm, inverses, load_sems.at[w_chunks])
    ocean_copy = pltpu.make_async_copy(ocean_hbm, ocean, load_sems.at[w_chunks + 1])

    barrier = pltpu.get_barrier_semaphore()

    x_here, y_here = lon // 8, lon // 2 % 4

    xs = [lax.rem(x_here + dx, 4) * 8 + core for dx in range(4)]
    ys = [lax.rem(y_here + dy, 4) * 2 for dy in range(4)]

    def plane(dz, each):
        z = lax.rem(lat + dz, n_lat)
        for dy in range(4):
            for dx in range(4):
                if dx or dy or dz:
                    each(z, xs[dx] + ys[dy])

    beside = {
        NORTH: ((lat + n_lat - 1) % n_lat, lon),
        SOUTH: ((lat + 1) % n_lat, lon),
        WEST: (lat, (lon + n_lon - 1) % n_lon),
        EAST: (lat, (lon + 1) % n_lon),
    }
    partner = (lat, lon + 1 - 2 * core)

    def greet(z, o):
        pl.semaphore_signal(barrier, inc=1, device_id=(z, o), device_id_type=MESH)

    for dz in (2, 1, 3, 0):
        plane(dz, greet)
    slant = [(beside[side][0], partner[1]) for side in (NORTH, SOUTH)]
    for other in (beside[WEST], beside[EAST], *slant):
        pl.semaphore_signal(barrier, inc=1, device_id=other, device_id_type=MESH)

    a_rows = mask_ref.shape[0]
    mask = mask_ref[...].astype(f32)
    masked = [atm_ref[f].astype(f32) * mask for f in range(atm_ref.shape[0])]
    for q in range(q_count):
        row = masked[0] * coupling_ref[q, 0]
        for f in range(1, atm_ref.shape[0]):
            row = row + masked[f] * coupling_ref[q, f]
        high, low = halves(row)
        contrib[pl.ds(q, a_rows, stride=8), :] = high.astype(f32)
        contrib[pl.ds(q_count + q, a_rows, stride=8), :] = low.astype(f32)
    table[...] = contrib[pl.ds(0, 8 * a_rows), :].reshape(a_rows, 8, 128)

    dest = dest_ref[...]
    named = (iota((devices, pairs), 0) == dest).astype(f32)
    before = one_hot(iota((pairs, pairs), 0) < iota((pairs, pairs), 1))
    rank = jnp.sum(named * dot(named.astype(bf16), before), axis=0, keepdims=True).astype(i32)
    lane = iota((128, pairs), 0)
    of_chip = one_hot(iota((chips, pairs), 0) == dest // 2)
    held = ((rank == lane % CAP) & (dest % 2 == lane % 32 // 16)).astype(f32)
    held = (held * block_ref[...].astype(f32)).astype(bf16)
    blocks = lax.dot_general(of_chip, held, (((1,), (1,)), ((), ())), preferred_element_type=f32)
    lanes = iota((chips, 128), 1)
    key = blocks + (lanes % 32 // 16 * 128 + lanes % 16 // CAP * o_rows).astype(f32)
    key = jnp.where(lanes // 32 == my_chip % 4, key, 0.0)
    for h in range(chips):
        meta[h] = key[h : h + 1]
    slot = dest * 8 + rank
    keys = jnp.concatenate([slot, slot + CAP], axis=1)

    def chunk_of_pairs(c, carry):
        weight_copy(c).wait()

        def four(i, carry):
            p = c * w_size + i * 4
            lefts = []
            for j in range(4):
                left = table[src_ref[p + j]]
                zero = jnp.zeros_like(left)
                lefts.append(jnp.concatenate([left, zero] if j % 2 == 0 else [zero, left], axis=1))
            left = jnp.concatenate(lefts, axis=0).astype(bf16)
            w = [weights[p + j] for j in range(4)]
            right = jnp.concatenate(
                [jnp.concatenate(w[:2], axis=0), jnp.concatenate(w[2:], axis=0)], axis=1
            )
            out = dot(left, right)
            for j in range(4):
                both = out[j * 8 : j * 8 + 8, j // 2 * 128 : j // 2 * 128 + 128]
                contrib[pl.ds(p + j, q_count, stride=pairs), :] = both[:q_count] + both[q_count:]
            return carry

        return lax.fori_loop(0, w_size // 4, four, carry, unroll=4)

    early = w_chunks - 2
    lax.fori_loop(0, early, chunk_of_pairs, 0)
    inverse_copy.start()
    ocean_copy.start()
    lax.fori_loop(early, w_chunks, chunk_of_pairs, 0)

    high, low = halves(
        jnp.concatenate(
            [contrib[pl.ds(h * 2 * pairs, 2 * pairs), :] for h in range(2)], axis=1
        )
    )
    chunk = devices * 8 // n_lat
    send_sem, meta_send_sem = ship_sems.at[0], ship_sems.at[1]
    recv_sems = [ship_sems.at[2 + dz] for dz in range(n_lat)]
    meta_recv_sems = [ship_sems.at[2 + n_lat + dz] for dz in range(n_lat)]

    def place(i):
        hot = one_hot(iota((chunk, 2 * pairs), 0) + i * chunk == keys)
        out = dot(hot, high) + dot(hot, low)
        for h in range(2):
            send[pl.ds(i * (chunk // 8), chunk // 8), pl.ds(h * 8, 8), :] = out[
                :, h * 128 : (h + 1) * 128
            ].reshape(chunk // 8, 8, 128)

    depth_copies = [
        pltpu.make_async_remote_copy(
            depth_ref, depth_in.at[(SOUTH, NORTH, EAST, WEST)[side]],
            depth_sems.at[side], depth_sems.at[4 + side],
            device_id=beside[side], device_id_type=MESH,
        )
        for side in range(4)
    ]
    mine = pl.ds(2 * my_chip, 2)
    for n, dz in enumerate(ORDER):
        place(lax.rem(lat + dz, n_lat))
        if n == 0:
            pl.semaphore_wait(barrier, chips + 3)
            for copy in depth_copies:
                copy.start()

        def ship(z, o):
            to = z * (n_lon // 2) + o // 2
            pltpu.make_async_remote_copy(
                send.at[pl.ds(2 * to, 2)], recv.at[mine], send_sem, recv_sems[dz],
                device_id=(z, o), device_id_type=MESH,
            ).start()
            pltpu.make_async_remote_copy(
                meta.at[to], recv_meta.at[my_chip], meta_send_sem, meta_recv_sems[dz],
                device_id=(z, o), device_id_type=MESH,
            ).start()

        plane(dz, ship)
    pltpu.make_async_copy(send.at[mine], recv.at[mine], recv_sems[0]).start()
    pltpu.make_async_copy(meta.at[my_chip], recv_meta.at[my_chip], meta_recv_sems[0]).start()

    inverse_copy.wait()
    ocean_copy.wait()
    packed[...] = jnp.zeros_like(packed)
    level = iota((levels, 128), 0)
    lane_id = iota((levels, 128), 1)
    low_levels = pl.ds(0, levels)

    def copy_out(q):
        return pltpu.make_async_copy(ocean.at[q], base_hbm.at[q], load_sems.at[w_chunks + 2 + q])

    def row_copy(side, q):
        return pltpu.make_async_remote_copy(
            row_out.at[side, q], row_in.at[1 - side, q],
            row_sems.at[side, q], row_sems.at[3 - side, q],
            device_id=beside[side], device_id_type=MESH,
        )

    def field(q, carry):
        def skew_in(l, carry):
            skewed[pl.ds(l * skew, o_rows), :] = ocean[q, l]
            return carry

        lax.fori_loop(0, levels, skew_in, 0, unroll=8)

        def mix(r, carry):
            i = q * o_rows + r
            column = pl.ds(r, levels, stride=skew)
            state = skewed[column, :]
            active = level < depth_ref[pl.ds(r, 1), :]
            inverse = inverses[q, r]
            left = jnp.concatenate(halves(inverse), axis=0)
            right = jnp.concatenate(halves(jnp.where(active, state, 0.0)), axis=1)
            out = dot(left, right)
            solved = out[:levels, :128] + (out[:levels, 128:] + out[levels:, :128])
            mixed = jnp.where(active, solved, state)
            skewed[column, :] = mixed
            turned = pltpu.roll(mixed, i, 1)
            packed[0, low_levels, :] = jnp.where(lane_id == i, turned, packed[0, low_levels, :])
            last = lax.rem(i + 127, 128)
            packed[1, low_levels, :] = jnp.where(lane_id == last, turned, packed[1, low_levels, :])
            gain = jnp.broadcast_to(inverse[:, :1], mixed.shape)
            packed[2, low_levels, :] = jnp.where(lane_id == i, gain, packed[2, low_levels, :])
            return carry

        lax.fori_loop(0, o_rows, mix, 0, unroll=4)

        def skew_out(l, carry):
            ocean[q, l] = skewed[pl.ds(l * skew, o_rows), :]
            return carry

        lax.fori_loop(0, levels, skew_out, 0, unroll=8)
        for s, r in ((0, 0), (1, o_rows - 1)):
            row_out[s, q] = skewed[pl.ds(r, levels, stride=skew), :]
        copy_out(q).start()
        for side in (NORTH, SOUTH):
            row_copy(side, q).start()
        return carry

    lax.fori_loop(0, q_count, field, 0)
    col_out[0] = jnp.transpose(packed[0])
    col_out[1] = jnp.transpose(pltpu.roll(packed[1], 1, 1))
    gain_ref[...] = jnp.transpose(packed[2])
    for s, r in ((0, 0), (1, o_rows - 1)):
        gain_out[s, pl.ds(0, q_count), :] = gain_ref[pl.ds(r, q_count, stride=o_rows), :]

    copies = []

    def hand(side, source, target):
        opposite = (SOUTH, NORTH, EAST, WEST)[side]
        n = len(copies)
        copy = pltpu.make_async_remote_copy(
            source, target(opposite), halo_send.at[n], halo_recv.at[n],
            device_id=beside[side], device_id_type=MESH,
        )
        copy.start()
        copies.append(copy)

    for side in (NORTH, SOUTH):
        hand(side, gain_out.at[side], lambda o: gain_strip_in.at[o])
    for side in (WEST, EAST):
        hand(side, col_out.at[side - 2], lambda o: col_in.at[o - 2])
        hand(side, gain_ref, lambda o: gain_in.at[o - 2])

    for copy in depth_copies:
        copy.wait()
    depth = depth_ref[...]
    in_band = (lat > 0).astype(i32), (lat < n_lat - 1).astype(i32)
    north_depth = depth_in[NORTH] * in_band[0]
    south_depth = depth_in[SOUTH] * in_band[1]
    row_id, cell_id = iota(depth.shape, 0), iota(depth.shape, 1)
    roll = pltpu.roll
    sides_ref[NORTH] = jnp.where(row_id == 0, roll(north_depth, 1, 0), roll(depth, 1, 0))
    sides_ref[SOUTH] = jnp.where(
        row_id == o_rows - 1, roll(south_depth, o_rows - 1, 0), roll(depth, o_rows - 1, 0)
    )
    sides_ref[WEST] = jnp.where(cell_id == 0, roll(depth_in[WEST], 1, 1), roll(depth, 1, 1))
    sides_ref[EAST] = jnp.where(cell_id == 127, roll(depth_in[EAST], 127, 1), roll(depth, 127, 1))

    def weigh(l, carry):
        count = jnp.zeros(depth.shape, f32)
        for s in range(4):
            count = count + jnp.where(l < sides_ref[s], diffusion_rate, 0.0)
        keep[l] = 1.0 - count
        return carry

    lax.fori_loop(0, levels, weigh, 0, unroll=4)
    keep_copy = pltpu.make_async_copy(keep, keep_hbm, load_sems.at[w_chunks + 2 + q_count])
    keep_copy.start()
    for q in range(q_count):
        gain = packed[2, low_levels, :]
        gain = gain if q == 0 else roll(gain, 128 - q * o_rows, 1)
        high, low = (part.astype(f32) for part in halves(gain))
        third = lane_id // o_rows
        gain = jnp.where(third == 0, high, jnp.where(third == 1, roll(low, 32, 1), roll(high, 64, 1)))
        gains_ref[q] = jnp.where(third == 3, 0.0, gain)

    partial[...] = jnp.zeros_like(partial)
    per_plane = chips // n_lat
    for dz in ORDER:
        z = lax.rem(lat + n_lat - dz, n_lat)
        some = pl.ds(z * per_plane, per_plane)
        pltpu.make_async_copy(recv_meta.at[some], recv_meta.at[some], meta_recv_sems[dz]).wait()
        some = pl.ds(z * 2 * per_plane, 2 * per_plane)
        pltpu.make_async_copy(recv.at[some], recv.at[some], recv_sems[dz]).wait()
        out = None
        for i in range(per_plane // 8):
            at = z * per_plane + i * 8
            keys = jnp.concatenate(
                [jnp.sum(recv_meta[pl.ds(at + 4 * h, 4)], axis=0) for h in range(2)], axis=1
            ).astype(i32)
            hot = one_hot(iota((256, 256), 0) == keys)
            both = jnp.concatenate(halves(recv[pl.ds(2 * at, 16)].reshape(256, 128)), axis=1)
            out = dot(hot, both) if out is None else out + dot(hot, both)
        partial[...] += (out[:, :128] + out[:, 128:]).reshape(2, 128, 128)

    own, other = partial[core], partial[1 - core]
    for e, mine_or in enumerate((core, 1 - core)):
        for side, r in ((0, 0), (1, o_rows - 1)):
            force_out[e, side, pl.ds(0, q_count), :] = partial[
                mine_or, pl.ds(r, q_count, stride=o_rows), :
            ]
    turned, turned_other = jnp.transpose(own), jnp.transpose(other)
    on_left = core == 0
    strip_out[0, pl.ds(0, 1), :] = turned[:1]
    strip_out[1, pl.ds(0, 1), :] = turned[127:]
    strip_out[2, pl.ds(0, 1), :] = jnp.where(on_left, turned_other[127:], turned_other[:1])
    inner = jnp.where(on_left, turned_other[:1], turned_other[127:])
    hops = [
        (partial.at[1 - core], partial_in, partner),
        (force_out.at[0, 0], force_in.at[0, 1], beside[NORTH]),
        (force_out.at[0, 1], force_in.at[0, 0], beside[SOUTH]),
        (force_out.at[1, 0], force_in.at[1, 1], slant[0]),
        (force_out.at[1, 1], force_in.at[1, 0], slant[1]),
        (strip_out.at[0], strip_in.at[1], beside[WEST]),
        (strip_out.at[1], strip_in.at[0], beside[EAST]),
        (strip_out.at[2], strip_in.at[2], (lat, lax.rem(lon + n_lon + 2 - 4 * core, n_lon))),
    ]
    forces = []
    for n, (source, target, device) in enumerate(hops):
        copy = pltpu.make_async_remote_copy(
            source, target, force_send.at[n], force_recv.at[n],
            device_id=device, device_id_type=MESH,
        )
        copy.start()
        forces.append(copy)

    for copy in copies:
        copy.wait()
    for q in range(q_count):
        for side in (NORTH, SOUTH):
            row_copy(side, q).wait()
    limits = [
        jnp.concatenate([jnp.broadcast_to(edge, (o_rows, 128))] * q_count, axis=0)
        for edge in (depth_in[WEST][:, 127:], depth_in[EAST][:, :1])
    ]
    strips = jnp.transpose(
        jnp.concatenate(
            [gain_strip_in[0], gain_strip_in[1], jnp.zeros((112, 128), f32)], axis=0
        )
    )
    for copy in forces:
        copy.wait()
    force_ref[...] = own + partial_in[...]
    edges = north_depth[o_rows - 1 :], south_depth[:1]
    for s in range(2):
        for q in range(q_count):
            gain = jnp.broadcast_to(strips[:levels, s * 8 + q : s * 8 + q + 1], (levels, 128))
            force = force_in[0, s, pl.ds(q, 1), :] + force_in[1, s, pl.ds(q, 1), :]
            value = row_in[s, q] + gain * force
            rows_ref[s, q] = jnp.where(level < edges[s], value, 0.0)
    level_lane = iota((128, 128), 1)
    edge = []
    for s in range(2):
        outer = strip_in[2, pl.ds(0, 1), :]
        rest_of = jnp.where(on_left, *((outer, inner) if s == 0 else (inner, outer)))
        strip = strip_in[s, pl.ds(0, 1), :] + rest_of
        strip = jnp.transpose(jnp.broadcast_to(strip, (128, 128)))
        value = col_in[s] + gain_in[s] * strip
        edge.append(jnp.where(level_lane < limits[s], value, 0.0))
    cols_ref[0] = jnp.where(level_lane < 64, edge[0], roll(edge[1], 64, 1))
    cols_ref[1] = jnp.where(level_lane < 64, roll(edge[0], 64, 1), edge[1])

    rest = pl.ds(0, 2 * (chips - 1))
    pltpu.make_async_copy(send.at[rest], send.at[rest], send_sem).wait()
    rest = pl.ds(0, chips - 1)
    pltpu.make_async_copy(meta.at[rest], meta.at[rest], meta_send_sem).wait()
    for q in range(q_count):
        copy_out(q).wait()
    keep_copy.wait()


def couple(src, coupling, dest, block, atm, mask, depth, weights, inverses, ocean, n_lat, n_lon):
    pairs = src.shape[0]
    q_count, o_rows, levels, _ = inverses.shape
    chips = n_lat * n_lon // 2
    vmem, smem, hbm = (
        pl.BlockSpec(memory_space=s) for s in (pltpu.VMEM, pltpu.SMEM, pl.ANY)
    )
    shape = jax.ShapeDtypeStruct
    V, DMA = pltpu.VMEM, pltpu.SemaphoreType.DMA
    return pl.pallas_call(
        functools.partial(couple_kernel, n_lat, n_lon),
        in_specs=[smem, smem] + [vmem] * 5 + [hbm] * 3,
        out_specs=[hbm] * 2 + [vmem] * 4,
        out_shape=[
            shape((q_count, levels, o_rows, 128), f32),
            shape((levels, o_rows, 128), f32),
            shape((128, 128), f32),
            shape((q_count, levels, 128), f32),
            shape((2, q_count, levels, 128), f32),
            shape((2, 128, 128), f32),
        ],
        scratch_shapes=[
            V(weights.shape, bf16),
            V(inverses.shape, f32),
            V(ocean.shape, f32),
            V((levels * (o_rows + 1), 128), f32),
            V((mask.shape[0], 8, 128), f32),
            V((4 * pairs, 128), f32),
            V((2 * chips, 16, 128), f32),
            V((chips, 1, 128), f32),
            V((2 * chips, 16, 128), f32),
            V((chips, 1, 128), f32),
            V((2, 128, 128), f32),
            V((128, 128), f32),
            V((3, 128, 128), f32),
            V((2, 128, 128), f32),
            V((128, 128), f32),
            V((2, 8, 128), f32),
            V((2, 2, 8, 128), f32),
            V((3, 8, 128), f32),
            V((2, q_count, levels, 128), f32),
            V((2, q_count, levels, 128), f32),
            V((2, 128, 128), f32),
            V((2, 128, 128), f32),
            V((2, 8, 128), f32),
            V((4, o_rows, 128), i32),
            V((2, 2, 8, 128), f32),
            V((3, 8, 128), f32),
            V((4, o_rows, 128), i32),
            V((levels, o_rows, 128), f32),
            DMA((15,)),
            DMA((10,)),
            DMA((4, q_count)),
            DMA((8,)),
            DMA((12,)),
            DMA((12,)),
            DMA((8,)),
            DMA((8,)),
        ],
        compiler_params=pltpu.CompilerParams(
            collective_id=0, has_side_effects=True, vmem_limit_bytes=VMEM_BYTES
        ),
        name="couple",
    )(src, coupling, dest, block, atm, mask, depth, weights, inverses, ocean)


def finish_kernel(
    base_ref, keep_ref, force_ref, gains_ref, rows_ref, cols_ref, depth_ref, out_ref,
    slabs, splits, sums, spots, forced,
):
    q = pl.program_id(0)
    levels, o_rows = base_ref.shape[1:3]
    cell = iota((o_rows, 128), 1)
    here = pl.ds(q * o_rows, o_rows)
    group = slabs[0].shape[0]
    groups = levels // group
    rim = (cell == 0) | (cell == 127)
    far = jnp.where(cell == 127, 64, 0)
    own_row = cell % o_rows == iota((o_rows, 128), 0)
    apart = iota((256, 128), 0) % 128 - iota((256, 128), 1)
    beside = one_hot((apart == 1) | (apart == -1))
    high, low = halves(force_ref[here, :])
    forces = jnp.concatenate([high, high, low, jnp.zeros_like(low)], axis=0)

    def tile(j):
        return pl.ds(j * o_rows, o_rows)

    def spot(n, j):
        gain = gains_ref[0, pl.ds(n * group + j, 1), :]
        spots[n % 2][tile(j), :] = jnp.where(own_row, gain, 0.0).astype(bf16)

    def force(n, j):
        slab, split, l = slabs[n % 2], splits[n % 2], n * group + j
        mixed = base_ref[0, l] + forced[n % 2][tile(j), :]
        mixed = jnp.where(l < depth_ref[...], mixed, 0.0)
        slab[j, pl.ds(8, o_rows), :] = mixed
        slab[j, pl.ds(7, 1), :] = rows_ref[0, 0, pl.ds(l, 1), :]
        slab[j, pl.ds(8 + o_rows, 1), :] = rows_ref[1, 0, pl.ds(l, 1), :]
        high, low = halves(mixed)
        split[tile(j), pl.ds(0, 128)] = high
        split[tile(j), pl.ds(128, 128)] = low

    def spread(n, j):
        slab, l = slabs[n % 2], n * group + j
        edge = jnp.take_along_axis(cols_ref[l // 64, here, :], far + l % 64, axis=1)
        near = slab[j, pl.ds(7, o_rows), :] + slab[j, pl.ds(9, o_rows), :]
        near = near + sums[n % 2][tile(j), :]
        near = near + jnp.where(rim, edge, 0.0)
        value = keep_ref[l] * slab[j, pl.ds(8, o_rows), :] + diffusion_rate * near
        out_ref[0, l] = jnp.where(l < depth_ref[...], value, base_ref[0, l])

    for n in range(-2, groups):
        if n >= 0:
            sums[n % 2][...] = dot(splits[n % 2][...], beside)
        if 0 <= n + 1 < groups:
            forced[(n + 1) % 2][...] = dot(spots[(n + 1) % 2][...], forces)
        for j in range(group):
            if n + 2 < groups:
                spot(n + 2, j)
            if n >= 0:
                spread(n, j)
            if 0 <= n + 1 < groups:
                force(n + 1, j)


def finish(base, keep, force, gains, rows, cols, depth):
    q_count, levels, o_rows, _ = base.shape
    group = 16
    full = lambda a: pl.BlockSpec(a.shape, lambda q: (0,) * a.ndim)
    block = pl.BlockSpec((1, levels, o_rows, 128), lambda q: (q, 0, 0, 0))
    V = pltpu.VMEM
    return pl.pallas_call(
        finish_kernel,
        grid=(q_count,),
        in_specs=[
            block,
            full(keep),
            full(force),
            pl.BlockSpec((1, levels, 128), lambda q: (q, 0, 0)),
            pl.BlockSpec((2, 1, levels, 128), lambda q: (0, q, 0, 0)),
            full(cols),
            full(depth),
        ],
        out_specs=block,
        out_shape=jax.ShapeDtypeStruct(base.shape, f32),
        scratch_shapes=[
            [V((group, o_rows + 16, 128), f32)] * 2,
            [V((group * o_rows, 256), bf16)] * 2,
            [V((group * o_rows, 128), f32)] * 2,
            [V((group * o_rows, 128), bf16)] * 2,
            [V((group * o_rows, 128), f32)] * 2,
        ],
        compiler_params=pltpu.CompilerParams(vmem_limit_bytes=VMEM_BYTES),
        name="finish",
    )(base, keep, force, gains, rows, cols, depth)


def on_device(
    atm_flux,
    sea_mask,
    src_block,
    dest_dev,
    dest_block,
    intersection_weights,
    coupling,
    inverses,
    ocean_state,
    depth_levels,
):
    n_lat, n_lon = lax.axis_size("lat"), lax.axis_size("lon")
    pairs = src_block.shape[0]
    q_count, levels, o_rows, cells = ocean_state.shape
    base, keep, force, gains, rows, cols = couple(
        src_block, coupling, dest_dev.reshape(1, pairs), dest_block.reshape(1, pairs),
        atm_flux, sea_mask, depth_levels, intersection_weights,
        inverses.reshape(q_count, o_rows, levels, levels),
        ocean_state, n_lat, n_lon,
    )
    return finish(base, keep, force, gains, rows, cols, depth_levels)


def solution(mesh):
    placed = (
        P(None, "lat", "lon"),
        P("lat", "lon"),
        P(("lat", "lon")),
        P(("lat", "lon"), None),
        P(("lat", "lon")),
        P(("lat", "lon"), None, None),
        P(),
        P(None, "lat", "lon", None, None),
        P(None, None, "lat", "lon"),
        P("lat", "lon"),
    )
    return jax.shard_map(
        on_device,
        mesh=mesh,
        in_specs=placed,
        out_specs=P(None, None, "lat", "lon"),
        check_vma=False,
    )
```
